32 devices in a mesh: fsdp: 8 (over z, x), tp: 4 (over y, core).
Axes of the slice: x: 2, y: 2, z: 4, core: 2. Of those that a mesh axis runs over, the one named last changes fastest.
Arguments:
- inputs: bfloat16 [2, 8, 1024, 2048], P(None, 'fsdp', 'tp'), may hold values from -6 to 6
- ln_gain: bfloat16 [2048], P(('fsdp', 'tp')), may hold values from 0.099609375 to 1.8984375
- ln_bias: bfloat16 [2048], P(('fsdp', 'tp')), may hold values from -3 to 3
- qkv_weight: bfloat16 [2048, 3, 2048], P('fsdp', None, 'tp'), may hold values from -0.125 to 0.125
- qkv_bias: bfloat16 [3, 32, 64], P(None, 'tp', 'fsdp'), may hold values from -3 to 3
- out_weight: bfloat16 [2048, 2048], P('tp', 'fsdp'), may hold values from -1.5 to 1.5
- out_bias: bfloat16 [2048], P(('fsdp', 'tp')), may hold values from -3 to 3
- up_weight: bfloat16 [2048, 8192], P('fsdp', 'tp'), may hold values from -0.125 to 0.125
- up_bias: bfloat16 [128, 64], P('tp', 'fsdp'), may hold values from -3 to 3
- down_weight: bfloat16 [8192, 2048], P('tp', 'fsdp'), may hold values from -0.0625 to 0.0625
- down_bias: bfloat16 [2048], P(('fsdp', 'tp')), may hold values from -3 to 3
- cotangent: bfloat16 [2, 8, 1024, 2048], P(None, 'fsdp', 'tp'), may hold values from -40 to 40
Outputs:
- output: bfloat16 [2, 8, 1024, 2048], P(None, 'fsdp', 'tp')
- input_grad: bfloat16 [2, 8, 1024, 2048], P(None, 'fsdp', 'tp')
- ln_gain_grad: float32 [2048], P(('fsdp', 'tp'))
- ln_bias_grad: float32 [2048], P(('fsdp', 'tp'))
- qkv_weight_grad: float32 [2048, 3, 2048], P('fsdp', None, 'tp')
- qkv_bias_grad: float32 [3, 32, 64], P(None, 'tp', 'fsdp')
- out_weight_grad: float32 [2048, 2048], P('tp', 'fsdp')
- out_bias_grad: float32 [2048], P(('fsdp', 'tp'))
- up_weight_grad: float32 [2048, 8192], P('fsdp', 'tp')
- up_bias_grad: float32 [128, 64], P('tp', 'fsdp')
- down_weight_grad: float32 [8192, 2048], P('tp', 'fsdp')
- down_bias_grad: float32 [2048], P(('fsdp', 'tp'))
The draws below stay inside these ranges and needn't reach their ends.
All inputs are finite; a program needn't handle non-finite values.
Results may differ from the reference program's by a relative error of at most 0.014.
Values may be sent and summed in bfloat16 or wider, within the bound.
No kernel may reach another device: no remote copies, remote signals or barrier semaphores. Data moves between devices by JAX's collectives and lax.ppermute only.
A program may use at most 320 MiB of HBM per device.

```python
import math
import jax
import jax.numpy as jnp
from jax import lax

D = 2048
HEADS = 32
HEAD_DIM = 64
ROT = 32
FF = 8192
LEN = 1024
MICRO = 2
SEQS = 8


def draw_cotangent(key, part):
    base_key, row_key = jax.random.split(key, 2)
    full_shape = (MICRO, SEQS, LEN, D)
    base_values = jnp.clip(jax.random.normal(base_key, full_shape, jnp.float32), -6.0, 6.0)
    row_scale = jnp.exp(jax.random.uniform(row_key, (MICRO, SEQS, LEN, 1), jnp.float32, -0.7, 0.7))
    rising = 1.0 + 2.0 * jnp.arange(SEQS, dtype=jnp.float32) / max(SEQS - 1, 1)
    return (base_values * row_scale * rising[None, :, None, None]).astype(jnp.bfloat16)


def block_scale(rng, extent, cuts, smallest, largest):
    factor_of = 1.0
    for axis_at, blocks in cuts:
        heights = jax.random.uniform(jax.random.fold_in(jax.random.fold_in(rng, 6), axis_at), (blocks,), jnp.float32, smallest / len(cuts), largest / len(cuts))
        factor_of = factor_of * jnp.repeat(jnp.exp(heights), extent[axis_at] // blocks).reshape((-1,) + (1,) * (len(extent) - 1 - axis_at))
    return factor_of


def noise(key, shape, deviation, reach, cuts=(), kind=jnp.bfloat16):
    values = jax.random.normal(key, shape, jnp.float32) * deviation
    if len(cuts) > 0:
        values = block_scale(key, shape, cuts, -0.22, 0.18) * values
    return jnp.clip(values, min=-reach, max=reach).astype(kind)


def setup_inputs(seed: int = 0) -> dict:
    keys = jax.random.split(jax.random.key(seed), 13)
    inputs = noise(keys[0], (MICRO, SEQS, LEN, D), 1.0, 6.0, ((1, 8), (2, 4)))
    ln_gain = jnp.clip(1.0 + 0.18 * jax.random.normal(keys[1], (D,), jnp.float32), 0.099609375, 1.8984375).astype(jnp.bfloat16)
    ln_bias = noise(keys[2], (D,), 0.5, 3.0, ((0, 32),))
    qkv_weight = noise(keys[3], (D, 3, D), D ** -0.5, 0.125, ((0, 8), (2, 4)))
    qkv_bias = noise(keys[4], (3, HEADS, HEAD_DIM), 0.5, 3.0, ((1, 4), (2, 8)))
    out_weight = noise(keys[5], (D, D), (max(D // 128, 1)) ** -0.5, 1.5, ((0, 4), (1, 8)))
    out_bias = noise(keys[6], (D,), 0.5, 3.0, ((0, 32),))
    up_weight = noise(keys[7], (D, FF), D ** -0.5, 0.125, ((0, 8), (1, 4)))
    up_bias = noise(keys[8], (FF // 64, 64), 0.5, 3.0, ((0, 4), (1, 8)))
    down_weight = noise(keys[9], (FF, D), FF ** -0.5, 0.0625, ((0, 4), (1, 8)))
    down_bias = noise(keys[10], (D,), 0.5, 3.0, ((0, 32),))
    cotangent = draw_cotangent(jax.random.fold_in(keys[12], 71), 0)
    return {"inputs": inputs, "ln_gain": ln_gain, "ln_bias": ln_bias, "qkv_weight": qkv_weight, "qkv_bias": qkv_bias, "out_weight": out_weight, "out_bias": out_bias, "up_weight": up_weight, "up_bias": up_bias, "down_weight": down_weight, "down_bias": down_bias, "cotangent": cotangent}


@jax.custom_vjp
def low(v):
    return lax.optimization_barrier(v.astype(jnp.bfloat16)).astype(jnp.float32)

@jax.custom_vjp
def low_back(v):
    return v

def low_keep(v):
    return (low(v), None)

def low_pass(kept, grad):
    return (grad,)

def back_keep(v):
    return (v, None)

def back_low(kept, grad):
    return (low(grad),)
low.defvjp(low_keep, low_pass)
low_back.defvjp(back_keep, back_low)
norm_epsilon = 1e-05
gelu_factor = 0.7978845608028654

def layer_norm(resid_rows, gain_vec, shift_vec):
    row_mean = lax.optimization_barrier(jnp.mean(resid_rows, axis=-1, keepdims=True))
    centred = resid_rows - row_mean
    row_var = lax.optimization_barrier(jnp.mean(centred * centred, axis=-1, keepdims=True))
    return centred * lax.rsqrt(row_var + norm_epsilon) * gain_vec + shift_vec

def gelu_tanh(inner):
    return 0.5 * inner * (1.0 + jnp.tanh(gelu_factor * (inner + 0.044715 * inner * inner * inner)))

def rotary_tables(length, head_dim, rot_dim):
    half_rot = rot_dim // 2
    inv_freq = 10000.0 ** (-2.0 * jnp.arange(half_rot, dtype=jnp.float32) / rot_dim)
    angles = jnp.arange(length, dtype=jnp.float32)[:, None] * inv_freq[None, :]
    rest_ones = jnp.ones((length, head_dim - rot_dim), jnp.float32)
    cosine_table = jnp.concatenate([jnp.cos(angles), jnp.cos(angles), rest_ones], axis=1)
    sine_table = jnp.concatenate([jnp.sin(angles), jnp.sin(angles), 0.0 * rest_ones], axis=1)
    return (cosine_table, sine_table)

def rotate(head_vals, cosine_table, sine_table, rot_dim):
    half_rot = rot_dim // 2
    turned = jnp.concatenate([-head_vals[..., half_rot:rot_dim], head_vals[..., :half_rot], 0.0 * head_vals[..., rot_dim:]], axis=-1)
    return head_vals * cosine_table[:, None, :] + turned * sine_table[:, None, :]

def head_attend(head_args):
    query_head, key_head, value_head = head_args
    length = query_head.shape[0]
    scores = low_back(jnp.dot(query_head, key_head.T, precision=lax.Precision.HIGHEST) * (1.0 / math.sqrt(HEAD_DIM)))
    row_ids = lax.broadcasted_iota(jnp.int32, (length, length), 0)
    col_ids = lax.broadcasted_iota(jnp.int32, (length, length), 1)
    scores = jnp.where(col_ids <= row_ids, scores, -1e+30)
    probs = jax.nn.softmax(scores, axis=-1)
    return jnp.dot(low(probs), value_head, precision=lax.Precision.HIGHEST)

def seq_forward(seq_rows, gain_vec, shift_vec, w_qkv, b_qkv, w_out, b_out, w_up, b_up, w_down, b_down):
    length = seq_rows.shape[0]
    normed = low(layer_norm(seq_rows, gain_vec, shift_vec))
    qkv_proj = jnp.dot(normed, w_qkv.reshape(D, 3 * D), precision=lax.Precision.HIGHEST) + b_qkv.reshape(3 * D)
    qkv_proj = low_back(qkv_proj).reshape(length, 3, HEADS, HEAD_DIM)
    cosine_table, sine_table = rotary_tables(length, HEAD_DIM, ROT)
    queries = low(rotate(qkv_proj[:, 0], cosine_table, sine_table, ROT))
    keys_rot = low(rotate(qkv_proj[:, 1], cosine_table, sine_table, ROT))
    values_low = low(qkv_proj[:, 2])
    attn = lax.map(jax.checkpoint(head_attend), (queries.transpose(1, 0, 2), keys_rot.transpose(1, 0, 2), values_low.transpose(1, 0, 2)))
    attn = low_back(low(attn.transpose(1, 0, 2).reshape(length, D)))
    pre_act = low_back(jnp.dot(normed, w_up, precision=lax.Precision.HIGHEST) + b_up.reshape(FF))
    act_low = low(gelu_tanh(pre_act))
    branch = jnp.dot(attn, w_out, precision=lax.Precision.HIGHEST) + jnp.dot(act_low, w_down, precision=lax.Precision.HIGHEST)
    return seq_rows + branch + b_out + b_down

def reference(inputs, ln_gain, ln_bias, qkv_weight, qkv_bias, out_weight, out_bias, up_weight, up_bias, down_weight, down_bias, cotangent):
    params = tuple((weight.astype(jnp.float32) for weight in (ln_gain, ln_bias, qkv_weight, qkv_bias, out_weight, out_bias, up_weight, up_bias, down_weight, down_bias)))
    seq_inputs = inputs.astype(jnp.float32).reshape(MICRO * SEQS, LEN, D)
    seq_cots = cotangent.astype(jnp.float32).reshape(MICRO * SEQS, LEN, D)

    def scan_step(grad_sums, seq_pair):
        seq_rows, seq_cot = seq_pair
        result, pull_back = jax.vjp(seq_forward, seq_rows, *params)
        pulled = pull_back(seq_cot)
        return (tuple((earlier + later for earlier, later in zip(grad_sums, pulled[1:]))), (result, pulled[0]))
    start_sums = tuple((jnp.zeros_like(weight) for weight in params))
    grad_sums, (results, row_grads) = lax.scan(scan_step, start_sums, (seq_inputs, seq_cots))
    output = results.reshape(inputs.shape).astype(jnp.bfloat16)
    input_grad = row_grads.reshape(inputs.shape).astype(jnp.bfloat16)
    return (output, input_grad, grad_sums[0], grad_sums[1], grad_sums[2], grad_sums[3], grad_sums[4], grad_sums[5], grad_sums[6], grad_sums[7], grad_sums[8], grad_sums[9])
```

```python
import functools
import math

import jax
import jax.numpy as jnp
from jax import lax
from jax.experimental import pallas as pl
from jax.experimental.pallas import tpu as pltpu
from jax.sharding import PartitionSpec as P

ROT = 32
LANES = 128

norm_epsilon = 1e-05
gelu_factor = 0.7978845608028654
mask_fill = -1e30
BF = jnp.bfloat16
F32 = jnp.float32
VMEM_LIMIT = 48 * 1024 * 1024


def layer_norm(resid_rows, gain_vec, shift_vec):
    row_mean = jnp.mean(resid_rows, axis=-1, keepdims=True)
    centred = resid_rows - row_mean
    row_var = jnp.mean(centred * centred, axis=-1, keepdims=True)
    return centred * lax.rsqrt(row_var + norm_epsilon) * gain_vec + shift_vec


def gelu_tanh(inner):
    return 0.5 * inner * (1.0 + jnp.tanh(gelu_factor * (inner + 0.044715 * inner * inner * inner)))


def rotary_tables(length, head_dim, rot_dim):
    half_rot = rot_dim // 2
    inv_freq = 10000.0 ** (-2.0 * jnp.arange(half_rot, dtype=F32) / rot_dim)
    angles = jnp.arange(length, dtype=F32)[:, None] * inv_freq[None, :]
    cos, sin = jnp.cos(angles), jnp.sin(angles)
    rest = jnp.ones((length, head_dim - rot_dim), F32)
    cosine = jnp.concatenate([cos, cos, rest], axis=1)
    lower = jnp.concatenate([-sin, 0.0 * sin, 0.0 * rest], axis=1)
    upper = jnp.concatenate([0.0 * sin, sin, 0.0 * rest], axis=1)
    copies = LANES // head_dim
    return tuple(jnp.tile(table, (1, copies)) for table in (cosine, lower, upper))


def turn(vals, cosine, lower, upper):
    half_rot = ROT // 2
    ahead = pltpu.roll(vals, LANES - half_rot, 1)
    behind = pltpu.roll(vals, half_rot, 1)
    return vals * cosine + ahead * lower + behind * upper


def dot_rows(left, right):
    return lax.dot_general(left, right, (((0,), (0,)), ((), ())), preferred_element_type=F32)


def dot_cols(left, right):
    return lax.dot_general(left, right, (((1,), (1,)), ((), ())), preferred_element_type=F32)


def dot_plain(left, right):
    return lax.dot_general(left, right, (((1,), (0,)), ((), ())), preferred_element_type=F32)


def causal_fill(scores, first, fill):
    keys, cols = scores.shape
    key_ids = lax.broadcasted_iota(jnp.int32, (keys, cols), 0)
    query_ids = lax.broadcasted_iota(jnp.int32, (keys, cols), 1) + first
    return jnp.where(key_ids <= query_ids, scores, fill)


def head_lanes(vals, head, head_dim):
    lane_ids = lax.broadcasted_iota(jnp.int32, vals.shape, 1)
    return jnp.where(lane_ids // head_dim == head, vals, jnp.zeros_like(vals))


def attend_kernel(head_dim, block, qkv_ref, cos_ref, low_ref, up_ref, rot_ref, attn_ref, lse_ref):
    length = qkv_ref.shape[0]
    scale = 1.0 / math.sqrt(head_dim)
    tables = (cos_ref[...], low_ref[...], up_ref[...])
    queries = turn(qkv_ref[:, :LANES], *tables).astype(BF)
    keys = turn(qkv_ref[:, LANES : 2 * LANES], *tables).astype(BF)
    values = qkv_ref[:, 2 * LANES :].astype(BF)
    rot_ref[:, :LANES] = queries
    rot_ref[:, LANES : 2 * LANES] = keys
    rot_ref[:, 2 * LANES :] = values
    heads = LANES // head_dim
    for first in range(0, length, block):
        last = first + block
        total = jnp.zeros((block, LANES), F32)
        for head in range(heads):
            query_block = head_lanes(queries[first:last], head, head_dim)
            scores = dot_cols(keys[:last], query_block) * scale
            scores = causal_fill(scores, first, mask_fill)
            col_max = jnp.max(scores, axis=0, keepdims=True)
            exp_scores = jnp.exp(scores - col_max)
            denom = jnp.sum(exp_scores, axis=0, keepdims=True)
            prob_low = (exp_scores * (1.0 / denom)).astype(BF)
            total += dot_rows(prob_low, head_lanes(values[:last], head, head_dim))
            lse_ref[0, head : head + 1, first:last] = col_max + jnp.log(denom)
        attn_ref[first:last, :] = total.astype(BF)


def attend_back_kernel(head_dim, block, rot_ref, grad_ref, lse_ref, cos_ref, low_ref, up_ref, out_ref, key_acc, value_acc):
    length = rot_ref.shape[0]
    scale = 1.0 / math.sqrt(head_dim)
    tables = (cos_ref[...], -low_ref[...], -up_ref[...])
    heads = LANES // head_dim
    key_acc[...] = jnp.zeros_like(key_acc)
    value_acc[...] = jnp.zeros_like(value_acc)
    for first in range(0, length, block):
        last = first + block
        total = jnp.zeros((block, LANES), F32)
        for head in range(heads):
            query_block = head_lanes(rot_ref[first:last, :LANES], head, head_dim)
            grad_block = head_lanes(grad_ref[first:last, :], head, head_dim)
            keys = rot_ref[:last, LANES : 2 * LANES]
            scores = dot_cols(keys, query_block) * scale
            probs = jnp.exp(scores - lse_ref[0, head : head + 1, first:last])
            probs = causal_fill(probs, first, 0.0)
            value_acc[:last, :] += dot_plain(probs.astype(BF), grad_block)
            prob_grad = dot_cols(rot_ref[:last, 2 * LANES :], grad_block)
            inner_sum = jnp.sum(probs * prob_grad, axis=0, keepdims=True)
            score_grad = (probs * (prob_grad - inner_sum)).astype(BF)
            total += dot_rows(score_grad, head_lanes(keys, head, head_dim))
            key_acc[:last, :] += dot_plain(score_grad, query_block)
        out_ref[first:last, :LANES] = turn(total * scale, *(table[first:last] for table in tables)).astype(BF)
    out_ref[:, LANES : 2 * LANES] = turn(key_acc[...] * scale, *tables).astype(BF)
    out_ref[:, 2 * LANES :] = value_acc[...].astype(BF)


def attention_cost(seqs, pairs, length, matmuls):
    flops = seqs * pairs * matmuls * 2 * 2 * length * length * LANES
    return pl.CostEstimate(flops=flops, bytes_accessed=seqs * pairs * length * LANES * 16, transcendentals=0)


def attend(qkv, tables, length, head_dim):
    tokens, width = qkv.shape
    seqs, pairs = tokens // length, width // (3 * LANES)
    heads = LANES // head_dim
    block = min(256, length)
    table_spec = pl.BlockSpec((length, LANES), lambda s, h: (0, 0))
    return pl.pallas_call(
        functools.partial(attend_kernel, head_dim, block),
        grid=(seqs, pairs),
        in_specs=[pl.BlockSpec((length, 3 * LANES), lambda s, h: (s, h))] + [table_spec] * 3,
        out_specs=[
            pl.BlockSpec((length, 3 * LANES), lambda s, h: (s, h)),
            pl.BlockSpec((length, LANES), lambda s, h: (s, h)),
            pl.BlockSpec((1, heads, length), lambda s, h: (s * pairs + h, 0, 0)),
        ],
        out_shape=[
            jax.ShapeDtypeStruct((tokens, width), BF),
            jax.ShapeDtypeStruct((tokens, pairs * LANES), BF),
            jax.ShapeDtypeStruct((seqs * pairs, heads, length), F32),
        ],
        compiler_params=pltpu.CompilerParams(vmem_limit_bytes=VMEM_LIMIT),
        cost_estimate=attention_cost(seqs, pairs, length, 3),
    )(qkv, *tables)


def attend_back(rot, attn_grad, lse, tables, length, head_dim):
    tokens, width = rot.shape
    seqs, pairs = tokens // length, width // (3 * LANES)
    heads = LANES // head_dim
    block = min(256, length)
    table_spec = pl.BlockSpec((length, LANES), lambda s, h: (0, 0))
    return pl.pallas_call(
        functools.partial(attend_back_kernel, head_dim, block),
        grid=(seqs, pairs),
        in_specs=[
            pl.BlockSpec((length, 3 * LANES), lambda s, h: (s, h)),
            pl.BlockSpec((length, LANES), lambda s, h: (s, h)),
            pl.BlockSpec((1, heads, length), lambda s, h: (s * pairs + h, 0, 0)),
        ]
        + [table_spec] * 3,
        out_specs=pl.BlockSpec((length, 3 * LANES), lambda s, h: (s, h)),
        out_shape=jax.ShapeDtypeStruct((tokens, width), BF),
        scratch_shapes=[pltpu.VMEM((length, LANES), F32), pltpu.VMEM((length, LANES), F32)],
        compiler_params=pltpu.CompilerParams(vmem_limit_bytes=VMEM_LIMIT),
        cost_estimate=attention_cost(seqs, pairs, length, 6),
    )(rot, attn_grad, lse, *tables)


def shards(
    inputs,
    ln_gain,
    ln_bias,
    qkv_weight,
    qkv_bias,
    out_weight,
    out_bias,
    up_weight,
    up_bias,
    down_weight,
    down_bias,
    cotangent,
):
    micro_count, _, token_rows, model_width = inputs.shape
    fsdp_size, tp_size = lax.axis_size("fsdp"), lax.axis_size("tp")
    line = fsdp_size // 2
    fsdp_at, tp_at = lax.axis_index("fsdp"), lax.axis_index("tp")
    line_at, pair_at = fsdp_at // 2, fsdp_at % 2
    plane_size = 2 * tp_size
    planes = [[plane * plane_size + i for i in range(plane_size)] for plane in range(line)]
    ring = [(f, ((f // 2 + 1) % line) * 2 + f % 2) for f in range(fsdp_size)]
    length = token_rows * tp_size
    head_dim = qkv_bias.shape[2] * fsdp_size
    shard_rows = model_width // fsdp_size
    line_rows = 2 * shard_rows
    attn_cols = out_weight.shape[0] // 2
    qkv_cols = 3 * attn_cols
    pairs = attn_cols // LANES
    mlp_cols = up_weight.shape[1] // 2
    both_axes = ("fsdp", "tp")

    def swap_pair(vals):
        return lax.ppermute(vals, "fsdp", [(f, f ^ 1) for f in range(fsdp_size)])

    def gather_plane(vals):
        return lax.all_gather(vals, both_axes, axis=0, tiled=True, axis_index_groups=planes)

    def scatter_plane(vals):
        return lax.psum_scatter(vals, both_axes, scatter_dimension=0, tiled=True, axis_index_groups=planes)

    def after(vals, *others):
        return lax.optimization_barrier((vals,) + others)[0]

    def gather_small(vals):
        cur = vals[None]
        bit = 1
        while bit < tp_size:
            other = lax.ppermute(cur, "tp", [(t, t ^ bit) for t in range(tp_size)])
            upper = (tp_at & bit) != 0
            cur = jnp.where(upper, jnp.concatenate([other, cur]), jnp.concatenate([cur, other]))
            bit *= 2
        bit = 1
        while bit < fsdp_size:
            other = lax.ppermute(cur, "fsdp", [(f, f ^ bit) for f in range(fsdp_size)])
            upper = (fsdp_at & bit) != 0
            cur = jnp.where(upper, jnp.concatenate([other, cur]), jnp.concatenate([cur, other]))
            bit *= 2
        return cur

    def sum_small(everywhere, over_fsdp):
        cur = everywhere
        bit = 1
        while bit < tp_size:
            cur = cur + lax.ppermute(cur, "tp", [(t, t ^ bit) for t in range(tp_size)])
            bit *= 2
        cur = jnp.concatenate([cur, over_fsdp])
        bit = 1
        while bit < fsdp_size:
            cur = cur + lax.ppermute(cur, "fsdp", [(f, f ^ bit) for f in range(fsdp_size)])
            bit *= 2
        return cur[: everywhere.shape[0]], cur[everywhere.shape[0] :]

    small = jnp.concatenate(
        [vec.reshape(-1) for vec in (ln_gain, ln_bias, out_bias, down_bias, qkv_bias, up_bias)]
    )
    small_all = gather_small(small)
    vec_size = ln_gain.shape[0]
    gain_vec, shift_vec, bias_out, bias_down = (
        small_all[:, i * vec_size : (i + 1) * vec_size].reshape(-1).astype(F32) for i in range(4)
    )
    bias_both = bias_out + bias_down
    mine = lax.dynamic_slice_in_dim(
        small_all.reshape(fsdp_size, tp_size, -1), tp_at, 1, axis=1
    )[:, 0].astype(F32)
    at = 4 * vec_size
    qkv_b = mine[:, at : at + qkv_bias.size].reshape(fsdp_size, 3, 2, pairs, -1, qkv_bias.shape[2])
    qkv_b = lax.dynamic_slice_in_dim(qkv_b, pair_at, 1, axis=2)[:, :, 0]
    qkv_b = qkv_b.transpose(2, 1, 3, 0, 4).reshape(1, qkv_cols)
    at += qkv_bias.size
    up_b = mine[:, at:].reshape(fsdp_size, up_bias.shape[0], up_bias.shape[1])
    up_b = up_b.transpose(1, 0, 2).reshape(2, mlp_cols)
    up_b = lax.dynamic_slice_in_dim(up_b, pair_at, 1, axis=0)

    def attn_half(half):
        qkv_part = lax.dynamic_slice_in_dim(qkv_weight, half * attn_cols, attn_cols, axis=2)
        qkv_part = qkv_part.reshape(shard_rows, 3, pairs, LANES).transpose(0, 2, 1, 3)
        out_part = lax.dynamic_slice_in_dim(out_weight, half * attn_cols, attn_cols, axis=0)
        return jnp.concatenate([qkv_part.reshape(shard_rows, qkv_cols), out_part.T], axis=1)

    def up_half(half):
        return lax.dynamic_slice_in_dim(up_weight, half * mlp_cols, mlp_cols, axis=1)

    def down_half(half):
        return lax.dynamic_slice_in_dim(down_weight, half * mlp_cols, mlp_cols, axis=0).T

    def pair_shard(half_of):
        own = half_of(pair_at)
        other = swap_pair(half_of(1 - pair_at))
        return jnp.where(
            pair_at == 0, jnp.concatenate([own, other]), jnp.concatenate([other, own])
        )

    def gather_line(shard):
        whole = jnp.zeros((line * line_rows, shard.shape[1]), BF)
        whole = lax.dynamic_update_slice_in_dim(whole, shard, line_at * line_rows, axis=0)
        moving = shard
        for step in range(1, line):
            moving = lax.ppermute(moving, "fsdp", ring)
            at_line = (line_at - step) % line
            whole = lax.dynamic_update_slice_in_dim(whole, moving, at_line * line_rows, axis=0)
        return whole, moving

    attn_shard = pair_shard(attn_half)
    w_attn, last_moved = gather_line(attn_shard)
    up_shard = pair_shard(up_half)
    up_shard = after(up_shard, last_moved)
    w_up, last_moved = gather_line(up_shard)
    down_shard = pair_shard(down_half)
    down_shard = after(down_shard, last_moved)
    w_down, _ = gather_line(down_shard)
    w_qkv, w_out = w_attn[:, :qkv_cols], w_attn[:, qkv_cols:]

    resid, cots, plane_rows, plane_cots = [], [], [], []
    for micro in range(micro_count):
        resid.append(inputs[micro].reshape(token_rows, model_width))
        cots.append(cotangent[micro].reshape(token_rows, model_width))
    before = None
    for micro in range(micro_count):
        sent = resid[micro] if before is None else after(resid[micro], before)
        before = gather_plane(sent)
        plane_rows.append(before)
    for micro in range(micro_count):
        before = gather_plane(after(cots[micro], before))
        plane_cots.append(before)

    tables = rotary_tables(length, head_dim, ROT)
    normed, rots, attns, lses, acts, pre_acts, outputs = ([] for _ in range(7))
    for micro in range(micro_count):
        normed.append(layer_norm(plane_rows[micro].astype(F32), gain_vec, shift_vec).astype(BF))
        qkv = dot_plain(normed[micro], w_qkv) + qkv_b
        rot, attn, lse = attend(qkv, tables, length, head_dim)
        rots.append(rot)
        attns.append(attn)
        lses.append(lse)
    for micro in range(micro_count):
        pre = dot_plain(normed[micro], w_up) + up_b
        pre_acts.append(pre)
        acts.append(gelu_tanh(pre).astype(BF))
    for micro in range(micro_count):
        branch = dot_cols(
            jnp.concatenate([attns[micro], acts[micro]], axis=1), jnp.concatenate([w_out, w_down], axis=1)
        ).astype(BF)
        branch = scatter_plane(branch).astype(F32)
        outputs.append((resid[micro].astype(F32) + branch + bias_both).astype(BF))

    def scatter_line(part):
        def own(step):
            at_line = (line_at - step) % line
            return lax.dynamic_slice_in_dim(part, at_line * line_rows, line_rows, axis=0).astype(F32)

        moving = own(1)
        for step in range(2, line + 1):
            moving = lax.ppermute(moving.astype(BF), "fsdp", ring).astype(F32) + own(step)
        keep = lax.dynamic_slice_in_dim(moving, pair_at * shard_rows, shard_rows, axis=0)
        give = lax.dynamic_slice_in_dim(moving, (1 - pair_at) * shard_rows, shard_rows, axis=0)
        got = swap_pair(give.astype(BF)).astype(F32)
        return jnp.where(pair_at == 0, keep, got), jnp.where(pair_at == 0, got, keep)

    down_part = sum(dot_rows(plane_cots[m], acts[m]) for m in range(micro_count)).astype(BF)
    down_grads = scatter_line(down_part)
    pre_grads = []
    for micro in range(micro_count):
        act_grad = dot_plain(plane_cots[micro], w_down)
        pre_grads.append(jax.vjp(gelu_tanh, pre_acts[micro])[1](act_grad)[0].astype(BF))
    up_part = sum(dot_rows(normed[m], pre_grads[m]) for m in range(micro_count)).astype(BF)
    up_grads = scatter_line(up_part)
    qkv_grads = []
    for micro in range(micro_count):
        attn_grad = dot_plain(plane_cots[micro], w_out).astype(BF)
        qkv_grads.append(attend_back(rots[micro], attn_grad, lses[micro], tables, length, head_dim))
    attn_part = jnp.concatenate(
        [
            sum(dot_rows(normed[m], qkv_grads[m]) for m in range(micro_count)).astype(BF),
            sum(dot_rows(plane_cots[m], attns[m]) for m in range(micro_count)).astype(BF),
        ],
        axis=1,
    )
    attn_grads = scatter_line(attn_part)
    input_grads = []
    gain_total = jnp.zeros((model_width,), F32)
    shift_total = jnp.zeros((model_width,), F32)
    bias_total = jnp.zeros((model_width,), F32)
    for micro in range(micro_count):
        normed_grad = dot_cols(
            jnp.concatenate([qkv_grads[micro], pre_grads[micro]], axis=1),
            jnp.concatenate([w_qkv, w_up], axis=1),
        ).astype(BF)
        normed_grad = scatter_plane(normed_grad).astype(F32)
        norm_back = jax.vjp(layer_norm, resid[micro].astype(F32), gain_vec, shift_vec)[1]
        rows_grad, gain_grad, shift_grad = norm_back(normed_grad)
        cot = cots[micro].astype(F32)
        input_grads.append((cot + rows_grad).astype(BF))
        gain_total += gain_grad
        shift_total += shift_grad
        bias_total += jnp.sum(cot, axis=0)

    up_b_grad = sum(jnp.sum(pre_grads[m].astype(F32), axis=0) for m in range(micro_count))
    qkv_b_grad = sum(jnp.sum(qkv_grads[m].astype(F32), axis=0) for m in range(micro_count))
    qkv_b_grad = qkv_b_grad.reshape(pairs, 3, -1).transpose(1, 0, 2).reshape(3, attn_cols)

    def in_half(vals):
        blank = jnp.zeros_like(vals)
        return jnp.where(
            pair_at == 0, jnp.concatenate([vals, blank], axis=-1), jnp.concatenate([blank, vals], axis=-1)
        )

    small_sums, bias_sums = sum_small(
        jnp.concatenate([gain_total, shift_total, bias_total]),
        jnp.concatenate([in_half(up_b_grad), in_half(qkv_b_grad).reshape(-1)]),
    )
    small_sums = small_sums.reshape(3, fsdp_size * tp_size, vec_size)
    small_sums = lax.dynamic_slice_in_dim(small_sums, fsdp_at * tp_size + tp_at, 1, axis=1)[:, 0]
    gain_sum, shift_sum, bias_sum = small_sums[0], small_sums[1], small_sums[2]
    up_b_sum = bias_sums[: 2 * mlp_cols].reshape(up_bias.shape[0], -1)
    up_b_sum = lax.dynamic_slice_in_dim(up_b_sum, fsdp_at * up_bias.shape[1], up_bias.shape[1], axis=1)
    qkv_b_sum = bias_sums[2 * mlp_cols :].reshape(3, qkv_bias.shape[1], -1)
    qkv_b_sum = lax.dynamic_slice_in_dim(qkv_b_sum, fsdp_at * qkv_bias.shape[2], qkv_bias.shape[2], axis=2)

    def qkv_columns(vals):
        return vals[:, :qkv_cols].reshape(shard_rows, pairs, 3, LANES).transpose(0, 2, 1, 3).reshape(
            shard_rows, 3, attn_cols
        )

    qkv_w_grad = jnp.concatenate([qkv_columns(half) for half in attn_grads], axis=2)
    out_w_grad = jnp.concatenate([half[:, qkv_cols:].T for half in attn_grads], axis=0)
    up_w_grad = jnp.concatenate(up_grads, axis=1)
    down_w_grad = jnp.concatenate([half.T for half in down_grads], axis=0)
    return (
        jnp.stack(outputs, axis=0)[:, None],
        jnp.stack(input_grads, axis=0)[:, None],
        gain_sum,
        shift_sum,
        qkv_w_grad,
        qkv_b_sum,
        out_w_grad,
        bias_sum,
        up_w_grad,
        up_b_sum,
        down_w_grad,
        bias_sum,
    )


def solution(mesh):
    return jax.shard_map(
        shards,
        mesh=mesh,
        in_specs=(
            P(None, "fsdp", "tp", None),
            P(("fsdp", "tp")),
            P(("fsdp", "tp")),
            P("fsdp", None, "tp"),
            P(None, "tp", "fsdp"),
            P("tp", "fsdp"),
            P(("fsdp", "tp")),
            P("fsdp", "tp"),
            P("tp", "fsdp"),
            P("tp", "fsdp"),
            P(("fsdp", "tp")),
            P(None, "fsdp", "tp", None),
        ),
        out_specs=(
            P(None, "fsdp", "tp", None),
            P(None, "fsdp", "tp", None),
            P(("fsdp", "tp")),
            P(("fsdp", "tp")),
            P("fsdp", None, "tp"),
            P(None, "tp", "fsdp"),
            P("tp", "fsdp"),
            P(("fsdp", "tp")),
            P("fsdp", "tp"),
            P("tp", "fsdp"),
            P("tp", "fsdp"),
            P(("fsdp", "tp")),
        ),
        check_vma=False,
    )
```

```python
import functools
import math

import jax
import jax.numpy as jnp
from jax import lax
from jax.experimental import pallas as pl
from jax.experimental.pallas import tpu as pltpu
from jax.sharding import PartitionSpec as P

ROT = 32
LANES = 128

norm_epsilon = 1e-05
gelu_factor = 0.7978845608028654
mask_fill = -1e30
BF = jnp.bfloat16
F32 = jnp.float32
VMEM_LIMIT = 56 * 1024 * 1024


def layer_norm(resid_rows, gain_vec, shift_vec):
    row_mean = jnp.mean(resid_rows, axis=-1, keepdims=True)
    centred = resid_rows - row_mean
    row_var = jnp.mean(centred * centred, axis=-1, keepdims=True)
    return centred * lax.rsqrt(row_var + norm_epsilon) * gain_vec + shift_vec


def gelu_tanh(inner):
    return 0.5 * inner * (1.0 + jnp.tanh(gelu_factor * (inner + 0.044715 * inner * inner * inner)))


def rotary_tables(length, head_dim, rot_dim):
    half_rot = rot_dim // 2
    inv_freq = 10000.0 ** (-2.0 * jnp.arange(half_rot, dtype=F32) / rot_dim)
    angles = jnp.arange(length, dtype=F32)[:, None] * inv_freq[None, :]
    cos, sin = jnp.cos(angles), jnp.sin(angles)
    rest = jnp.ones((length, head_dim - rot_dim), F32)
    cosine = jnp.concatenate([cos, cos, rest], axis=1)
    lower = jnp.concatenate([-sin, 0.0 * sin, 0.0 * rest], axis=1)
    upper = jnp.concatenate([0.0 * sin, sin, 0.0 * rest], axis=1)
    copies = LANES // head_dim
    return tuple(jnp.tile(table, (1, copies)) for table in (cosine, lower, upper))


def turn(vals, cosine, lower, upper):
    half_rot = ROT // 2
    ahead = pltpu.roll(vals, LANES - half_rot, 1)
    behind = pltpu.roll(vals, half_rot, 1)
    return vals * cosine + ahead * lower + behind * upper


def dot_rows(left, right):
    return lax.dot_general(left, right, (((0,), (0,)), ((), ())), preferred_element_type=F32)


def dot_cols(left, right):
    return lax.dot_general(left, right, (((1,), (1,)), ((), ())), preferred_element_type=F32)


def dot_plain(left, right):
    return lax.dot_general(left, right, (((1,), (0,)), ((), ())), preferred_element_type=F32)


def causal_fill(scores, first, fill):
    keys, cols = scores.shape
    key_ids = lax.broadcasted_iota(jnp.int32, (keys, cols), 0)
    query_ids = lax.broadcasted_iota(jnp.int32, (keys, cols), 1) + first
    return jnp.where(key_ids <= query_ids, scores, fill)


def head_lanes(vals, head, head_dim):
    lane_ids = lax.broadcasted_iota(jnp.int32, vals.shape, 1)
    return jnp.where(lane_ids // head_dim == head, vals, jnp.zeros_like(vals))


def attend_kernel(head_dim, block, qkv_ref, cos_ref, low_ref, up_ref, rot_ref, attn_ref, lse_ref):
    length = qkv_ref.shape[0]
    scale = 1.0 / math.sqrt(head_dim)
    tables = (cos_ref[...], low_ref[...], up_ref[...])
    queries = turn(qkv_ref[:, :LANES], *tables).astype(BF)
    keys = turn(qkv_ref[:, LANES : 2 * LANES], *tables).astype(BF)
    values = qkv_ref[:, 2 * LANES :].astype(BF)
    rot_ref[:, :LANES] = queries
    rot_ref[:, LANES : 2 * LANES] = keys
    rot_ref[:, 2 * LANES :] = values
    heads = LANES // head_dim
    for first in range(0, length, block):
        last = first + block
        total = jnp.zeros((block, LANES), F32)
        for head in range(heads):
            query_block = head_lanes(queries[first:last], head, head_dim)
            scores = dot_cols(keys[:last], query_block) * scale
            scores = causal_fill(scores, first, mask_fill)
            col_max = jnp.max(scores, axis=0, keepdims=True)
            exp_scores = jnp.exp(scores - col_max)
            denom = jnp.sum(exp_scores, axis=0, keepdims=True)
            prob_low = (exp_scores * (1.0 / denom)).astype(BF)
            total += dot_rows(prob_low, head_lanes(values[:last], head, head_dim))
            lse_ref[0, head : head + 1, first:last] = col_max + jnp.log(denom)
        attn_ref[first:last, :] = total.astype(BF)


def attend_back_kernel(head_dim, block, rot_ref, grad_ref, lse_ref, cos_ref, low_ref, up_ref, out_ref, key_acc, value_acc):
    length = rot_ref.shape[0]
    scale = 1.0 / math.sqrt(head_dim)
    tables = (cos_ref[...], -low_ref[...], -up_ref[...])
    heads = LANES // head_dim
    key_acc[...] = jnp.zeros_like(key_acc)
    value_acc[...] = jnp.zeros_like(value_acc)
    for first in range(0, length, block):
        last = first + block
        total = jnp.zeros((block, LANES), F32)
        for head in range(heads):
            query_block = head_lanes(rot_ref[first:last, :LANES], head, head_dim)
            grad_block = head_lanes(grad_ref[first:last, :], head, head_dim)
            keys = rot_ref[:last, LANES : 2 * LANES]
            scores = dot_cols(keys, query_block) * scale
            probs = jnp.exp(scores - lse_ref[0, head : head + 1, first:last])
            probs = causal_fill(probs, first, 0.0)
            value_acc[:last, :] += dot_plain(probs.astype(BF), grad_block)
            prob_grad = dot_cols(rot_ref[:last, 2 * LANES :], grad_block)
            inner_sum = jnp.sum(probs * prob_grad, axis=0, keepdims=True)
            score_grad = (probs * (prob_grad - inner_sum)).astype(BF)
            total += dot_rows(score_grad, head_lanes(keys, head, head_dim))
            key_acc[:last, :] += dot_plain(score_grad, query_block)
        out_ref[first:last, :LANES] = turn(total * scale, *(table[first:last] for table in tables)).astype(BF)
    out_ref[:, LANES : 2 * LANES] = turn(key_acc[...] * scale, *tables).astype(BF)
    out_ref[:, 2 * LANES :] = value_acc[...].astype(BF)


def attention_cost(seqs, pairs, length, matmuls):
    flops = seqs * pairs * matmuls * 2 * 2 * length * length * LANES
    return estimate(flops, seqs * pairs * length * LANES * 16)


def attend(qkv, tables, length, head_dim):
    tokens, width = qkv.shape
    seqs, pairs = tokens // length, width // (3 * LANES)
    heads = LANES // head_dim
    block = min(256, length)
    table_spec = pl.BlockSpec((length, LANES), lambda s, h: (0, 0))
    return pl.pallas_call(
        functools.partial(attend_kernel, head_dim, block),
        grid=(seqs, pairs),
        in_specs=[pl.BlockSpec((length, 3 * LANES), lambda s, h: (s, h))] + [table_spec] * 3,
        out_specs=[
            pl.BlockSpec((length, 3 * LANES), lambda s, h: (s, h)),
            pl.BlockSpec((length, LANES), lambda s, h: (s, h)),
            pl.BlockSpec((1, heads, length), lambda s, h: (s * pairs + h, 0, 0)),
        ],
        out_shape=[
            jax.ShapeDtypeStruct((tokens, width), BF),
            jax.ShapeDtypeStruct((tokens, pairs * LANES), BF),
            jax.ShapeDtypeStruct((seqs * pairs, heads, length), F32),
        ],
        compiler_params=pltpu.CompilerParams(vmem_limit_bytes=VMEM_LIMIT),
        cost_estimate=attention_cost(seqs, pairs, length, 3),
    )(qkv, *tables)


def attend_back(rot, attn_grad, lse, tables, length, head_dim):
    tokens, width = rot.shape
    seqs, pairs = tokens // length, width // (3 * LANES)
    heads = LANES // head_dim
    block = min(256, length)
    table_spec = pl.BlockSpec((length, LANES), lambda s, h: (0, 0))
    return pl.pallas_call(
        functools.partial(attend_back_kernel, head_dim, block),
        grid=(seqs, pairs),
        in_specs=[
            pl.BlockSpec((length, 3 * LANES), lambda s, h: (s, h)),
            pl.BlockSpec((length, LANES), lambda s, h: (s, h)),
            pl.BlockSpec((1, heads, length), lambda s, h: (s * pairs + h, 0, 0)),
        ]
        + [table_spec] * 3,
        out_specs=pl.BlockSpec((length, 3 * LANES), lambda s, h: (s, h)),
        out_shape=jax.ShapeDtypeStruct((tokens, width), BF),
        scratch_shapes=[pltpu.VMEM((length, LANES), F32), pltpu.VMEM((length, LANES), F32)],
        compiler_params=pltpu.CompilerParams(vmem_limit_bytes=VMEM_LIMIT),
        cost_estimate=attention_cost(seqs, pairs, length, 6),
    )(rot, attn_grad, lse, *tables)


def spec_rows(tile, width):
    return pl.BlockSpec((tile, width), lambda i, s: (i, 0))


def spec_whole(array):
    return pl.BlockSpec(array.shape, lambda i, s: (0,) * array.ndim)


def estimate(flops, moved):
    return pl.CostEstimate(flops=int(flops) // 64, bytes_accessed=int(moved) // 64, transcendentals=0)


def lined_dot(slots_ref, rows_ref, parts, cols):
    depth = parts[0].shape[0]
    total = None
    for at, part in enumerate(parts):
        first = pl.multiple_of(slots_ref[at] * depth, depth)
        piece = dot_plain(rows_ref[:, pl.ds(first, depth)], part[:, cols])
        total = piece if total is None else total + piece
    return total


def rows_call(kernel, slots, ins, in_specs, outs, tile, cost, out_specs=None):
    tokens = outs[0].shape[0]
    return pl.pallas_call(
        kernel,
        grid_spec=pltpu.PrefetchScalarGridSpec(
            num_scalar_prefetch=1,
            grid=(tokens // tile,),
            in_specs=in_specs,
            out_specs=out_specs or [spec_rows(tile, out.shape[1]) for out in outs],
        ),
        out_shape=outs,
        compiler_params=pltpu.CompilerParams(vmem_limit_bytes=VMEM_LIMIT),
        cost_estimate=cost,
    )(slots, *ins)


def norm_qkv(slots, rows, gain, shift, parts, bias):
    tokens, width = rows.shape
    cols, tile = bias.shape[1], 256

    def kernel(slots_ref, rows_ref, gain_ref, shift_ref, bias_ref, *refs):
        parts, (normed_ref, qkv_ref, stat_ref) = refs[:-3], refs[-3:]
        vals = rows_ref[...].astype(F32)
        mean = jnp.mean(vals, axis=-1, keepdims=True)
        centred = vals - mean
        var = jnp.mean(centred * centred, axis=-1, keepdims=True)
        scale = lax.rsqrt(var + norm_epsilon)
        normed_ref[...] = (centred * scale * gain_ref[...] + shift_ref[...]).astype(BF)
        lane_ids = lax.broadcasted_iota(jnp.int32, (tile, LANES), 1)
        stat_ref[...] = jnp.where(lane_ids == 0, mean, scale)
        qkv_ref[...] = lined_dot(slots_ref, normed_ref, parts, slice(0, cols)) + bias_ref[...]

    return rows_call(
        kernel,
        slots,
        [rows, gain, shift, bias, *parts],
        [spec_rows(tile, width)] + [spec_whole(array) for array in (gain, shift, bias, *parts)],
        [
            jax.ShapeDtypeStruct((tokens, width), BF),
            jax.ShapeDtypeStruct((tokens, cols), F32),
            jax.ShapeDtypeStruct((tokens, LANES), F32),
        ],
        tile,
        estimate(2 * tokens * width * cols, tokens * (4 * width + 4 * cols)),
    )


def up_act(slots, rows, parts, bias):
    tokens, width = rows.shape
    cols, tile, chunk = bias.shape[1], 512, 512

    def kernel(slots_ref, rows_ref, bias_ref, *refs):
        parts, (act_ref, slope_ref) = refs[:-2], refs[-2:]
        for at in range(0, cols, chunk):
            span = slice(at, at + chunk)
            pre = lined_dot(slots_ref, rows_ref, parts, span) + bias_ref[:, span]
            square = pre * pre
            tanh = jnp.tanh(gelu_factor * (pre * (1.0 + 0.044715 * square)))
            half = 0.5 * (1.0 + tanh)
            act_ref[:, span] = (pre * half).astype(BF)
            inner = gelu_factor * (1.0 + 3 * 0.044715 * square)
            slope_ref[:, span] = (half + 0.5 * pre * (1.0 - tanh * tanh) * inner).astype(BF)

    return rows_call(
        kernel,
        slots,
        [rows, bias, *parts],
        [spec_rows(tile, width)] + [spec_whole(array) for array in (bias, *parts)],
        [jax.ShapeDtypeStruct((tokens, cols), BF)] * 2,
        tile,
        estimate(2 * tokens * width * cols, tokens * (2 * width + 4 * cols)),
    )


def pre_grad_rows(slots, rows, parts, slope):
    tokens, width = rows.shape
    cols, tile = slope.shape[1], 512

    def kernel(slots_ref, rows_ref, slope_ref, *refs):
        parts, out_ref = refs[:-1], refs[-1]
        act_grad = lined_dot(slots_ref, rows_ref, parts, slice(0, cols))
        out_ref[...] = (act_grad * slope_ref[...].astype(F32)).astype(BF)

    return rows_call(
        kernel,
        slots,
        [rows, slope, *parts],
        [spec_rows(tile, width), spec_rows(tile, cols)] + [spec_whole(part) for part in parts],
        [jax.ShapeDtypeStruct((tokens, cols), BF)],
        tile,
        estimate(2 * tokens * width * cols, tokens * (2 * width + 4 * cols)),
    )[0]


def head_grad_rows(slots, rows, parts, first):
    tokens, width = rows.shape
    cols, tile = parts[0].shape[1] - first, 1024

    def kernel(slots_ref, rows_ref, *refs):
        parts, out_ref = refs[:-1], refs[-1]
        out_ref[...] = lined_dot(slots_ref, rows_ref, parts, slice(first, first + cols)).astype(BF)

    return rows_call(
        kernel,
        slots,
        [rows, *parts],
        [spec_rows(tile, width)] + [spec_whole(part) for part in parts],
        [jax.ShapeDtypeStruct((tokens, cols), BF)],
        tile,
        estimate(2 * tokens * width * cols, tokens * (2 * width + 2 * cols)),
    )[0]


def branch_rows(slots, one, one_parts, first, two, two_parts):
    tokens, cols = one.shape
    count, depth, tile = len(one_parts), one_parts[0].shape[0], 512
    width = count * depth

    def kernel(slots_ref, one_ref, two_ref, *refs):
        out_ref = refs[-1]
        for at in range(count):
            where = pl.multiple_of(slots_ref[at] * depth, depth)
            total = dot_cols(one_ref[...], refs[at][:, first : first + cols])
            total += dot_cols(two_ref[...], refs[count + at][...])
            out_ref[:, pl.ds(where, depth)] = total.astype(BF)

    return rows_call(
        kernel,
        slots,
        [one, two, *one_parts, *two_parts],
        [spec_rows(tile, cols), spec_rows(tile, two.shape[1])]
        + [spec_whole(part) for part in (*one_parts, *two_parts)],
        [jax.ShapeDtypeStruct((tokens, width), BF)],
        tile,
        estimate(2 * tokens * width * (cols + two.shape[1]), 2 * tokens * (width + cols + two.shape[1])),
    )[0]


def normed_grad_rows(slots, one, one_parts, two, two_parts, rows, stats):
    tokens, cols = one.shape
    count, depth, tile = len(one_parts), one_parts[0].shape[0], 512
    width = count * depth

    def kernel(slots_ref, one_ref, two_ref, rows_ref, stat_ref, *refs):
        out_ref, sum_ref = refs[-2:]

        @pl.when(pl.program_id(0) == 0)
        def _():
            sum_ref[...] = jnp.zeros_like(sum_ref)

        for at in range(count):
            where = pl.multiple_of(slots_ref[at] * depth, depth)
            span = pl.ds(where, depth)
            total = dot_cols(one_ref[...], refs[at][:, :cols])
            total += dot_cols(two_ref[...], refs[count + at][...])
            out_ref[:, span] = total.astype(BF)
            scaled = (rows_ref[:, span].astype(F32) - stat_ref[:, 0:1]) * stat_ref[:, 1:2]
            sum_ref[0:1, span] += jnp.sum(total * scaled, axis=0, keepdims=True)
            sum_ref[1:2, span] += jnp.sum(total, axis=0, keepdims=True)

    return rows_call(
        kernel,
        slots,
        [one, two, rows, stats, *one_parts, *two_parts],
        [spec_rows(tile, cols), spec_rows(tile, two.shape[1]), spec_rows(tile, width), spec_rows(tile, LANES)]
        + [spec_whole(part) for part in (*one_parts, *two_parts)],
        [jax.ShapeDtypeStruct((tokens, width), BF), jax.ShapeDtypeStruct((8, width), F32)],
        tile,
        estimate(2 * tokens * width * (cols + two.shape[1]), 2 * tokens * (2 * width + cols + two.shape[1])),
        [spec_rows(tile, width), pl.BlockSpec((8, width), lambda i, s: (0, 0))],
    )


def weight_grad(groups):
    tile, chunk = 512, 512
    micro_count = len(groups[0][0])
    tokens, width = groups[0][0][0].shape
    widths = [rights[0].shape[1] for _, rights in groups]
    cols, steps = sum(widths), tokens // tile
    arrays = [array for lefts, rights in groups for array in (*lefts, *rights)]

    def kernel(*refs):
        ins, out_ref, acc_ref = refs[: len(arrays)], refs[-2], refs[-1]
        step = pl.program_id(0)

        @pl.when(step == 0)
        def _():
            acc_ref[...] = jnp.zeros_like(acc_ref)

        for micro in range(micro_count):

            @pl.when(step // steps == micro)
            def _():
                first = 0
                for at, span in enumerate(widths):
                    left = ins[2 * micro_count * at + micro]
                    right = ins[2 * micro_count * at + micro_count + micro]
                    for row in range(0, width, chunk):
                        acc_ref[row : row + chunk, first : first + span] += dot_rows(
                            left[:, row : row + chunk], right[...]
                        )
                    first += span

        @pl.when(step == micro_count * steps - 1)
        def _():
            out_ref[...] = acc_ref[...].astype(BF)

    def side(micro, span):
        return pl.BlockSpec((tile, span), lambda i: (jnp.clip(i - micro * steps, 0, steps - 1), 0))

    in_specs = []
    for span in widths:
        in_specs += [side(micro, width) for micro in range(micro_count)]
        in_specs += [side(micro, span) for micro in range(micro_count)]
    return pl.pallas_call(
        kernel,
        grid=(micro_count * steps,),
        in_specs=in_specs,
        out_specs=pl.BlockSpec((width, cols), lambda i: (0, 0)),
        out_shape=jax.ShapeDtypeStruct((width, cols), BF),
        scratch_shapes=[pltpu.VMEM((width, cols), F32)],
        compiler_params=pltpu.CompilerParams(vmem_limit_bytes=VMEM_LIMIT),
        cost_estimate=estimate(
            2 * micro_count * tokens * width * cols, 2 * micro_count * tokens * (len(groups) * width + cols)
        ),
    )(*arrays)


def shards(
    inputs,
    ln_gain,
    ln_bias,
    qkv_weight,
    qkv_bias,
    out_weight,
    out_bias,
    up_weight,
    up_bias,
    down_weight,
    down_bias,
    cotangent,
):
    micro_count, _, token_rows, model_width = inputs.shape
    fsdp_size, tp_size = lax.axis_size("fsdp"), lax.axis_size("tp")
    line = fsdp_size // 2
    fsdp_at, tp_at = lax.axis_index("fsdp"), lax.axis_index("tp")
    line_at, pair_at = fsdp_at >> 1, fsdp_at & 1
    plane_size = 2 * tp_size
    planes = [[plane * plane_size + i for i in range(plane_size)] for plane in range(line)]
    ring = [(f, ((f // 2 + 1) % line) * 2 + f % 2) for f in range(fsdp_size)]
    length = token_rows * tp_size
    head_dim = qkv_bias.shape[2] * fsdp_size
    shard_rows = model_width // fsdp_size
    line_rows = 2 * shard_rows
    attn_cols = out_weight.shape[0] // 2
    qkv_cols = 3 * attn_cols
    pairs = attn_cols // LANES
    mlp_cols = up_weight.shape[1] // 2
    both_axes = ("fsdp", "tp")

    def swap_pair(vals):
        return lax.ppermute(vals, "fsdp", [(f, f ^ 1) for f in range(fsdp_size)])

    def gather_plane(vals):
        return lax.all_gather(vals, both_axes, axis=0, tiled=True, axis_index_groups=planes)

    def scatter_plane(vals):
        return lax.psum_scatter(vals, both_axes, scatter_dimension=0, tiled=True, axis_index_groups=planes)

    def after(vals, *others):
        return lax.optimization_barrier((vals,) + others)[0]

    def doubled(cur, axis, size, at, bit):
        other = lax.ppermute(cur, axis, [(i, i ^ bit) for i in range(size)])
        upper = (at & bit) != 0
        return jnp.where(upper, jnp.concatenate([other, cur]), jnp.concatenate([cur, other]))

    def sum_small(everywhere, over_fsdp):
        cur = everywhere
        bit = 1
        while bit < tp_size:
            cur = cur + lax.ppermute(cur, "tp", [(t, t ^ bit) for t in range(tp_size)])
            bit *= 2
        cur = jnp.concatenate([cur, over_fsdp])
        bit = 1
        while bit < fsdp_size:
            cur = cur + lax.ppermute(cur, "fsdp", [(f, f ^ bit) for f in range(fsdp_size)])
            bit *= 2
        return cur[: everywhere.shape[0]], cur[everywhere.shape[0] :]

    small = jnp.concatenate(
        [vec.reshape(-1) for vec in (ln_gain, ln_bias, out_bias, down_bias, qkv_bias, up_bias)]
    )
    small_all = small[None]
    for bit in range(tp_size.bit_length() - 1):
        small_all = doubled(small_all, "tp", tp_size, tp_at, 1 << bit)
    small_near = small_all
    def attn_half(half):
        qkv_part = lax.dynamic_slice_in_dim(qkv_weight, half * attn_cols, attn_cols, axis=2)
        qkv_part = qkv_part.reshape(shard_rows, 3, pairs, LANES).transpose(0, 2, 1, 3)
        out_part = lax.dynamic_slice_in_dim(out_weight, half * attn_cols, attn_cols, axis=0)
        return jnp.concatenate([qkv_part.reshape(shard_rows, qkv_cols), out_part.T], axis=1)

    def up_half(half):
        return lax.dynamic_slice_in_dim(up_weight, half * mlp_cols, mlp_cols, axis=1)

    def down_half(half):
        return lax.dynamic_slice_in_dim(down_weight, half * mlp_cols, mlp_cols, axis=0).T

    def pair_join(own, other):
        return jnp.where(pair_at == 0, jnp.concatenate([own, other]), jnp.concatenate([other, own]))

    def pair_shard(half_of, *behind):
        own = half_of(pair_at)
        other = swap_pair(after(half_of(1 - pair_at), *behind))
        return pair_join(own, other)

    class Box:
        def __init__(self, val):
            self.val = val

    class Line:
        tokens = []

        def tie(self, *boxes):
            held = []
            for box in (*boxes, *self.tokens):
                if box not in held:
                    held.append(box)
            if len(held) > 1:
                for box, val in zip(held, lax.optimization_barrier(tuple(box.val for box in held))):
                    box.val = val

        def run(self, piece, *boxes):
            self.tie(*boxes)
            results = [Box(val) for val in piece(*(box.val for box in boxes))]
            self.tokens = [results[0]]
            return results

        def sync(self, box):
            self.tokens = self.tokens + [box]

    order = Line()

    class Gather:
        def __init__(self, shard):
            self.parts = [shard]

        def move(self):
            if len(self.parts) < line:
                order.tie(self.parts[-1])
                self.parts.append(Box(lax.ppermute(self.parts[-1].val, "fsdp", ring)))

        def sync(self):
            order.sync(self.parts[-1])

        def finish(self):
            while len(self.parts) < line:
                self.move()
            self.sync()

        def vals(self):
            return [part.val for part in self.parts]

    class Scatter:
        def __init__(self, part):
            self.part, self.step = part, 1
            self.moving = Box(self.own().astype(BF))

        def own(self):
            at_line = lax.rem(line_at + line - self.step, line)
            return lax.dynamic_slice_in_dim(self.part.val, at_line * line_rows, line_rows, axis=0).astype(F32)

        def move(self):
            if self.step < line:
                self.step += 1
                order.tie(self.moving)
                came = lax.ppermute(self.moving.val, "fsdp", ring).astype(F32) + self.own()
                self.moving = Box(came.astype(BF) if self.step < line else came)

        def sync(self):
            order.sync(self.moving)

        def swap(self):
            while self.step < line:
                self.move()
            order.tie(self.moving)
            total = self.moving.val
            self.keep = lax.dynamic_slice_in_dim(total, pair_at * shard_rows, shard_rows, axis=0)
            give = lax.dynamic_slice_in_dim(total, (1 - pair_at) * shard_rows, shard_rows, axis=0)
            self.got = Box(swap_pair(give.astype(BF)))

        def halves(self):
            got = self.got.val.astype(F32)
            return jnp.where(pair_at == 0, self.keep, got), jnp.where(pair_at == 0, got, self.keep)

    resid = [inputs[m].reshape(token_rows, model_width) for m in range(micro_count)]
    cots = [cotangent[m].reshape(token_rows, model_width) for m in range(micro_count)]
    micros = range(micro_count)
    plane_rows, plane_cots = [None] * micro_count, [None] * micro_count

    def gather_behind(rows):
        sent = Box(rows)
        order.tie(sent)
        return Box(gather_plane(sent.val))

    def small_step(small_all, bit):
        if bit < fsdp_size.bit_length() - 1:
            order.tie(small_all)
            return Box(doubled(small_all.val, "fsdp", fsdp_size, fsdp_at, 1 << bit))
        return small_all

    small_all = Box(small_near)
    order.tokens = [small_all]
    plane_rows[0] = gather_behind(resid[0])
    attn_shard = Box(pair_shard(attn_half))
    order.tokens = [attn_shard]
    plane_rows[1] = gather_behind(resid[1])
    attn_ring = Gather(attn_shard)
    attn_ring.move()
    small_all = small_step(small_all, 0)
    attn_ring.sync()
    order.sync(small_all)
    up_send = Box(up_half(1 - pair_at))
    order.tie(up_send)
    up_shard = Box(pair_join(up_half(pair_at), swap_pair(up_send.val)))
    attn_ring.move()
    small_all = small_step(small_all, 1)
    attn_ring.sync()
    order.sync(small_all)
    order.sync(up_shard)
    plane_cots[0] = gather_behind(cots[0])
    down_send = Box(down_half(1 - pair_at))
    order.tie(down_send)
    down_shard = Box(pair_join(down_half(pair_at), swap_pair(down_send.val)))
    attn_ring.move()
    for bit in range(2, fsdp_size.bit_length() - 1):
        small_all = small_step(small_all, bit)
    attn_ring.finish()
    order.sync(small_all)
    order.tie()
    small_all = small_all.val
    vec_size = ln_gain.shape[0]
    gain_vec, shift_vec, bias_out, bias_down = (
        small_all[:, i * vec_size : (i + 1) * vec_size].reshape(-1).astype(F32) for i in range(4)
    )
    bias_both = bias_out + bias_down
    mine = lax.dynamic_slice_in_dim(
        small_all.reshape(fsdp_size, tp_size, -1), tp_at, 1, axis=1
    )[:, 0].astype(F32)
    at = 4 * vec_size
    qkv_b = mine[:, at : at + qkv_bias.size].reshape(fsdp_size, 3, 2, pairs, -1, qkv_bias.shape[2])
    qkv_b = lax.dynamic_slice_in_dim(qkv_b, pair_at, 1, axis=2)[:, :, 0]
    qkv_b = qkv_b.transpose(2, 1, 3, 0, 4).reshape(1, qkv_cols)
    at += qkv_bias.size
    up_b = mine[:, at:].reshape(fsdp_size, up_bias.shape[0], up_bias.shape[1])
    up_b = up_b.transpose(1, 0, 2).reshape(2, mlp_cols)
    up_b = lax.dynamic_slice_in_dim(up_b, pair_at, 1, axis=0)

    slots = jnp.stack([lax.rem(line_at + line - step, line) for step in range(line)]).astype(jnp.int32)
    tables = rotary_tables(length, head_dim, ROT)
    gain_row, shift_row = gain_vec[None], shift_vec[None]
    normed, qkvs, stats, rots, attns, lses, acts, slopes = ([None] * micro_count for _ in range(8))
    pre_grads, qkv_grads, back, sums, branches, attn_heads = ([None] * micro_count for _ in range(6))

    def norm_piece(m):
        normed[m], qkvs[m], stats[m] = order.run(
            lambda rows: norm_qkv(slots, rows, gain_row, shift_row, attn_ring.vals(), qkv_b), plane_rows[m]
        )

    def attend_piece(m):
        rots[m], attns[m], lses[m] = order.run(
            lambda vals: attend(vals, tables, length, head_dim), qkvs[m]
        )

    def up_piece(m):
        acts[m], slopes[m] = order.run(lambda rows: up_act(slots, rows, up_ring.vals(), up_b), normed[m])

    def head_grad_piece(m):
        (attn_heads[m],) = order.run(
            lambda cot: [head_grad_rows(slots, cot, attn_ring.vals(), qkv_cols)], plane_cots[m]
        )

    def attend_back_piece(m):
        (qkv_grads[m],) = order.run(
            lambda rot, grad, lse: [attend_back(rot, grad, lse, tables, length, head_dim)],
            rots[m],
            attn_heads[m],
            lses[m],
        )

    def pre_grad_piece(m):
        (pre_grads[m],) = order.run(
            lambda cot, slope: [pre_grad_rows(slots, cot, down_ring.vals(), slope)], plane_cots[m], slopes[m]
        )

    def weight_piece(*groups):
        flat = [box for lefts, rights in groups for box in (*lefts, *rights)]

        def piece(*flat):
            count = 2 * micro_count
            return [
                weight_grad(
                    [
                        (flat[at : at + micro_count], flat[at + micro_count : at + count])
                        for at in range(0, len(flat), count)
                    ]
                )
            ]

        return Scatter(order.run(piece, *flat)[0])

    def branch_piece(m):
        (branches[m],) = order.run(
            lambda attn, act: [branch_rows(slots, attn, attn_ring.vals(), qkv_cols, act, down_ring.vals())],
            attns[m],
            acts[m],
        )

    def normed_grad_piece(m):
        back[m], sums[m] = order.run(
            lambda one, two, rows, stat: normed_grad_rows(
                slots, one, attn_ring.vals(), two, up_ring.vals(), rows, stat
            ),
            qkv_grads[m],
            pre_grads[m],
            plane_rows[m],
            stats[m],
        )

    def scatter_behind(box):
        order.tie(box)
        return Box(scatter_plane(box.val))

    up_ring, down_ring = Gather(up_shard), Gather(down_shard)
    order.sync(down_shard)
    up_ring.move()
    norm_piece(0)
    up_ring.sync()
    plane_cots[1] = gather_behind(cots[1])
    up_ring.move()
    attend_piece(0)
    norm_piece(1)
    up_ring.sync()
    up_ring.move()
    attend_piece(1)
    head_grad_piece(0)
    up_ring.finish()
    down_ring.move()
    up_piece(0)
    down_ring.sync()
    down_ring.move()
    up_piece(1)
    down_ring.sync()
    down_ring.move()
    attend_back_piece(0)
    down_ring.finish()

    down_scatter = weight_piece((plane_cots, acts))
    down_scatter.move()
    pre_grad_piece(0)
    branch_piece(0)
    down_scatter.sync()
    branch_sums = [scatter_behind(branches[0])]
    down_scatter.move()
    pre_grad_piece(1)
    branch_piece(1)
    down_scatter.sync()
    branch_sums.append(scatter_behind(branches[1]))
    down_scatter.move()
    up_scatter = weight_piece((normed, pre_grads))
    down_scatter.sync()
    order.sync(branch_sums[0])
    down_scatter.swap()
    up_scatter.move()
    head_grad_piece(1)
    normed_grad_piece(0)
    up_scatter.sync()
    back_sums = [scatter_behind(back[0])]
    up_scatter.move()
    attend_back_piece(1)
    up_scatter.sync()
    order.sync(down_scatter.got)
    up_scatter.move()
    attn_scatter = weight_piece((normed, qkv_grads), (plane_cots, attns))
    up_scatter.sync()
    order.sync(branch_sums[1])
    up_scatter.swap()
    attn_scatter.move()
    normed_grad_piece(1)
    attn_scatter.sync()
    back_sums.append(scatter_behind(back[1]))
    attn_scatter.move()
    order.sync(up_scatter.got)
    attn_scatter.sync()
    attn_scatter.move()
    attn_scatter.swap()
    attn_grads, up_grads, down_grads = attn_scatter.halves(), up_scatter.halves(), down_scatter.halves()

    outputs, input_grads = [], []
    bias_total = jnp.zeros((model_width,), F32)
    for m in micros:
        outputs.append((resid[m].astype(F32) + branch_sums[m].val.astype(F32) + bias_both).astype(BF))
        vals, cot = resid[m].astype(F32), cots[m].astype(F32)
        pull_back = jax.vjp(lambda vals: layer_norm(vals, gain_vec, shift_vec), vals)[1]
        input_grads.append((cot + pull_back(back_sums[m].val.astype(F32))[0]).astype(BF))
        bias_total += jnp.sum(cot, axis=0)
    gain_total, shift_total = (sum(part.val[i] for part in sums) for i in range(2))

    up_b_grad = sum(jnp.sum(pre_grads[m].val.astype(F32), axis=0) for m in micros)
    qkv_b_grad = sum(jnp.sum(qkv_grads[m].val.astype(F32), axis=0) for m in micros)
    qkv_b_grad = qkv_b_grad.reshape(pairs, 3, -1).transpose(1, 0, 2).reshape(3, attn_cols)

    def in_half(vals):
        blank = jnp.zeros_like(vals)
        return jnp.where(
            pair_at == 0, jnp.concatenate([vals, blank], axis=-1), jnp.concatenate([blank, vals], axis=-1)
        )

    small_sums, bias_sums = sum_small(
        jnp.concatenate([gain_total, shift_total, bias_total]),
        jnp.concatenate([in_half(up_b_grad), in_half(qkv_b_grad).reshape(-1)]),
    )
    small_sums = small_sums.reshape(3, fsdp_size * tp_size, vec_size)
    small_sums = lax.dynamic_slice_in_dim(small_sums, fsdp_at * tp_size + tp_at, 1, axis=1)[:, 0]
    gain_sum, shift_sum, bias_sum = small_sums[0], small_sums[1], small_sums[2]
    up_b_sum = bias_sums[: 2 * mlp_cols].reshape(up_bias.shape[0], -1)
    up_b_sum = lax.dynamic_slice_in_dim(up_b_sum, fsdp_at * up_bias.shape[1], up_bias.shape[1], axis=1)
    qkv_b_sum = bias_sums[2 * mlp_cols :].reshape(3, qkv_bias.shape[1], -1)
    qkv_b_sum = lax.dynamic_slice_in_dim(qkv_b_sum, fsdp_at * qkv_bias.shape[2], qkv_bias.shape[2], axis=2)

    def qkv_columns(vals):
        return vals[:, :qkv_cols].reshape(shard_rows, pairs, 3, LANES).transpose(0, 2, 1, 3).reshape(
            shard_rows, 3, attn_cols
        )

    qkv_w_grad = jnp.concatenate([qkv_columns(half) for half in attn_grads], axis=2)
    out_w_grad = jnp.concatenate([half[:, qkv_cols:].T for half in attn_grads], axis=0)
    up_w_grad = jnp.concatenate(up_grads, axis=1)
    down_w_grad = jnp.concatenate([half.T for half in down_grads], axis=0)
    return (
        jnp.stack(outputs, axis=0)[:, None],
        jnp.stack(input_grads, axis=0)[:, None],
        gain_sum,
        shift_sum,
        qkv_w_grad,
        qkv_b_sum,
        out_w_grad,
        bias_sum,
        up_w_grad,
        up_b_sum,
        down_w_grad,
        bias_sum,
    )


def solution(mesh):
    return jax.shard_map(
        shards,
        mesh=mesh,
        in_specs=(
            P(None, "fsdp", "tp", None),
            P(("fsdp", "tp")),
            P(("fsdp", "tp")),
            P("fsdp", None, "tp"),
            P(None, "tp", "fsdp"),
            P("tp", "fsdp"),
            P(("fsdp", "tp")),
            P("fsdp", "tp"),
            P("tp", "fsdp"),
            P("tp", "fsdp"),
            P(("fsdp", "tp")),
            P(None, "fsdp", "tp", None),
        ),
        out_specs=(
            P(None, "fsdp", "tp", None),
            P(None, "fsdp", "tp", None),
            P(("fsdp", "tp")),
            P(("fsdp", "tp")),
            P("fsdp", None, "tp"),
            P(None, "tp", "fsdp"),
            P("tp", "fsdp"),
            P(("fsdp", "tp")),
            P("fsdp", "tp"),
            P("tp", "fsdp"),
            P("tp", "fsdp"),
            P(("fsdp", "tp")),
        ),
        check_vma=False,
    )
```

```python
import functools
import math

import jax
import jax.numpy as jnp
from jax import lax
from jax.experimental import pallas as pl
from jax.experimental.pallas import tpu as pltpu
from jax.sharding import PartitionSpec as P

ROT = 32
LANES = 128

norm_epsilon = 1e-05
gelu_factor = 0.7978845608028654
mask_fill = -1e30
BF = jnp.bfloat16
F32 = jnp.float32
VMEM_LIMIT = 56 * 1024 * 1024


def layer_norm(resid_rows, gain_vec, shift_vec):
    row_mean = jnp.mean(resid_rows, axis=-1, keepdims=True)
    centred = resid_rows - row_mean
    row_var = jnp.mean(centred * centred, axis=-1, keepdims=True)
    return centred * lax.rsqrt(row_var + norm_epsilon) * gain_vec + shift_vec


def gelu_tanh(inner):
    return 0.5 * inner * (1.0 + jnp.tanh(gelu_factor * (inner + 0.044715 * inner * inner * inner)))


def rotary_tables(length, head_dim, rot_dim):
    half_rot = rot_dim // 2
    inv_freq = 10000.0 ** (-2.0 * jnp.arange(half_rot, dtype=F32) / rot_dim)
    angles = jnp.arange(length, dtype=F32)[:, None] * inv_freq[None, :]
    cos, sin = jnp.cos(angles), jnp.sin(angles)
    rest = jnp.ones((length, head_dim - rot_dim), F32)
    cosine = jnp.concatenate([cos, cos, rest], axis=1)
    lower = jnp.concatenate([-sin, 0.0 * sin, 0.0 * rest], axis=1)
    upper = jnp.concatenate([0.0 * sin, sin, 0.0 * rest], axis=1)
    copies = LANES // head_dim
    return tuple(jnp.tile(table, (1, copies)) for table in (cosine, lower, upper))


def turn(vals, cosine, lower, upper):
    half_rot = ROT // 2
    ahead = pltpu.roll(vals, LANES - half_rot, 1)
    behind = pltpu.roll(vals, half_rot, 1)
    return vals * cosine + ahead * lower + behind * upper


def dot_rows(left, right):
    return lax.dot_general(left, right, (((0,), (0,)), ((), ())), preferred_element_type=F32)


def dot_cols(left, right):
    return lax.dot_general(left, right, (((1,), (1,)), ((), ())), preferred_element_type=F32)


def dot_plain(left, right):
    return lax.dot_general(left, right, (((1,), (0,)), ((), ())), preferred_element_type=F32)


def head_lanes(vals, head, head_dim):
    lane_ids = lax.broadcasted_iota(jnp.int32, vals.shape, 1)
    return jnp.where(lane_ids // head_dim == head, vals, jnp.zeros_like(vals))


def seen_keys(block):
    key_ids = lax.broadcasted_iota(jnp.int32, (block, block), 0)
    return key_ids <= lax.broadcasted_iota(jnp.int32, (block, block), 1)


def attend_kernel(head_dim, block, qkv_ref, cos_ref, low_ref, up_ref, rot_ref, attn_ref, lse_ref):
    length = qkv_ref.shape[0]
    scale = 1.0 / math.sqrt(head_dim)
    tables = (cos_ref[...], low_ref[...], up_ref[...])
    rot_ref[:, :LANES] = turn(qkv_ref[:, :LANES], *tables).astype(BF) * BF(scale)
    rot_ref[:, LANES : 2 * LANES] = turn(qkv_ref[:, LANES : 2 * LANES], *tables).astype(BF)
    rot_ref[:, 2 * LANES :] = qkv_ref[:, 2 * LANES :].astype(BF)
    heads = LANES // head_dim
    seen = seen_keys(block)
    for first in range(0, length, block):
        last = first + block
        total = jnp.zeros((block, LANES), F32)
        for head in range(heads):
            query_block = head_lanes(rot_ref[first:last, :LANES], head, head_dim)
            scores = jnp.where(seen, dot_cols(rot_ref[first:last, LANES : 2 * LANES], query_block), mask_fill)
            col_max = jnp.max(scores, axis=0, keepdims=True)
            if first:
                before = dot_cols(rot_ref[:first, LANES : 2 * LANES], query_block)
                col_max = jnp.maximum(col_max, jnp.max(before, axis=0, keepdims=True))
            probs = jnp.exp(scores - col_max)
            denom = jnp.sum(probs, axis=0, keepdims=True)
            part = dot_rows(probs.astype(BF), head_lanes(rot_ref[first:last, 2 * LANES :], head, head_dim))
            if first:
                probs = jnp.exp(before - col_max)
                denom += jnp.sum(probs, axis=0, keepdims=True)
                part += dot_rows(probs.astype(BF), head_lanes(rot_ref[:first, 2 * LANES :], head, head_dim))
            total += part * jnp.broadcast_to(1.0 / denom, (LANES, block)).T
            lse_ref[0, head : head + 1, first:last] = col_max + jnp.log(denom)
        attn_ref[first:last, :] = total.astype(BF)


def attend_back_kernel(head_dim, block, rot_ref, grad_ref, attn_ref, lse_ref, cos_ref, low_ref, up_ref, out_ref, sum_ref, key_acc, value_acc):
    length = rot_ref.shape[0]
    scale = 1.0 / math.sqrt(head_dim)
    heads = LANES // head_dim
    seen = seen_keys(block)

    def back(vals, span):
        return turn(vals, cos_ref[span, :], -low_ref[span, :], -up_ref[span, :])

    query_sum = jnp.zeros((1, LANES), F32)
    key_acc[...] = jnp.zeros_like(key_acc)
    value_acc[...] = jnp.zeros_like(value_acc)
    for first in range(0, length, block):
        last = first + block
        total = jnp.zeros((block, LANES), F32)
        inner = (grad_ref[first:last, :].astype(F32) * attn_ref[first:last, :].astype(F32)).T
        for head in range(heads):
            query_block = head_lanes(rot_ref[first:last, :LANES], head, head_dim)
            grad_block = head_lanes(grad_ref[first:last, :], head, head_dim)
            lse = lse_ref[0, head : head + 1, first:last]
            inner_sum = jnp.sum(inner[head * head_dim : (head + 1) * head_dim], axis=0, keepdims=True)
            for start, stop in ((0, first), (first, last)):
                if start == stop:
                    continue
                keys = rot_ref[start:stop, LANES : 2 * LANES]
                probs = jnp.exp(dot_cols(keys, query_block) - lse)
                if start == first:
                    probs = jnp.where(seen, probs, 0.0)
                value_acc[start:stop, :] += dot_plain(probs.astype(BF), grad_block)
                prob_grad = dot_cols(rot_ref[start:stop, 2 * LANES :], grad_block)
                score_grad = (probs * (prob_grad - inner_sum)).astype(BF)
                total += dot_rows(score_grad, head_lanes(keys, head, head_dim))
                key_acc[start:stop, :] += dot_plain(score_grad, query_block)
        turned = back(total * scale, slice(first, last))
        query_sum += jnp.sum(turned, axis=0, keepdims=True)
        out_ref[first:last, :LANES] = turned.astype(BF)
    turned = back(key_acc[...], slice(0, length))
    out_ref[:, LANES : 2 * LANES] = turned.astype(BF)
    out_ref[:, 2 * LANES :] = value_acc[...].astype(BF)
    sum_ref[0:1, :LANES] = query_sum
    sum_ref[0:1, LANES : 2 * LANES] = jnp.sum(turned, axis=0, keepdims=True)
    sum_ref[0:1, 2 * LANES :] = jnp.sum(value_acc[...], axis=0, keepdims=True)


def attention_cost(seqs, pairs, length, matmuls):
    flops = seqs * pairs * matmuls * 2 * 2 * length * length * LANES
    return estimate(flops, seqs * pairs * length * LANES * 16)


def attend(qkv, tables, length, head_dim):
    tokens, width = qkv.shape
    seqs, pairs = tokens // length, width // (3 * LANES)
    heads = LANES // head_dim
    block = min(512, length)
    table_spec = pl.BlockSpec((length, LANES), lambda s, h: (0, 0))
    return pl.pallas_call(
        functools.partial(attend_kernel, head_dim, block),
        grid=(seqs, pairs),
        in_specs=[pl.BlockSpec((length, 3 * LANES), lambda s, h: (s, h))] + [table_spec] * 3,
        out_specs=[
            pl.BlockSpec((length, 3 * LANES), lambda s, h: (s, h)),
            pl.BlockSpec((length, LANES), lambda s, h: (s, h)),
            pl.BlockSpec((1, heads, length), lambda s, h: (s * pairs + h, 0, 0)),
        ],
        out_shape=[
            jax.ShapeDtypeStruct((tokens, width), BF),
            jax.ShapeDtypeStruct((tokens, pairs * LANES), BF),
            jax.ShapeDtypeStruct((seqs * pairs, heads, length), F32),
        ],
        compiler_params=pltpu.CompilerParams(vmem_limit_bytes=VMEM_LIMIT),
        cost_estimate=attention_cost(seqs, pairs, length, 3),
    )(qkv, *tables)


def attend_back(rot, attn_grad, attn, lse, tables, length, head_dim):
    tokens, width = rot.shape
    seqs, pairs = tokens // length, width // (3 * LANES)
    heads = LANES // head_dim
    block = min(512, length)
    table_spec = pl.BlockSpec((length, LANES), lambda s, h: (0, 0))
    return pl.pallas_call(
        functools.partial(attend_back_kernel, head_dim, block),
        grid=(seqs, pairs),
        in_specs=[
            pl.BlockSpec((length, 3 * LANES), lambda s, h: (s, h)),
            pl.BlockSpec((length, LANES), lambda s, h: (s, h)),
            pl.BlockSpec((length, LANES), lambda s, h: (s, h)),
            pl.BlockSpec((1, heads, length), lambda s, h: (s * pairs + h, 0, 0)),
        ]
        + [table_spec] * 3,
        out_specs=[
            pl.BlockSpec((length, 3 * LANES), lambda s, h: (s, h)),
            pl.BlockSpec((8, 3 * LANES), lambda s, h: (s, h)),
        ],
        out_shape=[jax.ShapeDtypeStruct((tokens, width), BF), jax.ShapeDtypeStruct((8 * seqs, width), F32)],
        scratch_shapes=[pltpu.VMEM((length, LANES), F32), pltpu.VMEM((length, LANES), F32)],
        compiler_params=pltpu.CompilerParams(vmem_limit_bytes=VMEM_LIMIT),
        cost_estimate=attention_cost(seqs, pairs, length, 6),
    )(rot, attn_grad, attn, lse, *tables)


def spec_rows(tile, width):
    return pl.BlockSpec((tile, width), lambda i, s: (i, 0))


def spec_whole(array):
    return pl.BlockSpec(array.shape, lambda i, s: (0,) * array.ndim)


def estimate(flops, moved):
    return pl.CostEstimate(flops=int(flops) // 64, bytes_accessed=int(moved) // 64, transcendentals=0)


def lined_dot(slots_ref, rows_ref, parts, cols):
    depth = parts[0].shape[0]
    total = None
    for at, part in enumerate(parts):
        first = pl.multiple_of(slots_ref[at] * depth, depth)
        piece = dot_plain(rows_ref[:, pl.ds(first, depth)], part[:, cols])
        total = piece if total is None else total + piece
    return total


def rows_call(kernel, slots, ins, in_specs, outs, tile, cost, out_specs=None, steps=None):
    return pl.pallas_call(
        kernel,
        grid_spec=pltpu.PrefetchScalarGridSpec(
            num_scalar_prefetch=1,
            grid=(steps or outs[0].shape[0] // tile,),
            in_specs=in_specs,
            out_specs=out_specs or [spec_rows(tile, out.shape[1]) for out in outs],
        ),
        out_shape=outs,
        compiler_params=pltpu.CompilerParams(vmem_limit_bytes=VMEM_LIMIT),
        cost_estimate=cost,
    )(slots, *ins)


def norm_qkv(slots, rows, gain, shift, parts, bias):
    tokens, width = rows.shape
    cols, tile = bias.shape[1], 256

    def kernel(slots_ref, rows_ref, gain_ref, shift_ref, bias_ref, *refs):
        parts, (normed_ref, qkv_ref, stat_ref) = refs[:-3], refs[-3:]
        vals = rows_ref[...].astype(F32)
        mean = jnp.mean(vals, axis=-1, keepdims=True)
        centred = vals - mean
        var = jnp.mean(centred * centred, axis=-1, keepdims=True)
        scale = lax.rsqrt(var + norm_epsilon)
        normed_ref[...] = (centred * scale * gain_ref[...] + shift_ref[...]).astype(BF)
        lane_ids = lax.broadcasted_iota(jnp.int32, (tile, LANES), 1)
        stat_ref[...] = jnp.where(lane_ids == 0, mean, scale)
        qkv_ref[...] = lined_dot(slots_ref, normed_ref, parts, slice(0, cols)) + bias_ref[...]

    return rows_call(
        kernel,
        slots,
        [rows, gain, shift, bias, *parts],
        [spec_rows(tile, width)] + [spec_whole(array) for array in (gain, shift, bias, *parts)],
        [
            jax.ShapeDtypeStruct((tokens, width), BF),
            jax.ShapeDtypeStruct((tokens, cols), F32),
            jax.ShapeDtypeStruct((tokens, LANES), F32),
        ],
        tile,
        estimate(2 * tokens * width * cols, tokens * (4 * width + 4 * cols)),
    )


def micro_spec(micro, steps, tile, width):
    return pl.BlockSpec((tile, width), lambda i, s: (jnp.clip(i - micro * steps, 0, steps - 1), 0))


def up_act(slots, rows, parts, bias):
    count = len(rows)
    tokens, width = rows[0].shape
    cols, tile, chunk = bias.shape[1], 512, 512
    steps = tokens // tile

    def kernel(slots_ref, bias_ref, *refs):
        ins, parts, outs = refs[:count], refs[count : -2 * count], refs[-2 * count :]
        for micro in range(count):

            @pl.when(pl.program_id(0) // steps == micro)
            def _():
                for at in range(0, cols, chunk):
                    span = slice(at, at + chunk)
                    pre = lined_dot(slots_ref, ins[micro], parts, span) + bias_ref[:, span]
                    square = pre * pre
                    tanh = jnp.tanh(gelu_factor * (pre * (1.0 + 0.044715 * square)))
                    half = 0.5 * (1.0 + tanh)
                    outs[micro][:, span] = (pre * half).astype(BF)
                    inner = gelu_factor * (1.0 + 3 * 0.044715 * square)
                    slope = half + 0.5 * pre * (1.0 - tanh * tanh) * inner
                    outs[count + micro][:, span] = slope.astype(BF)

    outs = rows_call(
        kernel,
        slots,
        [bias, *rows, *parts],
        [spec_whole(bias)]
        + [micro_spec(m, steps, tile, width) for m in range(count)]
        + [spec_whole(part) for part in parts],
        [jax.ShapeDtypeStruct((tokens, cols), BF)] * (2 * count),
        tile,
        estimate(2 * count * tokens * width * cols, count * tokens * (2 * width + 4 * cols)),
        [micro_spec(m, steps, tile, cols) for m in range(count)] * 2,
        count * steps,
    )
    return outs[:count], outs[count:]


def pre_grad_rows(slots, rows, parts, slopes):
    count = len(rows)
    tokens, width = rows[0].shape
    cols, tile = slopes[0].shape[1], 512
    steps = tokens // tile

    def kernel(slots_ref, *refs):
        ins, slopes, parts = refs[:count], refs[count : 2 * count], refs[2 * count : -count - 1]
        outs, sum_ref = refs[-count - 1 : -1], refs[-1]

        @pl.when(pl.program_id(0) == 0)
        def _():
            sum_ref[...] = jnp.zeros_like(sum_ref)

        for micro in range(count):

            @pl.when(pl.program_id(0) // steps == micro)
            def _():
                act_grad = lined_dot(slots_ref, ins[micro], parts, slice(0, cols))
                grad = act_grad * slopes[micro][...].astype(F32)
                outs[micro][...] = grad.astype(BF)
                sum_ref[0:1, :] += jnp.sum(grad, axis=0, keepdims=True)

    return rows_call(
        kernel,
        slots,
        [*rows, *slopes, *parts],
        [micro_spec(m, steps, tile, width) for m in range(count)]
        + [micro_spec(m, steps, tile, cols) for m in range(count)]
        + [spec_whole(part) for part in parts],
        [jax.ShapeDtypeStruct((tokens, cols), BF)] * count + [jax.ShapeDtypeStruct((8, cols), F32)],
        tile,
        estimate(2 * count * tokens * width * cols, count * tokens * (2 * width + 4 * cols)),
        [micro_spec(m, steps, tile, cols) for m in range(count)] + [pl.BlockSpec((8, cols), lambda i, s: (0, 0))],
        count * steps,
    )


def head_grad_rows(slots, rows, parts, first):
    tokens, width = rows.shape
    cols, tile = parts[0].shape[1] - first, 1024

    def kernel(slots_ref, rows_ref, *refs):
        parts, out_ref = refs[:-1], refs[-1]
        out_ref[...] = lined_dot(slots_ref, rows_ref, parts, slice(first, first + cols)).astype(BF)

    return rows_call(
        kernel,
        slots,
        [rows, *parts],
        [spec_rows(tile, width)] + [spec_whole(part) for part in parts],
        [jax.ShapeDtypeStruct((tokens, cols), BF)],
        tile,
        estimate(2 * tokens * width * cols, tokens * (2 * width + 2 * cols)),
    )[0]


def branch_rows(slots, ones, one_parts, first, twos, two_parts, block):
    micros = len(ones)
    tokens, cols = ones[0].shape
    count, depth = len(one_parts), one_parts[0].shape[0]
    held = 2
    tile = held * block
    width, steps = count * depth, tokens // tile

    def kernel(slots_ref, *refs):
        ones, twos, out_ref = refs[:micros], refs[micros : 2 * micros], refs[-1]
        parts = refs[2 * micros : -1]
        for micro in range(micros):

            @pl.when(pl.program_id(0) // steps == micro)
            def _():
                for at in range(count):
                    where = pl.multiple_of(slots_ref[at] * depth, depth)
                    total = dot_cols(ones[micro][...], parts[at][:, first : first + cols])
                    total += dot_cols(twos[micro][...], parts[count + at][...])
                    out_ref[:, 0, :, pl.ds(where, depth)] = total.astype(BF).reshape(held, block, depth)

    return rows_call(
        kernel,
        slots,
        [*ones, *twos, *one_parts, *two_parts],
        [micro_spec(m, steps, tile, cols) for m in range(micros)]
        + [micro_spec(m, steps, tile, twos[0].shape[1]) for m in range(micros)]
        + [spec_whole(part) for part in (*one_parts, *two_parts)],
        [jax.ShapeDtypeStruct((tokens // block, micros, block, width), BF)],
        tile,
        estimate(2 * micros * tokens * width * (cols + twos[0].shape[1]), 2 * micros * tokens * (width + cols)),
        [pl.BlockSpec((held, 1, block, width), lambda i, s: (lax.rem(i, steps), i // steps, 0, 0))],
        micros * steps,
    )[0]


def normed_grad_rows(slots, one, one_parts, two, two_parts, rows, stats):
    tokens, cols = one.shape
    count, depth, tile = len(one_parts), one_parts[0].shape[0], 512
    width = count * depth

    def kernel(slots_ref, one_ref, two_ref, rows_ref, stat_ref, *refs):
        out_ref, sum_ref = refs[-2:]

        @pl.when(pl.program_id(0) == 0)
        def _():
            sum_ref[...] = jnp.zeros_like(sum_ref)

        for at in range(count):
            where = pl.multiple_of(slots_ref[at] * depth, depth)
            span = pl.ds(where, depth)
            total = dot_cols(one_ref[...], refs[at][:, :cols])
            total += dot_cols(two_ref[...], refs[count + at][...])
            out_ref[:, span] = total.astype(BF)
            scaled = (rows_ref[:, span].astype(F32) - stat_ref[:, 0:1]) * stat_ref[:, 1:2]
            sum_ref[0:1, span] += jnp.sum(total * scaled, axis=0, keepdims=True)
            sum_ref[1:2, span] += jnp.sum(total, axis=0, keepdims=True)

    return rows_call(
        kernel,
        slots,
        [one, two, rows, stats, *one_parts, *two_parts],
        [spec_rows(tile, cols), spec_rows(tile, two.shape[1]), spec_rows(tile, width), spec_rows(tile, LANES)]
        + [spec_whole(part) for part in (*one_parts, *two_parts)],
        [jax.ShapeDtypeStruct((tokens, width), BF), jax.ShapeDtypeStruct((8, width), F32)],
        tile,
        estimate(2 * tokens * width * (cols + two.shape[1]), 2 * tokens * (2 * width + cols + two.shape[1])),
        [spec_rows(tile, width), pl.BlockSpec((8, width), lambda i, s: (0, 0))],
    )


def weight_grad(groups):
    tile, chunk = 512, 512
    micro_count = len(groups[0][0])
    tokens, width = groups[0][0][0].shape
    widths = [rights[0].shape[1] for _, rights in groups]
    cols, steps = sum(widths), tokens // tile
    arrays = [array for lefts, rights in groups for array in (*lefts, *rights)]

    def kernel(*refs):
        ins, out_ref, acc_ref = refs[: len(arrays)], refs[-2], refs[-1]
        step = pl.program_id(0)

        @pl.when(step == 0)
        def _():
            acc_ref[...] = jnp.zeros_like(acc_ref)

        for micro in range(micro_count):

            @pl.when(step // steps == micro)
            def _():
                first = 0
                for at, span in enumerate(widths):
                    left = ins[2 * micro_count * at + micro]
                    right = ins[2 * micro_count * at + micro_count + micro]
                    for row in range(0, width, chunk):
                        acc_ref[row : row + chunk, first : first + span] += dot_rows(
                            left[:, row : row + chunk], right[...]
                        )
                    first += span

        @pl.when(step == micro_count * steps - 1)
        def _():
            out_ref[...] = acc_ref[...].astype(BF)

    def side(micro, span):
        return pl.BlockSpec((tile, span), lambda i: (jnp.clip(i - micro * steps, 0, steps - 1), 0))

    in_specs = []
    for span in widths:
        in_specs += [side(micro, width) for micro in range(micro_count)]
        in_specs += [side(micro, span) for micro in range(micro_count)]
    return pl.pallas_call(
        kernel,
        grid=(micro_count * steps,),
        in_specs=in_specs,
        out_specs=pl.BlockSpec((width, cols), lambda i: (0, 0)),
        out_shape=jax.ShapeDtypeStruct((width, cols), BF),
        scratch_shapes=[pltpu.VMEM((width, cols), F32)],
        compiler_params=pltpu.CompilerParams(vmem_limit_bytes=VMEM_LIMIT),
        cost_estimate=estimate(
            2 * micro_count * tokens * width * cols, 2 * micro_count * tokens * (len(groups) * width + cols)
        ),
    )(*arrays)


def shards(
    inputs,
    ln_gain,
    ln_bias,
    qkv_weight,
    qkv_bias,
    out_weight,
    out_bias,
    up_weight,
    up_bias,
    down_weight,
    down_bias,
    cotangent,
):
    micro_count, _, token_rows, model_width = inputs.shape
    fsdp_size, tp_size = lax.axis_size("fsdp"), lax.axis_size("tp")
    line = fsdp_size // 2
    fsdp_at, tp_at = lax.axis_index("fsdp"), lax.axis_index("tp")
    line_at, pair_at = fsdp_at >> 1, fsdp_at & 1
    plane_size = 2 * tp_size
    planes = [[plane * plane_size + i for i in range(plane_size)] for plane in range(line)]
    ring = [(f, ((f // 2 + 1) % line) * 2 + f % 2) for f in range(fsdp_size)]
    length = token_rows * tp_size
    head_dim = qkv_bias.shape[2] * fsdp_size
    shard_rows = model_width // fsdp_size
    line_rows = 2 * shard_rows
    attn_cols = out_weight.shape[0] // 2
    qkv_cols = 3 * attn_cols
    pairs = attn_cols // LANES
    mlp_cols = up_weight.shape[1] // 2
    both_axes = ("fsdp", "tp")

    def swap_pair(vals):
        return lax.ppermute(vals, "fsdp", [(f, f ^ 1) for f in range(fsdp_size)])

    def gather_plane(vals):
        return lax.all_gather(vals, both_axes, axis=0, tiled=True, axis_index_groups=planes)

    def scatter_plane(vals):
        return lax.psum_scatter(vals, both_axes, scatter_dimension=0, tiled=True, axis_index_groups=planes)

    def after(vals, *others):
        return lax.optimization_barrier((vals,) + others)[0]

    def doubled(cur, axis, size, at, bit):
        other = lax.ppermute(cur, axis, [(i, i ^ bit) for i in range(size)])
        upper = (at & bit) != 0
        return jnp.where(upper, jnp.concatenate([other, cur]), jnp.concatenate([cur, other]))

    small = jnp.concatenate(
        [vec.reshape(-1) for vec in (ln_gain, ln_bias, out_bias, down_bias, qkv_bias, up_bias)]
    )
    small_all = small[None]
    for bit in range(tp_size.bit_length() - 1):
        small_all = doubled(small_all, "tp", tp_size, tp_at, 1 << bit)
    small_near = small_all
    def attn_half(half):
        qkv_part = lax.dynamic_slice_in_dim(qkv_weight, half * attn_cols, attn_cols, axis=2)
        qkv_part = qkv_part.reshape(shard_rows, 3, pairs, LANES).transpose(0, 2, 1, 3)
        out_part = lax.dynamic_slice_in_dim(out_weight, half * attn_cols, attn_cols, axis=0)
        return jnp.concatenate([qkv_part.reshape(shard_rows, qkv_cols), out_part.T], axis=1)

    def up_half(half):
        return lax.dynamic_slice_in_dim(up_weight, half * mlp_cols, mlp_cols, axis=1)

    def down_half(half):
        return lax.dynamic_slice_in_dim(down_weight, half * mlp_cols, mlp_cols, axis=0).T

    def pair_join(own, other):
        return jnp.where(pair_at == 0, jnp.concatenate([own, other]), jnp.concatenate([other, own]))

    def pair_shard(half_of, *behind):
        own = half_of(pair_at)
        other = swap_pair(after(half_of(1 - pair_at), *behind))
        return pair_join(own, other)

    class Box:
        def __init__(self, val):
            self.val = val

    class Line:
        tokens = []

        def tie(self, *boxes):
            held = []
            for box in (*boxes, *self.tokens):
                if box not in held:
                    held.append(box)
            if len(held) > 1:
                for box, val in zip(held, lax.optimization_barrier(tuple(box.val for box in held))):
                    box.val = val

        def run(self, piece, *boxes):
            self.tie(*boxes)
            results = [Box(val) for val in piece(*(box.val for box in boxes))]
            self.tokens = [results[0]]
            return results

        def sync(self, box):
            self.tokens = self.tokens + [box]

    order = Line()

    class Gather:
        def __init__(self, shard):
            self.parts = [shard]

        def move(self):
            if len(self.parts) < line:
                order.tie(self.parts[-1])
                self.parts.append(Box(lax.ppermute(self.parts[-1].val, "fsdp", ring)))

        def sync(self):
            order.sync(self.parts[-1])

        def finish(self):
            while len(self.parts) < line:
                self.move()
            self.sync()

        def vals(self):
            return [part.val for part in self.parts]

    class Scatter:
        def __init__(self, part):
            self.part, self.step = part, 1
            self.moving = Box(self.own().astype(BF))

        def own(self):
            at_line = lax.rem(line_at + line - self.step, line)
            return lax.dynamic_slice_in_dim(self.part.val, at_line * line_rows, line_rows, axis=0).astype(F32)

        def move(self):
            if self.step < line:
                self.step += 1
                order.tie(self.moving)
                came = lax.ppermute(self.moving.val, "fsdp", ring).astype(F32) + self.own()
                self.moving = Box(came.astype(BF) if self.step < line else came)

        def sync(self):
            order.sync(self.moving)

        def swap(self):
            while self.step < line:
                self.move()
            order.tie(self.moving)
            total = self.moving.val
            self.keep = lax.dynamic_slice_in_dim(total, pair_at * shard_rows, shard_rows, axis=0)
            give = lax.dynamic_slice_in_dim(total, (1 - pair_at) * shard_rows, shard_rows, axis=0)
            self.got = Box(swap_pair(give.astype(BF)))

        def halves(self):
            got = self.got.val.astype(F32)
            return jnp.where(pair_at == 0, self.keep, got), jnp.where(pair_at == 0, got, self.keep)

    class SmallSum:
        def __init__(self, everywhere, over_fsdp):
            self.cur, self.rest = Box(everywhere), over_fsdp
            self.size = everywhere.shape[0]
            bits = [("tp", tp_size, bit) for bit in range(tp_size.bit_length() - 1)]
            self.steps = bits + [("fsdp", fsdp_size, bit) for bit in range(fsdp_size.bit_length() - 1)]

        def move(self):
            if self.steps:
                axis, size, bit = self.steps.pop(0)
                if axis == "fsdp" and bit == 0:
                    self.cur = Box(jnp.concatenate([self.cur.val, self.rest]))
                order.tie(self.cur)
                other = lax.ppermute(self.cur.val, axis, [(i, i ^ (1 << bit)) for i in range(size)])
                self.cur = Box(self.cur.val + other)

        def split(self):
            while self.steps:
                self.move()
            return self.cur.val[: self.size], self.cur.val[self.size :]

    resid = [inputs[m].reshape(token_rows, model_width) for m in range(micro_count)]
    cots = [cotangent[m].reshape(token_rows, model_width) for m in range(micro_count)]
    micros = range(micro_count)
    plane_rows, plane_cots = [None] * micro_count, [None] * micro_count

    def gather_behind(rows):
        sent = Box(rows)
        order.tie(sent)
        return Box(gather_plane(sent.val))

    def small_step(small_all, bit):
        if bit < fsdp_size.bit_length() - 1:
            order.tie(small_all)
            return Box(doubled(small_all.val, "fsdp", fsdp_size, fsdp_at, 1 << bit))
        return small_all

    small_all = Box(small_near)
    order.tokens = [small_all]
    plane_rows[0] = gather_behind(resid[0])
    attn_shard = Box(pair_shard(attn_half))
    order.tokens = [attn_shard]
    plane_rows[1] = gather_behind(resid[1])
    attn_ring = Gather(attn_shard)
    attn_ring.move()
    small_all = small_step(small_all, 0)
    attn_ring.sync()
    order.sync(small_all)
    bias_total = Box(sum(jnp.sum(cots[m].astype(F32), axis=0) for m in micros))
    order.sync(bias_total)
    up_send = Box(up_half(1 - pair_at))
    order.tie(up_send)
    up_shard = Box(pair_join(up_half(pair_at), swap_pair(up_send.val)))
    attn_ring.move()
    small_all = small_step(small_all, 1)
    attn_ring.sync()
    order.sync(small_all)
    order.sync(up_shard)
    plane_cots[0] = gather_behind(cots[0])
    down_send = Box(down_half(1 - pair_at))
    order.tie(down_send)
    down_shard = Box(pair_join(down_half(pair_at), swap_pair(down_send.val)))
    attn_ring.move()
    for bit in range(2, fsdp_size.bit_length() - 1):
        small_all = small_step(small_all, bit)
    attn_ring.finish()
    order.sync(small_all)
    order.tie()
    small_all = small_all.val
    vec_size = ln_gain.shape[0]
    gain_vec, shift_vec, bias_out, bias_down = (
        small_all[:, i * vec_size : (i + 1) * vec_size].reshape(-1).astype(F32) for i in range(4)
    )
    bias_both = bias_out + bias_down
    mine = lax.dynamic_slice_in_dim(
        small_all.reshape(fsdp_size, tp_size, -1), tp_at, 1, axis=1
    )[:, 0].astype(F32)
    at = 4 * vec_size
    qkv_b = mine[:, at : at + qkv_bias.size].reshape(fsdp_size, 3, 2, pairs, -1, qkv_bias.shape[2])
    qkv_b = lax.dynamic_slice_in_dim(qkv_b, pair_at, 1, axis=2)[:, :, 0]
    qkv_b = qkv_b.transpose(2, 1, 3, 0, 4).reshape(1, qkv_cols)
    at += qkv_bias.size
    up_b = mine[:, at:].reshape(fsdp_size, up_bias.shape[0], up_bias.shape[1])
    up_b = up_b.transpose(1, 0, 2).reshape(2, mlp_cols)
    up_b = lax.dynamic_slice_in_dim(up_b, pair_at, 1, axis=0)

    slots = jnp.stack([lax.rem(line_at + line - step, line) for step in range(line)]).astype(jnp.int32)
    tables = rotary_tables(length, head_dim, ROT)
    gain_row, shift_row = gain_vec[None], shift_vec[None]
    normed, qkvs, stats, rots, attns, lses, acts, slopes = ([None] * micro_count for _ in range(8))
    pre_grads, qkv_grads, qkv_sums, back, sums, attn_heads = ([None] * micro_count for _ in range(6))

    def norm_piece(m):
        normed[m], qkvs[m], stats[m] = order.run(
            lambda rows: norm_qkv(slots, rows, gain_row, shift_row, attn_ring.vals(), qkv_b), plane_rows[m]
        )

    def attend_piece(m):
        rots[m], attns[m], lses[m] = order.run(
            lambda vals: attend(vals, tables, length, head_dim), qkvs[m]
        )

    def up_piece():
        def piece(*rows):
            return [val for vals in up_act(slots, rows, up_ring.vals(), up_b) for val in vals]

        results = order.run(piece, *normed)
        acts[:], slopes[:] = results[:micro_count], results[micro_count:]

    def head_grad_piece(m):
        (attn_heads[m],) = order.run(
            lambda cot: [head_grad_rows(slots, cot, attn_ring.vals(), qkv_cols)], plane_cots[m]
        )

    def attend_back_piece(m):
        qkv_grads[m], qkv_sums[m] = order.run(
            lambda rot, grad, attn, lse: attend_back(rot, grad, attn, lse, tables, length, head_dim),
            rots[m],
            attn_heads[m],
            attns[m],
            lses[m],
        )

    def pre_grad_piece():
        def piece(*vals):
            return pre_grad_rows(slots, vals[:micro_count], down_ring.vals(), vals[micro_count:])

        *pre_grads[:], up_sums = order.run(piece, *plane_cots, *slopes)
        return up_sums

    def weight_piece(*groups):
        flat = [box for lefts, rights in groups for box in (*lefts, *rights)]

        def piece(*flat):
            count = 2 * micro_count
            return [
                weight_grad(
                    [
                        (flat[at : at + micro_count], flat[at + micro_count : at + count])
                        for at in range(0, len(flat), count)
                    ]
                )
            ]

        return Scatter(order.run(piece, *flat)[0])

    def branch_piece():
        def piece(*vals):
            rows = branch_rows(
                slots,
                vals[:micro_count],
                attn_ring.vals(),
                qkv_cols,
                vals[micro_count:],
                down_ring.vals(),
                token_rows,
            )
            return [rows.reshape(-1, model_width)]

        return order.run(piece, *attns, *acts)[0]

    def normed_grad_piece(m):
        back[m], sums[m] = order.run(
            lambda one, two, rows, stat: normed_grad_rows(
                slots, one, attn_ring.vals(), two, up_ring.vals(), rows, stat
            ),
            qkv_grads[m],
            pre_grads[m],
            plane_rows[m],
            stats[m],
        )

    def scatter_behind(box):
        order.tie(box)
        return Box(scatter_plane(box.val))

    up_ring, down_ring = Gather(up_shard), Gather(down_shard)
    order.sync(down_shard)
    up_ring.move()
    norm_piece(0)
    up_ring.sync()
    plane_cots[1] = gather_behind(cots[1])
    up_ring.move()
    attend_piece(0)
    norm_piece(1)
    up_ring.sync()
    up_ring.move()
    attend_piece(1)
    head_grad_piece(0)
    up_ring.finish()
    down_ring.move()
    up_piece()
    down_ring.sync()
    down_ring.move()
    attend_back_piece(0)
    down_ring.sync()
    down_ring.move()

    down_scatter = weight_piece((plane_cots, acts))
    down_ring.finish()
    down_scatter.move()
    branch = branch_piece()
    down_scatter.sync()
    branch_sum = scatter_behind(branch)
    down_scatter.move()
    up_sums = pre_grad_piece()
    down_scatter.sync()
    down_scatter.move()
    up_scatter = weight_piece((normed, pre_grads))
    down_scatter.sync()
    down_scatter.swap()
    up_scatter.move()
    normed_grad_piece(0)
    up_scatter.sync()
    order.sync(down_scatter.got)
    back_sums = [scatter_behind(back[0])]
    up_scatter.move()
    head_grad_piece(1)
    attend_back_piece(1)
    up_scatter.sync()
    up_scatter.move()
    attn_scatter = weight_piece((normed, qkv_grads), (plane_cots, attns))
    up_scatter.sync()
    order.sync(branch_sum)
    up_scatter.swap()
    attn_scatter.move()
    normed_grad_piece(1)
    attn_scatter.sync()
    order.sync(up_scatter.got)
    back_sums.append(scatter_behind(back[1]))

    attn_scatter.move()
    up_b_grad = up_sums.val[0]
    qkv_b_grad = sum(jnp.sum(part.val.reshape(-1, 8, qkv_cols)[:, 0], axis=0) for part in qkv_sums)
    qkv_b_grad = qkv_b_grad.reshape(pairs, 3, -1).transpose(1, 0, 2).reshape(3, attn_cols)

    def in_half(vals):
        blank = jnp.zeros_like(vals)
        return jnp.where(
            pair_at == 0, jnp.concatenate([vals, blank], axis=-1), jnp.concatenate([blank, vals], axis=-1)
        )

    gain_total, shift_total = (sum(part.val[i] for part in sums) for i in range(2))
    tail = SmallSum(
        jnp.concatenate([gain_total, shift_total, bias_total.val]),
        jnp.concatenate([in_half(up_b_grad), in_half(qkv_b_grad).reshape(-1)]),
    )
    tail.move()
    tail.move()
    attn_scatter.sync()
    attn_scatter.move()
    tail.move()
    down_w_grad = Box(jnp.concatenate([half.T for half in down_scatter.halves()], axis=0))
    up_w_grad = Box(jnp.concatenate(up_scatter.halves(), axis=1))
    order.sync(down_w_grad)
    order.sync(up_w_grad)
    attn_scatter.sync()
    attn_scatter.swap()
    tail.move()
    tail.move()
    order.sync(tail.cur)
    small_sums, bias_sums = tail.split()
    attn_grads = attn_scatter.halves()

    outputs, input_grads = [], []
    for m in micros:
        outputs.append((resid[m].astype(F32) + branch_sum.val.reshape(micro_count, token_rows, -1)[m].astype(F32) + bias_both).astype(BF))
        order.tie(back_sums[m])
        vals, cot = resid[m].astype(F32), cots[m].astype(F32)
        pull_back = jax.vjp(lambda vals: layer_norm(vals, gain_vec, shift_vec), vals)[1]
        input_grads.append((cot + pull_back(back_sums[m].val.astype(F32))[0]).astype(BF))

    small_sums = small_sums.reshape(3, fsdp_size * tp_size, vec_size)
    small_sums = lax.dynamic_slice_in_dim(small_sums, fsdp_at * tp_size + tp_at, 1, axis=1)[:, 0]
    gain_sum, shift_sum, bias_sum = small_sums[0], small_sums[1], small_sums[2]
    up_b_sum = bias_sums[: 2 * mlp_cols].reshape(up_bias.shape[0], -1)
    up_b_sum = lax.dynamic_slice_in_dim(up_b_sum, fsdp_at * up_bias.shape[1], up_bias.shape[1], axis=1)
    qkv_b_sum = bias_sums[2 * mlp_cols :].reshape(3, qkv_bias.shape[1], -1)
    qkv_b_sum = lax.dynamic_slice_in_dim(qkv_b_sum, fsdp_at * qkv_bias.shape[2], qkv_bias.shape[2], axis=2)

    def qkv_columns(vals):
        return vals[:, :qkv_cols].reshape(shard_rows, pairs, 3, LANES).transpose(0, 2, 1, 3).reshape(
            shard_rows, 3, attn_cols
        )

    qkv_w_grad = jnp.concatenate([qkv_columns(half) for half in attn_grads], axis=2)
    out_w_grad = jnp.concatenate([half[:, qkv_cols:].T for half in attn_grads], axis=0)
    return (
        jnp.stack(outputs, axis=0)[:, None],
        jnp.stack(input_grads, axis=0)[:, None],
        gain_sum,
        shift_sum,
        qkv_w_grad,
        qkv_b_sum,
        out_w_grad,
        bias_sum,
        up_w_grad.val,
        up_b_sum,
        down_w_grad.val,
        bias_sum,
    )


def solution(mesh):
    return jax.shard_map(
        shards,
        mesh=mesh,
        in_specs=(
            P(None, "fsdp", "tp", None),
            P(("fsdp", "tp")),
            P(("fsdp", "tp")),
            P("fsdp", None, "tp"),
            P(None, "tp", "fsdp"),
            P("tp", "fsdp"),
            P(("fsdp", "tp")),
            P("fsdp", "tp"),
            P("tp", "fsdp"),
            P("tp", "fsdp"),
            P(("fsdp", "tp")),
            P(None, "fsdp", "tp", None),
        ),
        out_specs=(
            P(None, "fsdp", "tp", None),
            P(None, "fsdp", "tp", None),
            P(("fsdp", "tp")),
            P(("fsdp", "tp")),
            P("fsdp", None, "tp"),
            P(None, "tp", "fsdp"),
            P("tp", "fsdp"),
            P(("fsdp", "tp")),
            P("fsdp", "tp"),
            P("tp", "fsdp"),
            P("tp", "fsdp"),
            P(("fsdp", "tp")),
        ),
        check_vma=False,
    )
```

```python
import functools
import math

import jax
import jax.numpy as jnp
from jax import lax
from jax.experimental import pallas as pl
from jax.experimental.pallas import tpu as pltpu
from jax.sharding import PartitionSpec as P

ROT = 32
LANES = 128

norm_epsilon = 1e-05
gelu_factor = 0.7978845608028654
mask_fill = -1e30
BF = jnp.bfloat16
F32 = jnp.float32
VMEM_LIMIT = 56 * 1024 * 1024


def layer_norm(resid_rows, gain_vec, shift_vec):
    row_mean = jnp.mean(resid_rows, axis=-1, keepdims=True)
    centred = resid_rows - row_mean
    row_var = jnp.mean(centred * centred, axis=-1, keepdims=True)
    return centred * lax.rsqrt(row_var + norm_epsilon) * gain_vec + shift_vec


def gelu_tanh(inner):
    return 0.5 * inner * (1.0 + jnp.tanh(gelu_factor * (inner + 0.044715 * inner * inner * inner)))


def rotary_tables(length, head_dim, rot_dim):
    half_rot = rot_dim // 2
    inv_freq = 10000.0 ** (-2.0 * jnp.arange(half_rot, dtype=F32) / rot_dim)
    angles = jnp.arange(length, dtype=F32)[:, None] * inv_freq[None, :]
    cos, sin = jnp.cos(angles), jnp.sin(angles)
    rest = jnp.ones((length, head_dim - rot_dim), F32)
    cosine = jnp.concatenate([cos, cos, rest], axis=1)
    lower = jnp.concatenate([-sin, 0.0 * sin, 0.0 * rest], axis=1)
    upper = jnp.concatenate([0.0 * sin, sin, 0.0 * rest], axis=1)
    copies = LANES // head_dim
    return tuple(jnp.tile(table, (1, copies)) for table in (cosine, lower, upper))


def turn(vals, cosine, lower, upper):
    half_rot = ROT // 2
    ahead = pltpu.roll(vals, LANES - half_rot, 1)
    behind = pltpu.roll(vals, half_rot, 1)
    return vals * cosine + ahead * lower + behind * upper


def dot_rows(left, right):
    return lax.dot_general(left, right, (((0,), (0,)), ((), ())), preferred_element_type=F32)


def dot_cols(left, right):
    return lax.dot_general(left, right, (((1,), (1,)), ((), ())), preferred_element_type=F32)


def dot_plain(left, right):
    return lax.dot_general(left, right, (((1,), (0,)), ((), ())), preferred_element_type=F32)


def head_lanes(vals, head, head_dim):
    lane_ids = lax.broadcasted_iota(jnp.int32, vals.shape, 1)
    return jnp.where(lane_ids // head_dim == head, vals, jnp.zeros_like(vals))


def seen_keys(block):
    key_ids = lax.broadcasted_iota(jnp.int32, (block, block), 0)
    return key_ids <= lax.broadcasted_iota(jnp.int32, (block, block), 1)


def attend_kernel(head_dim, block, qkv_ref, cos_ref, low_ref, up_ref, rot_ref, attn_ref, lse_ref):
    length = qkv_ref.shape[0]
    scale = 1.0 / math.sqrt(head_dim)
    tables = (cos_ref[...], low_ref[...], up_ref[...])
    rot_ref[:, :LANES] = turn(qkv_ref[:, :LANES], *tables).astype(BF) * BF(scale)
    rot_ref[:, LANES : 2 * LANES] = turn(qkv_ref[:, LANES : 2 * LANES], *tables).astype(BF)
    rot_ref[:, 2 * LANES :] = qkv_ref[:, 2 * LANES :].astype(BF)
    heads = LANES // head_dim
    seen = seen_keys(block)
    for first in range(0, length, block):
        last = first + block
        total = jnp.zeros((block, LANES), F32)
        for head in range(heads):
            query_block = head_lanes(rot_ref[first:last, :LANES], head, head_dim)
            scores = jnp.where(seen, dot_cols(rot_ref[first:last, LANES : 2 * LANES], query_block), mask_fill)
            col_max = jnp.max(scores, axis=0, keepdims=True)
            if first:
                before = dot_cols(rot_ref[:first, LANES : 2 * LANES], query_block)
                col_max = jnp.maximum(col_max, jnp.max(before, axis=0, keepdims=True))
            probs = jnp.exp(scores - col_max)
            denom = jnp.sum(probs, axis=0, keepdims=True)
            part = dot_rows(probs.astype(BF), head_lanes(rot_ref[first:last, 2 * LANES :], head, head_dim))
            if first:
                probs = jnp.exp(before - col_max)
                denom += jnp.sum(probs, axis=0, keepdims=True)
                part += dot_rows(probs.astype(BF), head_lanes(rot_ref[:first, 2 * LANES :], head, head_dim))
            total += part * jnp.broadcast_to(1.0 / denom, (LANES, block)).T
            lse_ref[0, head : head + 1, first:last] = col_max + jnp.log(denom)
        attn_ref[first:last, :] = total.astype(BF)


def attend_back_kernel(head_dim, block, rot_ref, grad_ref, attn_ref, lse_ref, cos_ref, low_ref, up_ref, out_ref, sum_ref, key_acc, value_acc):
    length = rot_ref.shape[0]
    scale = 1.0 / math.sqrt(head_dim)
    heads = LANES // head_dim
    seen = seen_keys(block)

    def back(vals, span):
        return turn(vals, cos_ref[span, :], -low_ref[span, :], -up_ref[span, :])

    query_sum = jnp.zeros((1, LANES), F32)
    key_acc[...] = jnp.zeros_like(key_acc)
    value_acc[...] = jnp.zeros_like(value_acc)
    for first in range(0, length, block):
        last = first + block
        total = jnp.zeros((block, LANES), F32)
        inner = (grad_ref[first:last, :].astype(F32) * attn_ref[first:last, :].astype(F32)).T
        for head in range(heads):
            query_block = head_lanes(rot_ref[first:last, :LANES], head, head_dim)
            grad_block = head_lanes(grad_ref[first:last, :], head, head_dim)
            lse = lse_ref[0, head : head + 1, first:last]
            inner_sum = jnp.sum(inner[head * head_dim : (head + 1) * head_dim], axis=0, keepdims=True)
            for start, stop in ((0, first), (first, last)):
                if start == stop:
                    continue
                keys = rot_ref[start:stop, LANES : 2 * LANES]
                probs = jnp.exp(dot_cols(keys, query_block) - lse)
                if start == first:
                    probs = jnp.where(seen, probs, 0.0)
                value_acc[start:stop, :] += dot_plain(probs.astype(BF), grad_block)
                prob_grad = dot_cols(rot_ref[start:stop, 2 * LANES :], grad_block)
                score_grad = (probs * (prob_grad - inner_sum)).astype(BF)
                total += dot_rows(score_grad, head_lanes(keys, head, head_dim))
                key_acc[start:stop, :] += dot_plain(score_grad, query_block)
        turned = back(total * scale, slice(first, last))
        query_sum += jnp.sum(turned, axis=0, keepdims=True)
        out_ref[first:last, :LANES] = turned.astype(BF)
    turned = back(key_acc[...], slice(0, length))
    out_ref[:, LANES : 2 * LANES] = turned.astype(BF)
    out_ref[:, 2 * LANES :] = value_acc[...].astype(BF)
    sum_ref[0:1, :LANES] = query_sum
    sum_ref[0:1, LANES : 2 * LANES] = jnp.sum(turned, axis=0, keepdims=True)
    sum_ref[0:1, 2 * LANES :] = jnp.sum(value_acc[...], axis=0, keepdims=True)


def attention_cost(seqs, pairs, length, matmuls):
    flops = seqs * pairs * matmuls * 2 * 2 * length * length * LANES
    return estimate(flops, seqs * pairs * length * LANES * 16)


def attend(qkv, tables, length, head_dim):
    tokens, width = qkv.shape
    seqs, pairs = tokens // length, width // (3 * LANES)
    heads = LANES // head_dim
    block = min(512, length)
    table_spec = pl.BlockSpec((length, LANES), lambda s, h: (0, 0))
    return pl.pallas_call(
        functools.partial(attend_kernel, head_dim, block),
        grid=(seqs, pairs),
        in_specs=[pl.BlockSpec((length, 3 * LANES), lambda s, h: (s, h))] + [table_spec] * 3,
        out_specs=[
            pl.BlockSpec((length, 3 * LANES), lambda s, h: (s, h)),
            pl.BlockSpec((length, LANES), lambda s, h: (s, h)),
            pl.BlockSpec((1, heads, length), lambda s, h: (s * pairs + h, 0, 0)),
        ],
        out_shape=[
            jax.ShapeDtypeStruct((tokens, width), BF),
            jax.ShapeDtypeStruct((tokens, pairs * LANES), BF),
            jax.ShapeDtypeStruct((seqs * pairs, heads, length), F32),
        ],
        compiler_params=pltpu.CompilerParams(vmem_limit_bytes=VMEM_LIMIT),
        cost_estimate=attention_cost(seqs, pairs, length, 3),
    )(qkv, *tables)


def attend_back(rot, attn_grad, attn, lse, tables, length, head_dim):
    tokens, width = rot.shape
    seqs, pairs = tokens // length, width // (3 * LANES)
    heads = LANES // head_dim
    block = min(512, length)
    table_spec = pl.BlockSpec((length, LANES), lambda s, h: (0, 0))
    return pl.pallas_call(
        functools.partial(attend_back_kernel, head_dim, block),
        grid=(seqs, pairs),
        in_specs=[
            pl.BlockSpec((length, 3 * LANES), lambda s, h: (s, h)),
            pl.BlockSpec((length, LANES), lambda s, h: (s, h)),
            pl.BlockSpec((length, LANES), lambda s, h: (s, h)),
            pl.BlockSpec((1, heads, length), lambda s, h: (s * pairs + h, 0, 0)),
        ]
        + [table_spec] * 3,
        out_specs=[
            pl.BlockSpec((length, 3 * LANES), lambda s, h: (s, h)),
            pl.BlockSpec((8, 3 * LANES), lambda s, h: (s, h)),
        ],
        out_shape=[jax.ShapeDtypeStruct((tokens, width), BF), jax.ShapeDtypeStruct((8 * seqs, width), F32)],
        scratch_shapes=[pltpu.VMEM((length, LANES), F32), pltpu.VMEM((length, LANES), F32)],
        compiler_params=pltpu.CompilerParams(vmem_limit_bytes=VMEM_LIMIT),
        cost_estimate=attention_cost(seqs, pairs, length, 6),
    )(rot, attn_grad, attn, lse, *tables)


def spec_rows(tile, width):
    return pl.BlockSpec((tile, width), lambda i, s: (i, 0))


def spec_whole(array):
    return pl.BlockSpec(array.shape, lambda i, s: (0,) * array.ndim)


def estimate(flops, moved):
    return pl.CostEstimate(flops=int(flops) // 64, bytes_accessed=int(moved) // 64, transcendentals=0)


def lined_dot(slots_ref, rows_ref, parts, cols):
    depth = parts[0].shape[0]
    total = None
    for at, part in enumerate(parts):
        first = pl.multiple_of(slots_ref[at] * depth, depth)
        piece = dot_plain(rows_ref[:, pl.ds(first, depth)], part[:, cols])
        total = piece if total is None else total + piece
    return total


def rows_call(kernel, slots, ins, in_specs, outs, tile, cost, out_specs=None, steps=None):
    return pl.pallas_call(
        kernel,
        grid_spec=pltpu.PrefetchScalarGridSpec(
            num_scalar_prefetch=1,
            grid=(steps or outs[0].shape[0] // tile,),
            in_specs=in_specs,
            out_specs=out_specs or [spec_rows(tile, out.shape[1]) for out in outs],
        ),
        out_shape=outs,
        compiler_params=pltpu.CompilerParams(vmem_limit_bytes=VMEM_LIMIT),
        cost_estimate=cost,
    )(slots, *ins)


def norm_qkv(slots, rows, gain, shift, parts, bias):
    tokens, width = rows.shape
    cols, tile = bias.shape[1], 256

    def kernel(slots_ref, rows_ref, gain_ref, shift_ref, bias_ref, *refs):
        parts, (normed_ref, qkv_ref, stat_ref) = refs[:-3], refs[-3:]
        vals = rows_ref[...].astype(F32)
        mean = jnp.mean(vals, axis=-1, keepdims=True)
        centred = vals - mean
        var = jnp.mean(centred * centred, axis=-1, keepdims=True)
        scale = lax.rsqrt(var + norm_epsilon)
        normed_ref[...] = (centred * scale * gain_ref[...] + shift_ref[...]).astype(BF)
        lane_ids = lax.broadcasted_iota(jnp.int32, (tile, LANES), 1)
        stat_ref[...] = jnp.where(lane_ids == 0, mean, scale)
        qkv_ref[...] = lined_dot(slots_ref, normed_ref, parts, slice(0, cols)) + bias_ref[...]

    return rows_call(
        kernel,
        slots,
        [rows, gain, shift, bias, *parts],
        [spec_rows(tile, width)] + [spec_whole(array) for array in (gain, shift, bias, *parts)],
        [
            jax.ShapeDtypeStruct((tokens, width), BF),
            jax.ShapeDtypeStruct((tokens, cols), F32),
            jax.ShapeDtypeStruct((tokens, LANES), F32),
        ],
        tile,
        estimate(2 * tokens * width * cols, tokens * (4 * width + 4 * cols)),
    )


def micro_spec(micro, steps, tile, width):
    return pl.BlockSpec((tile, width), lambda i, s: (jnp.clip(i - micro * steps, 0, steps - 1), 0))


def up_act(slots, rows, parts, bias):
    count = len(rows)
    tokens, width = rows[0].shape
    cols, tile, chunk = bias.shape[1], 512, 512
    steps = tokens // tile

    def kernel(slots_ref, bias_ref, *refs):
        ins, parts, outs = refs[:count], refs[count : -2 * count], refs[-2 * count :]
        for micro in range(count):

            @pl.when(pl.program_id(0) // steps == micro)
            def _():
                for at in range(0, cols, chunk):
                    span = slice(at, at + chunk)
                    pre = lined_dot(slots_ref, ins[micro], parts, span) + bias_ref[:, span]
                    square = pre * pre
                    tanh = jnp.tanh(gelu_factor * (pre * (1.0 + 0.044715 * square)))
                    half = 0.5 * (1.0 + tanh)
                    outs[micro][:, span] = (pre * half).astype(BF)
                    inner = gelu_factor * (1.0 + 3 * 0.044715 * square)
                    slope = half + 0.5 * pre * (1.0 - tanh * tanh) * inner
                    outs[count + micro][:, span] = slope.astype(BF)

    outs = rows_call(
        kernel,
        slots,
        [bias, *rows, *parts],
        [spec_whole(bias)]
        + [micro_spec(m, steps, tile, width) for m in range(count)]
        + [spec_whole(part) for part in parts],
        [jax.ShapeDtypeStruct((tokens, cols), BF)] * (2 * count),
        tile,
        estimate(2 * count * tokens * width * cols, count * tokens * (2 * width + 4 * cols)),
        [micro_spec(m, steps, tile, cols) for m in range(count)] * 2,
        count * steps,
    )
    return outs[:count], outs[count:]


def pre_grad_rows(slots, rows, parts, slopes):
    count = len(rows)
    tokens, width = rows[0].shape
    cols, tile = slopes[0].shape[1], 512
    steps = tokens // tile

    def kernel(slots_ref, *refs):
        ins, slopes, parts = refs[:count], refs[count : 2 * count], refs[2 * count : -count - 1]
        outs, sum_ref = refs[-count - 1 : -1], refs[-1]

        @pl.when(pl.program_id(0) == 0)
        def _():
            sum_ref[...] = jnp.zeros_like(sum_ref)

        for micro in range(count):

            @pl.when(pl.program_id(0) // steps == micro)
            def _():
                act_grad = lined_dot(slots_ref, ins[micro], parts, slice(0, cols))
                grad = act_grad * slopes[micro][...].astype(F32)
                outs[micro][...] = grad.astype(BF)
                sum_ref[0:1, :] += jnp.sum(grad, axis=0, keepdims=True)

    return rows_call(
        kernel,
        slots,
        [*rows, *slopes, *parts],
        [micro_spec(m, steps, tile, width) for m in range(count)]
        + [micro_spec(m, steps, tile, cols) for m in range(count)]
        + [spec_whole(part) for part in parts],
        [jax.ShapeDtypeStruct((tokens, cols), BF)] * count + [jax.ShapeDtypeStruct((8, cols), F32)],
        tile,
        estimate(2 * count * tokens * width * cols, count * tokens * (2 * width + 4 * cols)),
        [micro_spec(m, steps, tile, cols) for m in range(count)] + [pl.BlockSpec((8, cols), lambda i, s: (0, 0))],
        count * steps,
    )


def head_grad_rows(slots, rows, parts, first):
    tokens, width = rows.shape
    cols, tile = parts[0].shape[1] - first, 1024

    def kernel(slots_ref, rows_ref, *refs):
        parts, out_ref = refs[:-1], refs[-1]
        out_ref[...] = lined_dot(slots_ref, rows_ref, parts, slice(first, first + cols)).astype(BF)

    return rows_call(
        kernel,
        slots,
        [rows, *parts],
        [spec_rows(tile, width)] + [spec_whole(part) for part in parts],
        [jax.ShapeDtypeStruct((tokens, cols), BF)],
        tile,
        estimate(2 * tokens * width * cols, tokens * (2 * width + 2 * cols)),
    )[0]


def branch_rows(slots, ones, one_parts, first, twos, two_parts, block):
    micros = len(ones)
    tokens, cols = ones[0].shape
    count, depth = len(one_parts), one_parts[0].shape[0]
    held = 2
    tile = held * block
    width, steps = count * depth, tokens // tile

    def kernel(slots_ref, *refs):
        ones, twos, out_ref = refs[:micros], refs[micros : 2 * micros], refs[-1]
        parts = refs[2 * micros : -1]
        for micro in range(micros):

            @pl.when(pl.program_id(0) // steps == micro)
            def _():
                for at in range(count):
                    where = pl.multiple_of(slots_ref[at] * depth, depth)
                    total = dot_cols(ones[micro][...], parts[at][:, first : first + cols])
                    total += dot_cols(twos[micro][...], parts[count + at][...])
                    out_ref[:, 0, :, pl.ds(where, depth)] = total.astype(BF).reshape(held, block, depth)

    return rows_call(
        kernel,
        slots,
        [*ones, *twos, *one_parts, *two_parts],
        [micro_spec(m, steps, tile, cols) for m in range(micros)]
        + [micro_spec(m, steps, tile, twos[0].shape[1]) for m in range(micros)]
        + [spec_whole(part) for part in (*one_parts, *two_parts)],
        [jax.ShapeDtypeStruct((tokens // block, micros, block, width), BF)],
        tile,
        estimate(2 * micros * tokens * width * (cols + twos[0].shape[1]), 2 * micros * tokens * (width + cols)),
        [pl.BlockSpec((held, 1, block, width), lambda i, s: (lax.rem(i, steps), i // steps, 0, 0))],
        micros * steps,
    )[0]


def normed_grad_rows(slots, one, one_parts, two, two_parts, rows, stats, block, split):
    tokens, cols = one.shape
    count, depth = len(one_parts), one_parts[0].shape[0]
    tile = 2 * block
    width = count * depth

    def kernel(slots_ref, one_ref, two_ref, rows_ref, stat_ref, *refs):
        outs, sum_ref = refs[2 * count : -1], refs[-1]

        @pl.when(pl.program_id(0) == 0)
        def _():
            sum_ref[...] = jnp.zeros_like(sum_ref)

        for at in range(count):
            where = pl.multiple_of(slots_ref[at] * depth, depth)
            span = pl.ds(where, depth)
            total = dot_cols(one_ref[...], refs[at][:, :cols])
            total += dot_cols(two_ref[...], refs[count + at][...])
            if split:
                first = slots_ref[count] == 0
                outs[0][:, span] = jnp.where(first, total[:block], total[block:]).astype(BF)
                outs[1][:, span] = jnp.where(first, total[block:], total[:block]).astype(BF)
            else:
                outs[0][:, span] = total.astype(BF)
            scaled = (rows_ref[:, span].astype(F32) - stat_ref[:, 0:1]) * stat_ref[:, 1:2]
            sum_ref[0:1, span] += jnp.sum(total * scaled, axis=0, keepdims=True)
            sum_ref[1:2, span] += jnp.sum(total, axis=0, keepdims=True)

    pieces = 2 if split else 1
    return rows_call(
        kernel,
        slots,
        [one, two, rows, stats, *one_parts, *two_parts],
        [spec_rows(tile, cols), spec_rows(tile, two.shape[1]), spec_rows(tile, width), spec_rows(tile, LANES)]
        + [spec_whole(part) for part in (*one_parts, *two_parts)],
        [jax.ShapeDtypeStruct((tokens // pieces, width), BF)] * pieces + [jax.ShapeDtypeStruct((8, width), F32)],
        tile,
        estimate(2 * tokens * width * (cols + two.shape[1]), 2 * tokens * (2 * width + cols + two.shape[1])),
        [spec_rows(tile // pieces, width)] * pieces + [pl.BlockSpec((8, width), lambda i, s: (0, 0))],
        tokens // tile,
    )


def norm_back(rows, cots, pieces, gain, micro, earlier=None):
    micros, tokens, width = rows.shape
    tile = tokens // 2

    def kernel(rows_ref, cot_ref, gain_ref, *refs):
        vals = rows_ref[0].astype(F32)
        mean = jnp.mean(vals, axis=-1, keepdims=True)
        centred = vals - mean
        scale = lax.rsqrt(jnp.mean(centred * centred, axis=-1, keepdims=True) + norm_epsilon)
        scaled = centred * scale
        grad = refs[0][...].astype(F32)
        for ref in refs[1 : len(pieces)]:
            grad += ref[...].astype(F32)
        grad *= gain_ref[...]
        inner = jnp.mean(grad * scaled, axis=-1, keepdims=True)
        grad = (grad - jnp.mean(grad, axis=-1, keepdims=True) - scaled * inner) * scale
        refs[-1][0] = (cot_ref[0].astype(F32) + grad).astype(BF)

    at_micro = pl.BlockSpec((1, tile, width), lambda i: (micro, i, 0))
    given = [] if earlier is None else [earlier]
    return pl.pallas_call(
        kernel,
        grid=(tokens // tile,),
        in_specs=[at_micro, at_micro, pl.BlockSpec((1, width), lambda i: (0, 0))]
        + [pl.BlockSpec((tile, width), lambda i: (i, 0))] * len(pieces)
        + [pl.BlockSpec(memory_space=pl.ANY)] * len(given),
        out_specs=at_micro,
        out_shape=jax.ShapeDtypeStruct(rows.shape, BF),
        input_output_aliases={3 + len(pieces): 0} if given else {},
        compiler_params=pltpu.CompilerParams(vmem_limit_bytes=VMEM_LIMIT),
        cost_estimate=estimate(20 * tokens * width, 10 * tokens * width),
    )(rows, cots, gain, *pieces, *given)


def weight_grad(groups):
    tile, chunk = 512, 512
    micro_count = len(groups[0][0])
    tokens, width = groups[0][0][0].shape
    widths = [rights[0].shape[1] for _, rights in groups]
    cols, steps = sum(widths), tokens // tile
    arrays = [array for lefts, rights in groups for array in (*lefts, *rights)]

    def kernel(*refs):
        ins, out_ref, acc_ref = refs[: len(arrays)], refs[-2], refs[-1]
        step = pl.program_id(0)

        @pl.when(step == 0)
        def _():
            acc_ref[...] = jnp.zeros_like(acc_ref)

        for micro in range(micro_count):

            @pl.when(step // steps == micro)
            def _():
                first = 0
                for at, span in enumerate(widths):
                    left = ins[2 * micro_count * at + micro]
                    right = ins[2 * micro_count * at + micro_count + micro]
                    for row in range(0, width, chunk):
                        acc_ref[row : row + chunk, first : first + span] += dot_rows(
                            left[:, row : row + chunk], right[...]
                        )
                    first += span

        @pl.when(step == micro_count * steps - 1)
        def _():
            out_ref[...] = acc_ref[...].astype(BF)

    def side(micro, span):
        return pl.BlockSpec((tile, span), lambda i: (jnp.clip(i - micro * steps, 0, steps - 1), 0))

    in_specs = []
    for span in widths:
        in_specs += [side(micro, width) for micro in range(micro_count)]
        in_specs += [side(micro, span) for micro in range(micro_count)]
    return pl.pallas_call(
        kernel,
        grid=(micro_count * steps,),
        in_specs=in_specs,
        out_specs=pl.BlockSpec((width, cols), lambda i: (0, 0)),
        out_shape=jax.ShapeDtypeStruct((width, cols), BF),
        scratch_shapes=[pltpu.VMEM((width, cols), F32)],
        compiler_params=pltpu.CompilerParams(vmem_limit_bytes=VMEM_LIMIT),
        cost_estimate=estimate(
            2 * micro_count * tokens * width * cols, 2 * micro_count * tokens * (len(groups) * width + cols)
        ),
    )(*arrays)


def shards(
    inputs,
    ln_gain,
    ln_bias,
    qkv_weight,
    qkv_bias,
    out_weight,
    out_bias,
    up_weight,
    up_bias,
    down_weight,
    down_bias,
    cotangent,
):
    micro_count, _, token_rows, model_width = inputs.shape
    fsdp_size, tp_size = lax.axis_size("fsdp"), lax.axis_size("tp")
    line = fsdp_size // 2
    fsdp_at, tp_at = lax.axis_index("fsdp"), lax.axis_index("tp")
    line_at, pair_at = fsdp_at >> 1, fsdp_at & 1
    plane_size = 2 * tp_size
    planes = [[plane * plane_size + i for i in range(plane_size)] for plane in range(line)]
    ring = [(f, ((f // 2 + 1) % line) * 2 + f % 2) for f in range(fsdp_size)]
    length = token_rows * tp_size
    head_dim = qkv_bias.shape[2] * fsdp_size
    shard_rows = model_width // fsdp_size
    line_rows = 2 * shard_rows
    attn_cols = out_weight.shape[0] // 2
    qkv_cols = 3 * attn_cols
    pairs = attn_cols // LANES
    mlp_cols = up_weight.shape[1] // 2
    both_axes = ("fsdp", "tp")

    def swap_pair(vals):
        return lax.ppermute(vals, "fsdp", [(f, f ^ 1) for f in range(fsdp_size)])

    def gather_plane(vals):
        return lax.all_gather(vals, both_axes, axis=0, tiled=True, axis_index_groups=planes)

    def scatter_plane(vals):
        return lax.psum_scatter(vals, both_axes, scatter_dimension=0, tiled=True, axis_index_groups=planes)

    def doubled(cur, axis, size, at, bit):
        other = lax.ppermute(cur, axis, [(i, i ^ bit) for i in range(size)])
        upper = (at & bit) != 0
        return jnp.where(upper, jnp.concatenate([other, cur]), jnp.concatenate([cur, other]))

    def attn_half(half):
        qkv_part = lax.dynamic_slice_in_dim(qkv_weight, half * attn_cols, attn_cols, axis=2)
        qkv_part = qkv_part.reshape(shard_rows, 3, pairs, LANES).transpose(0, 2, 1, 3)
        out_part = lax.dynamic_slice_in_dim(out_weight, half * attn_cols, attn_cols, axis=0)
        return jnp.concatenate([qkv_part.reshape(shard_rows, qkv_cols), out_part.T], axis=1)

    def up_half(half):
        return lax.dynamic_slice_in_dim(up_weight, half * mlp_cols, mlp_cols, axis=1)

    def down_half(half):
        return lax.dynamic_slice_in_dim(down_weight, half * mlp_cols, mlp_cols, axis=0).T

    def pair_join(own, other):
        return jnp.where(pair_at == 0, jnp.concatenate([own, other]), jnp.concatenate([other, own]))

    class Box:
        def __init__(self, val):
            self.val = val

    class Line:
        tokens = []

        def tie(self, *boxes):
            held = []
            for box in (*boxes, *self.tokens):
                if box not in held:
                    held.append(box)
            if len(held) > 1:
                for box, val in zip(held, lax.optimization_barrier(tuple(box.val for box in held))):
                    box.val = val

        def run(self, piece, *boxes):
            self.tie(*boxes)
            results = [Box(val) for val in piece(*(box.val for box in boxes))]
            self.tokens = [results[0]]
            return results

        def sync(self, box):
            self.tokens = self.tokens + [box]

    order = Line()

    class Gather:
        def __init__(self, shard):
            self.parts = [shard]

        def move(self):
            if len(self.parts) < line:
                order.tie(self.parts[-1])
                self.parts.append(Box(lax.ppermute(self.parts[-1].val, "fsdp", ring)))

        def sync(self):
            order.sync(self.parts[-1])

        def finish(self):
            while len(self.parts) < line:
                self.move()
            self.sync()

        def vals(self):
            return [part.val for part in self.parts]

    class Scatter:
        def __init__(self, part):
            self.part, self.step, self.came = part, 1, None

        def total(self):
            at_line = lax.rem(line_at + line - self.step, line)
            own = lax.dynamic_slice_in_dim(self.part.val, at_line * line_rows, line_rows, axis=0)
            if self.came is None:
                return own
            order.tie(self.came)
            return self.came.val.astype(F32) + own.astype(F32)

        def move(self):
            if self.step < line:
                sent = Box(self.total().astype(BF))
                if self.came is None:
                    order.tie(sent)
                self.came = Box(lax.ppermute(sent.val, "fsdp", ring))
                self.step += 1

        def sync(self):
            order.sync(self.came)

        def swap(self):
            while self.step < line:
                self.move()
            total = self.total()
            self.keep = lax.dynamic_slice_in_dim(total, pair_at * shard_rows, shard_rows, axis=0)
            give = lax.dynamic_slice_in_dim(total, (1 - pair_at) * shard_rows, shard_rows, axis=0)
            self.got = Box(swap_pair(give.astype(BF)))

        def halves(self):
            got = self.got.val.astype(F32)
            return jnp.where(pair_at == 0, self.keep, got), jnp.where(pair_at == 0, got, self.keep)

    class SmallSum:
        def __init__(self, everywhere, over_fsdp):
            self.cur, self.rest = Box(everywhere), over_fsdp
            self.size = everywhere.shape[0]
            bits = [("tp", tp_size, bit) for bit in range(tp_size.bit_length() - 1)]
            self.steps = bits + [("fsdp", fsdp_size, bit) for bit in range(fsdp_size.bit_length() - 1)]

        def move(self):
            if self.steps:
                axis, size, bit = self.steps.pop(0)
                if axis == "fsdp" and bit == 0:
                    self.cur = Box(jnp.concatenate([self.cur.val, self.rest]))
                order.tie(self.cur)
                other = lax.ppermute(self.cur.val, axis, [(i, i ^ (1 << bit)) for i in range(size)])
                self.cur = Box(self.cur.val + other)

        def split(self):
            while self.steps:
                self.move()
            return self.cur.val[: self.size], self.cur.val[self.size :]

    resid = [inputs[m].reshape(token_rows, model_width) for m in range(micro_count)]
    cots = [cotangent[m].reshape(token_rows, model_width) for m in range(micro_count)]
    micros = range(micro_count)
    plane_rows, plane_cots = [None] * micro_count, [None] * micro_count

    small = jnp.concatenate(
        [vec.reshape(-1) for vec in (ln_gain, ln_bias, out_bias, down_bias, qkv_bias, up_bias)]
    )
    attn_send = Box(attn_half(1 - pair_at))
    small_all = Box(small[None])
    order.tokens = []
    order.tie(small_all, attn_send)
    small_all = small_all.val
    for bit in range(tp_size.bit_length() - 1):
        small_all = doubled(small_all, "tp", tp_size, tp_at, 1 << bit)
    small_near = small_all

    def gather_behind(rows):
        sent = Box(rows)
        order.tie(sent)
        return Box(gather_plane(sent.val))

    def small_step(small_all, bit):
        if bit < fsdp_size.bit_length() - 1:
            order.tie(small_all)
            return Box(doubled(small_all.val, "fsdp", fsdp_size, fsdp_at, 1 << bit))
        return small_all

    small_all = Box(small_near)
    order.tokens = [small_all]
    plane_rows[0] = gather_behind(resid[0])
    attn_shard = Box(pair_join(attn_half(pair_at), swap_pair(attn_send.val)))
    order.tokens = [attn_shard, small_all]
    attn_ring = Gather(attn_shard)
    attn_ring.move()
    plane_rows[1] = gather_behind(resid[1])
    small_all = small_step(small_all, 0)
    bias_total = Box(sum(jnp.sum(cots[m].astype(F32), axis=0) for m in micros))
    up_send = Box(up_half(1 - pair_at))
    order.tie(up_send)
    up_got = Box(swap_pair(up_send.val))
    attn_ring.sync()
    order.sync(small_all)
    attn_ring.move()
    order.sync(bias_total)
    small_all = small_step(small_all, 1)
    down_send = Box(down_half(1 - pair_at))
    order.tie(down_send, up_got)
    down_got = Box(swap_pair(down_send.val))
    up_shard = Box(pair_join(up_half(pair_at), up_got.val))
    attn_ring.sync()
    order.sync(small_all)
    attn_ring.move()
    plane_cots[0] = gather_behind(cots[0])
    for bit in range(2, fsdp_size.bit_length() - 1):
        small_all = small_step(small_all, bit)
    order.sync(up_shard)
    order.tie(down_got)
    down_shard = Box(pair_join(down_half(pair_at), down_got.val))
    attn_ring.finish()
    order.sync(small_all)
    order.tie(up_shard)
    small_all = small_all.val
    vec_size = ln_gain.shape[0]
    gain_vec, shift_vec, bias_out, bias_down = (
        small_all[:, i * vec_size : (i + 1) * vec_size].reshape(-1).astype(F32) for i in range(4)
    )
    bias_both = bias_out + bias_down
    mine = lax.dynamic_slice_in_dim(
        small_all.reshape(fsdp_size, tp_size, -1), tp_at, 1, axis=1
    )[:, 0].astype(F32)
    at = 4 * vec_size
    qkv_b = mine[:, at : at + qkv_bias.size].reshape(fsdp_size, 3, 2, pairs, -1, qkv_bias.shape[2])
    qkv_b = lax.dynamic_slice_in_dim(qkv_b, pair_at, 1, axis=2)[:, :, 0]
    qkv_b = qkv_b.transpose(2, 1, 3, 0, 4).reshape(1, qkv_cols)
    at += qkv_bias.size
    up_b = mine[:, at:].reshape(fsdp_size, up_bias.shape[0], up_bias.shape[1])
    up_b = up_b.transpose(1, 0, 2).reshape(2, mlp_cols)
    up_b = lax.dynamic_slice_in_dim(up_b, pair_at, 1, axis=0)

    slots = [lax.rem(line_at + line - step, line) for step in range(line)]
    slots = jnp.stack(slots + [tp_at & 1]).astype(jnp.int32)
    tables = rotary_tables(length, head_dim, ROT)
    gain_row, shift_row = gain_vec[None], shift_vec[None]
    normed, qkvs, stats, rots, attns, lses, acts, slopes = ([None] * micro_count for _ in range(8))
    pre_grads, qkv_grads, qkv_sums, sums, attn_heads = ([None] * micro_count for _ in range(5))

    def norm_piece(m):
        normed[m], qkvs[m], stats[m] = order.run(
            lambda rows: norm_qkv(slots, rows, gain_row, shift_row, attn_ring.vals(), qkv_b), plane_rows[m]
        )

    def attend_piece(m):
        rots[m], attns[m], lses[m] = order.run(
            lambda vals: attend(vals, tables, length, head_dim), qkvs[m]
        )

    def up_piece():
        def piece(*rows):
            return [val for vals in up_act(slots, rows, up_ring.vals(), up_b) for val in vals]

        results = order.run(piece, *normed)
        acts[:], slopes[:] = results[:micro_count], results[micro_count:]

    def head_grad_piece(m):
        (attn_heads[m],) = order.run(
            lambda cot: [head_grad_rows(slots, cot, attn_ring.vals(), qkv_cols)], plane_cots[m]
        )

    def attend_back_piece(m):
        qkv_grads[m], qkv_sums[m] = order.run(
            lambda rot, grad, attn, lse: attend_back(rot, grad, attn, lse, tables, length, head_dim),
            rots[m],
            attn_heads[m],
            attns[m],
            lses[m],
        )

    def pre_grad_piece():
        def piece(*vals):
            return pre_grad_rows(slots, vals[:micro_count], down_ring.vals(), vals[micro_count:])

        *pre_grads[:], up_sums = order.run(piece, *plane_cots, *slopes)
        return up_sums

    def weight_piece(*groups):
        flat = [box for lefts, rights in groups for box in (*lefts, *rights)]

        def piece(*flat):
            count = 2 * micro_count
            return [
                weight_grad(
                    [
                        (flat[at : at + micro_count], flat[at + micro_count : at + count])
                        for at in range(0, len(flat), count)
                    ]
                )
            ]

        return Scatter(order.run(piece, *flat)[0])

    def branch_piece():
        def piece(*vals):
            rows = branch_rows(
                slots,
                vals[:micro_count],
                attn_ring.vals(),
                qkv_cols,
                vals[micro_count:],
                down_ring.vals(),
                token_rows,
            )
            return [rows.reshape(-1, model_width)]

        return order.run(piece, *attns, *acts)[0]

    def normed_grad_piece(m, split=False):
        *back, sums[m] = order.run(
            lambda one, two, rows, stat: normed_grad_rows(
                slots, one, attn_ring.vals(), two, up_ring.vals(), rows, stat, token_rows, split
            ),
            qkv_grads[m],
            pre_grads[m],
            plane_rows[m],
            stats[m],
        )
        return back

    def scatter_behind(box):
        order.tie(box)
        return Box(scatter_plane(box.val))

    up_ring, down_ring = Gather(up_shard), Gather(down_shard)
    order.sync(down_shard)
    up_ring.move()
    norm_piece(0)
    up_ring.sync()
    plane_cots[1] = gather_behind(cots[1])
    up_ring.move()
    attend_piece(0)
    norm_piece(1)
    up_ring.sync()
    up_ring.move()
    attend_piece(1)
    head_grad_piece(0)
    up_ring.finish()
    down_ring.move()
    up_piece()
    down_ring.sync()
    down_ring.move()
    attend_back_piece(0)
    down_ring.sync()
    down_ring.move()

    down_scatter = weight_piece((plane_cots, acts))
    down_ring.finish()
    down_scatter.move()
    branch = branch_piece()
    down_scatter.sync()
    branch_sum = scatter_behind(branch)
    down_scatter.move()
    up_sums = pre_grad_piece()
    down_scatter.sync()
    down_scatter.move()
    up_scatter = weight_piece((normed, pre_grads))
    down_scatter.sync()
    down_scatter.swap()
    up_scatter.move()
    head_grad_piece(1)
    attend_back_piece(1)
    up_scatter.sync()
    order.sync(down_scatter.got)
    up_scatter.move()
    attn_scatter = weight_piece((normed, qkv_grads), (plane_cots, attns))
    up_scatter.sync()
    up_scatter.move()
    (back,) = normed_grad_piece(0)
    up_scatter.sync()
    order.sync(branch_sum)
    back_sum = scatter_behind(back)
    up_scatter.swap()
    attn_scatter.move()
    keep, give = normed_grad_piece(1, True)

    def swap_core(vals):
        return lax.ppermute(vals, "tp", [(t, t ^ 1) for t in range(tp_size)])

    def swap_y(vals):
        return lax.ppermute(vals, "tp", [(t, t ^ 2) for t in range(tp_size)])

    y_at, half = tp_at >> 1, model_width // 2
    attn_scatter.sync()
    order.sync(up_scatter.got)
    order.tie(give)
    got = Box(swap_core(give.val))
    attn_scatter.move()

    up_b_grad = up_sums.val[0]
    qkv_b_grad = sum(jnp.sum(part.val.reshape(-1, 8, qkv_cols)[:, 0], axis=0) for part in qkv_sums)
    qkv_b_grad = qkv_b_grad.reshape(pairs, 3, -1).transpose(1, 0, 2).reshape(3, attn_cols)

    def in_half(vals):
        blank = jnp.zeros_like(vals)
        return jnp.where(
            pair_at == 0, jnp.concatenate([vals, blank], axis=-1), jnp.concatenate([blank, vals], axis=-1)
        )

    gain_total, shift_total = (sum(part.val[i] for part in sums) for i in range(2))
    tail = SmallSum(
        jnp.concatenate([gain_total, shift_total, bias_total.val]),
        jnp.concatenate([in_half(up_b_grad), in_half(qkv_b_grad).reshape(-1)]),
    )
    order.tie(got)
    blocks = Box((got.val.astype(F32) + keep.val.astype(F32)).astype(BF).reshape(4, token_rows, model_width))
    order.sync(blocks)

    def block(pair, y):
        return lax.dynamic_index_in_dim(blocks.val, pair * 2 + y, 0, keepdims=False)

    far = block(1 - pair_at, 1 - y_at)
    from_pair, from_y = Box(swap_pair(far[:, :half])), Box(swap_y(far[:, half:]))
    tail.move()
    tail.move()
    order.tie(from_pair, from_y)
    for_y, for_pair = block(pair_at, 1 - y_at), block(1 - pair_at, y_at)
    for_y = jnp.concatenate(
        [(for_y[:, :half].astype(F32) + from_pair.val.astype(F32)).astype(BF), for_y[:, half:]], axis=1
    )
    for_pair = jnp.concatenate(
        [for_pair[:, :half], (for_pair[:, half:].astype(F32) + from_y.val.astype(F32)).astype(BF)], axis=1
    )
    from_pair, from_y = Box(swap_pair(for_pair)), Box(swap_y(for_y))
    attn_scatter.sync()
    attn_scatter.move()
    tail.move()
    down_w_grad = Box(jnp.concatenate([part.T for part in down_scatter.halves()], axis=0))
    up_w_grad = Box(jnp.concatenate(up_scatter.halves(), axis=1))
    order.sync(down_w_grad)
    order.sync(up_w_grad)
    attn_scatter.sync()
    attn_scatter.swap()
    tail.move()
    tail.move()
    order.sync(tail.cur)
    order.tie(from_pair, from_y)
    gained = norm_back(
        inputs[:, 0], cotangent[:, 0], [block(pair_at, y_at), from_pair.val, from_y.val], gain_row, 1,
        norm_back(inputs[:, 0], cotangent[:, 0], [back_sum.val], gain_row, 0),
    )
    small_sums, bias_sums = tail.split()
    attn_grads = attn_scatter.halves()
    branch_sum = branch_sum.val.reshape(micro_count, token_rows, model_width)
    output = (inputs[:, 0].astype(F32) + branch_sum.astype(F32) + bias_both).astype(BF)

    small_sums = small_sums.reshape(3, fsdp_size * tp_size, vec_size)
    small_sums = lax.dynamic_slice_in_dim(small_sums, fsdp_at * tp_size + tp_at, 1, axis=1)[:, 0]
    gain_sum, shift_sum, bias_sum = small_sums[0], small_sums[1], small_sums[2]
    up_b_sum = bias_sums[: 2 * mlp_cols].reshape(up_bias.shape[0], -1)
    up_b_sum = lax.dynamic_slice_in_dim(up_b_sum, fsdp_at * up_bias.shape[1], up_bias.shape[1], axis=1)
    qkv_b_sum = bias_sums[2 * mlp_cols :].reshape(3, qkv_bias.shape[1], -1)
    qkv_b_sum = lax.dynamic_slice_in_dim(qkv_b_sum, fsdp_at * qkv_bias.shape[2], qkv_bias.shape[2], axis=2)

    def qkv_columns(vals):
        return vals[:, :qkv_cols].reshape(shard_rows, pairs, 3, LANES).transpose(0, 2, 1, 3).reshape(
            shard_rows, 3, attn_cols
        )

    qkv_w_grad = jnp.concatenate([qkv_columns(half) for half in attn_grads], axis=2)
    out_w_grad = jnp.concatenate([half[:, qkv_cols:].T for half in attn_grads], axis=0)
    return (
        output[:, None],
        gained[:, None],
        gain_sum,
        shift_sum,
        qkv_w_grad,
        qkv_b_sum,
        out_w_grad,
        bias_sum,
        up_w_grad.val,
        up_b_sum,
        down_w_grad.val,
        bias_sum,
    )


def solution(mesh):
    return jax.shard_map(
        shards,
        mesh=mesh,
        in_specs=(
            P(None, "fsdp", "tp", None),
            P(("fsdp", "tp")),
            P(("fsdp", "tp")),
            P("fsdp", None, "tp"),
            P(None, "tp", "fsdp"),
            P("tp", "fsdp"),
            P(("fsdp", "tp")),
            P("fsdp", "tp"),
            P("tp", "fsdp"),
            P("tp", "fsdp"),
            P(("fsdp", "tp")),
            P(None, "fsdp", "tp", None),
        ),
        out_specs=(
            P(None, "fsdp", "tp", None),
            P(None, "fsdp", "tp", None),
            P(("fsdp", "tp")),
            P(("fsdp", "tp")),
            P("fsdp", None, "tp"),
            P(None, "tp", "fsdp"),
            P("tp", "fsdp"),
            P(("fsdp", "tp")),
            P("fsdp", "tp"),
            P("tp", "fsdp"),
            P("tp", "fsdp"),
            P(("fsdp", "tp")),
        ),
        check_vma=False,
    )
```

```python
import functools
import math

import jax
import jax.numpy as jnp
from jax import lax
from jax.experimental import pallas as pl
from jax.experimental.pallas import tpu as pltpu
from jax.sharding import PartitionSpec as P

ROT = 32
LANES = 128

norm_epsilon = 1e-05
gelu_factor = 0.7978845608028654
mask_fill = -1e30
BF = jnp.bfloat16
F32 = jnp.float32
VMEM_LIMIT = 56 * 1024 * 1024


def rotary_tables(length, head_dim, rot_dim):
    half_rot = rot_dim // 2
    inv_freq = 10000.0 ** (-2.0 * jnp.arange(half_rot, dtype=F32) / rot_dim)
    angles = jnp.arange(length, dtype=F32)[:, None] * inv_freq[None, :]
    cos, sin = jnp.cos(angles), jnp.sin(angles)
    rest = jnp.ones((length, head_dim - rot_dim), F32)
    cosine = jnp.concatenate([cos, cos, rest], axis=1)
    lower = jnp.concatenate([-sin, 0.0 * sin, 0.0 * rest], axis=1)
    upper = jnp.concatenate([0.0 * sin, sin, 0.0 * rest], axis=1)
    copies = LANES // head_dim
    return tuple(jnp.tile(table, (1, copies)) for table in (cosine, lower, upper))


def turn(vals, cosine, lower, upper):
    half_rot = ROT // 2
    ahead = pltpu.roll(vals, LANES - half_rot, 1)
    behind = pltpu.roll(vals, half_rot, 1)
    return vals * cosine + ahead * lower + behind * upper


def dot_rows(left, right):
    return lax.dot_general(left, right, (((0,), (0,)), ((), ())), preferred_element_type=F32)


def dot_cols(left, right):
    return lax.dot_general(left, right, (((1,), (1,)), ((), ())), preferred_element_type=F32)


def dot_plain(left, right):
    return lax.dot_general(left, right, (((1,), (0,)), ((), ())), preferred_element_type=F32)


def head_lanes(vals, head, head_dim):
    lane_ids = lax.broadcasted_iota(jnp.int32, vals.shape, 1)
    return jnp.where(lane_ids // head_dim == head, vals, jnp.zeros_like(vals))


def seen_keys(block):
    key_ids = lax.broadcasted_iota(jnp.int32, (block, block), 0)
    return key_ids <= lax.broadcasted_iota(jnp.int32, (block, block), 1)


def attend_kernel(head_dim, block, qkv_ref, cos_ref, low_ref, up_ref, rot_ref, attn_ref, lse_ref):
    length = qkv_ref.shape[0]
    scale = 1.0 / math.sqrt(head_dim)
    tables = (cos_ref[...], low_ref[...], up_ref[...])
    rot_ref[:, :LANES] = turn(qkv_ref[:, :LANES], *tables).astype(BF) * BF(scale)
    rot_ref[:, LANES : 2 * LANES] = turn(qkv_ref[:, LANES : 2 * LANES], *tables).astype(BF)
    rot_ref[:, 2 * LANES :] = qkv_ref[:, 2 * LANES :].astype(BF)
    heads = LANES // head_dim
    seen = seen_keys(block)
    for first in range(0, length, block):
        last = first + block
        total = jnp.zeros((block, LANES), F32)
        for head in range(heads):
            query_block = head_lanes(rot_ref[first:last, :LANES], head, head_dim)
            scores = jnp.where(seen, dot_cols(rot_ref[first:last, LANES : 2 * LANES], query_block), mask_fill)
            col_max = jnp.max(scores, axis=0, keepdims=True)
            if first:
                before = dot_cols(rot_ref[:first, LANES : 2 * LANES], query_block)
                col_max = jnp.maximum(col_max, jnp.max(before, axis=0, keepdims=True))
            probs = jnp.exp(scores - col_max)
            denom = jnp.sum(probs, axis=0, keepdims=True)
            part = dot_rows(probs.astype(BF), head_lanes(rot_ref[first:last, 2 * LANES :], head, head_dim))
            if first:
                probs = jnp.exp(before - col_max)
                denom += jnp.sum(probs, axis=0, keepdims=True)
                part += dot_rows(probs.astype(BF), head_lanes(rot_ref[:first, 2 * LANES :], head, head_dim))
            total += part * jnp.broadcast_to(1.0 / denom, (LANES, block)).T
            lse_ref[0, head : head + 1, first:last] = col_max + jnp.log(denom)
        attn_ref[first:last, :] = total.astype(BF)


def attend_back_kernel(head_dim, block, rot_ref, grad_ref, attn_ref, lse_ref, cos_ref, low_ref, up_ref, out_ref, sum_ref, key_acc, value_acc):
    length = rot_ref.shape[0]
    scale = 1.0 / math.sqrt(head_dim)
    heads = LANES // head_dim
    seen = seen_keys(block)

    def back(vals, span):
        return turn(vals, cos_ref[span, :], -low_ref[span, :], -up_ref[span, :])

    query_sum = jnp.zeros((1, LANES), F32)
    key_acc[...] = jnp.zeros_like(key_acc)
    value_acc[...] = jnp.zeros_like(value_acc)
    for first in range(0, length, block):
        last = first + block
        total = jnp.zeros((block, LANES), F32)
        inner = (grad_ref[first:last, :].astype(F32) * attn_ref[first:last, :].astype(F32)).T
        for head in range(heads):
            query_block = head_lanes(rot_ref[first:last, :LANES], head, head_dim)
            grad_block = head_lanes(grad_ref[first:last, :], head, head_dim)
            lse = lse_ref[0, head : head + 1, first:last]
            inner_sum = jnp.sum(inner[head * head_dim : (head + 1) * head_dim], axis=0, keepdims=True)
            for start, stop in ((0, first), (first, last)):
                if start == stop:
                    continue
                keys = rot_ref[start:stop, LANES : 2 * LANES]
                probs = jnp.exp(dot_cols(keys, query_block) - lse)
                if start == first:
                    probs = jnp.where(seen, probs, 0.0)
                value_acc[start:stop, :] += dot_plain(probs.astype(BF), grad_block)
                prob_grad = dot_cols(rot_ref[start:stop, 2 * LANES :], grad_block)
                score_grad = (probs * (prob_grad - inner_sum)).astype(BF)
                total += dot_rows(score_grad, head_lanes(keys, head, head_dim))
                key_acc[start:stop, :] += dot_plain(score_grad, query_block)
        turned = back(total * scale, slice(first, last))
        query_sum += jnp.sum(turned, axis=0, keepdims=True)
        out_ref[first:last, :LANES] = turned.astype(BF)
    turned = back(key_acc[...], slice(0, length))
    out_ref[:, LANES : 2 * LANES] = turned.astype(BF)
    out_ref[:, 2 * LANES :] = value_acc[...].astype(BF)
    sum_ref[0:1, :LANES] = query_sum
    sum_ref[0:1, LANES : 2 * LANES] = jnp.sum(turned, axis=0, keepdims=True)
    sum_ref[0:1, 2 * LANES :] = jnp.sum(value_acc[...], axis=0, keepdims=True)


def attention_cost(seqs, pairs, length, matmuls):
    flops = seqs * pairs * matmuls * 2 * 2 * length * length * LANES
    return estimate(flops, seqs * pairs * length * LANES * 16)


def attend(qkv, tables, length, head_dim):
    tokens, width = qkv.shape
    seqs, pairs = tokens // length, width // (3 * LANES)
    heads = LANES // head_dim
    block = min(512, length)
    table_spec = pl.BlockSpec((length, LANES), lambda s, h: (0, 0))
    return pl.pallas_call(
        functools.partial(attend_kernel, head_dim, block),
        grid=(seqs, pairs),
        in_specs=[pl.BlockSpec((length, 3 * LANES), lambda s, h: (s, h))] + [table_spec] * 3,
        out_specs=[
            pl.BlockSpec((length, 3 * LANES), lambda s, h: (s, h)),
            pl.BlockSpec((length, LANES), lambda s, h: (s, h)),
            pl.BlockSpec((1, heads, length), lambda s, h: (s * pairs + h, 0, 0)),
        ],
        out_shape=[
            jax.ShapeDtypeStruct((tokens, width), BF),
            jax.ShapeDtypeStruct((tokens, pairs * LANES), BF),
            jax.ShapeDtypeStruct((seqs * pairs, heads, length), F32),
        ],
        compiler_params=pltpu.CompilerParams(vmem_limit_bytes=VMEM_LIMIT),
        cost_estimate=attention_cost(seqs, pairs, length, 3),
    )(qkv, *tables)


def attend_back(rot, attn_grad, attn, lse, tables, length, head_dim):
    tokens, width = rot.shape
    seqs, pairs = tokens // length, width // (3 * LANES)
    heads = LANES // head_dim
    block = min(512, length)
    table_spec = pl.BlockSpec((length, LANES), lambda s, h: (0, 0))
    return pl.pallas_call(
        functools.partial(attend_back_kernel, head_dim, block),
        grid=(seqs, pairs),
        in_specs=[
            pl.BlockSpec((length, 3 * LANES), lambda s, h: (s, h)),
            pl.BlockSpec((length, LANES), lambda s, h: (s, h)),
            pl.BlockSpec((length, LANES), lambda s, h: (s, h)),
            pl.BlockSpec((1, heads, length), lambda s, h: (s * pairs + h, 0, 0)),
        ]
        + [table_spec] * 3,
        out_specs=[
            pl.BlockSpec((length, 3 * LANES), lambda s, h: (s, h)),
            pl.BlockSpec((8, 3 * LANES), lambda s, h: (s, h)),
        ],
        out_shape=[jax.ShapeDtypeStruct((tokens, width), BF), jax.ShapeDtypeStruct((8 * seqs, width), F32)],
        scratch_shapes=[pltpu.VMEM((length, LANES), F32), pltpu.VMEM((length, LANES), F32)],
        compiler_params=pltpu.CompilerParams(vmem_limit_bytes=VMEM_LIMIT),
        cost_estimate=attention_cost(seqs, pairs, length, 6),
    )(rot, attn_grad, attn, lse, *tables)


def spec_rows(tile, width):
    return pl.BlockSpec((tile, width), lambda i, s: (i, 0))


def spec_whole(array):
    return pl.BlockSpec(array.shape, lambda i, s: (0,) * array.ndim)


def estimate(flops, moved):
    return pl.CostEstimate(flops=int(flops) // 64, bytes_accessed=int(moved) // 64, transcendentals=0)


def lined_dot(slots_ref, rows_ref, parts, cols):
    depth = parts[0].shape[0]
    total = None
    for at, part in enumerate(parts):
        first = pl.multiple_of(slots_ref[at] * depth, depth)
        piece = dot_plain(rows_ref[:, pl.ds(first, depth)], part[:, cols])
        total = piece if total is None else total + piece
    return total


def rows_call(kernel, slots, ins, in_specs, outs, tile, cost, out_specs=None, steps=None):
    return pl.pallas_call(
        kernel,
        grid_spec=pltpu.PrefetchScalarGridSpec(
            num_scalar_prefetch=1,
            grid=(steps or outs[0].shape[0] // tile,),
            in_specs=in_specs,
            out_specs=out_specs or [spec_rows(tile, out.shape[1]) for out in outs],
        ),
        out_shape=outs,
        compiler_params=pltpu.CompilerParams(vmem_limit_bytes=VMEM_LIMIT),
        cost_estimate=cost,
    )(slots, *ins)


def normalise(rows):
    micros, tokens, width = rows.shape

    def kernel(rows_ref, out_ref):
        vals = rows_ref[0].astype(F32)
        mean = jnp.mean(vals, axis=-1, keepdims=True)
        centred = vals - mean
        var = jnp.mean(centred * centred, axis=-1, keepdims=True)
        out_ref[...] = (centred * lax.rsqrt(var + norm_epsilon)).astype(BF)

    def one(micro):
        return pl.pallas_call(
            kernel,
            grid=(2,),
            in_specs=[pl.BlockSpec((1, tokens // 2, width), lambda i: (micro, i, 0))],
            out_specs=pl.BlockSpec((tokens // 2, width), lambda i: (i, 0)),
            out_shape=jax.ShapeDtypeStruct((tokens, width), BF),
            compiler_params=pltpu.CompilerParams(vmem_limit_bytes=VMEM_LIMIT),
            cost_estimate=estimate(10 * tokens * width, 4 * tokens * width),
        )(rows)

    return [one(micro) for micro in range(micros)]


def norm_qkv(slots, rows, gain, shift, parts, bias):
    tokens, width = rows.shape
    cols, tile = bias.shape[1], 512

    def kernel(slots_ref, rows_ref, gain_ref, shift_ref, bias_ref, *refs):
        parts, (normed_ref, qkv_ref) = refs[:-2], refs[-2:]
        normed_ref[...] = (rows_ref[...].astype(F32) * gain_ref[...] + shift_ref[...]).astype(BF)
        qkv_ref[...] = lined_dot(slots_ref, normed_ref, parts, slice(0, cols)) + bias_ref[...]

    return rows_call(
        kernel,
        slots,
        [rows, gain, shift, bias, *parts],
        [spec_rows(tile, width)] + [spec_whole(array) for array in (gain, shift, bias, *parts)],
        [jax.ShapeDtypeStruct((tokens, width), BF), jax.ShapeDtypeStruct((tokens, cols), F32)],
        tile,
        estimate(2 * tokens * width * cols, tokens * (4 * width + 4 * cols)),
    )


def micro_spec(micro, steps, tile, width):
    return pl.BlockSpec((tile, width), lambda i, s: (jnp.clip(i - micro * steps, 0, steps - 1), 0))


def up_act(slots, rows, parts, bias):
    count = len(rows)
    tokens, width = rows[0].shape
    cols, tile, chunk = bias.shape[1], 512, 512
    steps = tokens // tile

    def kernel(slots_ref, bias_ref, *refs):
        ins, parts, outs = refs[:count], refs[count : -2 * count], refs[-2 * count :]
        for micro in range(count):

            @pl.when(pl.program_id(0) // steps == micro)
            def _():
                for at in range(0, cols, chunk):
                    span = slice(at, at + chunk)
                    pre = lined_dot(slots_ref, ins[micro], parts, span) + bias_ref[:, span]
                    square = pre * pre
                    tanh = jnp.tanh(pre * (gelu_factor + (gelu_factor * 0.044715) * square))
                    half = 0.5 + 0.5 * tanh
                    act = pre * half
                    outs[micro][:, span] = act.astype(BF)
                    inner = 2 * gelu_factor + (6 * 0.044715 * gelu_factor) * square
                    outs[count + micro][:, span] = (half + (act - act * half) * inner).astype(BF)

    outs = rows_call(
        kernel,
        slots,
        [bias, *rows, *parts],
        [spec_whole(bias)]
        + [micro_spec(m, steps, tile, width) for m in range(count)]
        + [spec_whole(part) for part in parts],
        [jax.ShapeDtypeStruct((tokens, cols), BF)] * (2 * count),
        tile,
        estimate(2 * count * tokens * width * cols, count * tokens * (2 * width + 4 * cols)),
        [micro_spec(m, steps, tile, cols) for m in range(count)] * 2,
        count * steps,
    )
    return outs[:count], outs[count:]


def pre_grad_rows(slots, rows, parts, slopes):
    count = len(rows)
    tokens, width = rows[0].shape
    cols, tile = slopes[0].shape[1], 512
    steps = tokens // tile

    def kernel(slots_ref, *refs):
        ins, slopes, parts = refs[:count], refs[count : 2 * count], refs[2 * count : -count - 1]
        outs, sum_ref = refs[-count - 1 : -1], refs[-1]

        @pl.when(pl.program_id(0) == 0)
        def _():
            sum_ref[...] = jnp.zeros_like(sum_ref)

        for micro in range(count):

            @pl.when(pl.program_id(0) // steps == micro)
            def _():
                act_grad = lined_dot(slots_ref, ins[micro], parts, slice(0, cols))
                grad = act_grad * slopes[micro][...].astype(F32)
                outs[micro][...] = grad.astype(BF)
                sum_ref[0:1, :] += jnp.sum(grad, axis=0, keepdims=True)

    return rows_call(
        kernel,
        slots,
        [*rows, *slopes, *parts],
        [micro_spec(m, steps, tile, width) for m in range(count)]
        + [micro_spec(m, steps, tile, cols) for m in range(count)]
        + [spec_whole(part) for part in parts],
        [jax.ShapeDtypeStruct((tokens, cols), BF)] * count + [jax.ShapeDtypeStruct((8, cols), F32)],
        tile,
        estimate(2 * count * tokens * width * cols, count * tokens * (2 * width + 4 * cols)),
        [micro_spec(m, steps, tile, cols) for m in range(count)] + [pl.BlockSpec((8, cols), lambda i, s: (0, 0))],
        count * steps,
    )


def head_grad_rows(slots, rows, parts, first):
    tokens, width = rows.shape
    cols, tile = parts[0].shape[1] - first, 1024

    def kernel(slots_ref, rows_ref, *refs):
        parts, out_ref = refs[:-1], refs[-1]
        out_ref[...] = lined_dot(slots_ref, rows_ref, parts, slice(first, first + cols)).astype(BF)

    return rows_call(
        kernel,
        slots,
        [rows, *parts],
        [spec_rows(tile, width)] + [spec_whole(part) for part in parts],
        [jax.ShapeDtypeStruct((tokens, cols), BF)],
        tile,
        estimate(2 * tokens * width * cols, tokens * (2 * width + 2 * cols)),
    )[0]


def branch_rows(slots, ones, one_parts, first, twos, two_parts, block):
    micros = len(ones)
    tokens, cols = ones[0].shape
    count, depth = len(one_parts), one_parts[0].shape[0]
    held = 2
    tile = held * block
    width, steps = count * depth, tokens // tile

    def kernel(slots_ref, *refs):
        ones, twos, out_ref = refs[:micros], refs[micros : 2 * micros], refs[-1]
        parts = refs[2 * micros : -1]
        for micro in range(micros):

            @pl.when(pl.program_id(0) // steps == micro)
            def _():
                for at in range(count):
                    where = pl.multiple_of(slots_ref[at] * depth, depth)
                    total = dot_cols(ones[micro][...], parts[at][:, first : first + cols])
                    total += dot_cols(twos[micro][...], parts[count + at][...])
                    out_ref[:, 0, :, pl.ds(where, depth)] = total.astype(BF).reshape(held, block, depth)

    return rows_call(
        kernel,
        slots,
        [*ones, *twos, *one_parts, *two_parts],
        [micro_spec(m, steps, tile, cols) for m in range(micros)]
        + [micro_spec(m, steps, tile, twos[0].shape[1]) for m in range(micros)]
        + [spec_whole(part) for part in (*one_parts, *two_parts)],
        [jax.ShapeDtypeStruct((tokens // block, micros, block, width), BF)],
        tile,
        estimate(2 * micros * tokens * width * (cols + twos[0].shape[1]), 2 * micros * tokens * (width + cols)),
        [pl.BlockSpec((held, 1, block, width), lambda i, s: (lax.rem(i, steps), i // steps, 0, 0))],
        micros * steps,
    )[0]


def normed_grad_rows(slots, one, one_parts, two, two_parts, rows, block, split):
    tokens, cols = one.shape
    count, depth = len(one_parts), one_parts[0].shape[0]
    tile = 2 * block
    width = count * depth

    def kernel(slots_ref, one_ref, two_ref, rows_ref, *refs):
        outs, sum_ref = refs[2 * count : -1], refs[-1]

        @pl.when(pl.program_id(0) == 0)
        def _():
            sum_ref[...] = jnp.zeros_like(sum_ref)

        for at in range(count):
            where = pl.multiple_of(slots_ref[at] * depth, depth)
            span = pl.ds(where, depth)
            total = dot_cols(one_ref[...], refs[at][:, :cols])
            total += dot_cols(two_ref[...], refs[count + at][...])
            if split:
                first = slots_ref[count] == 0
                outs[0][:, span] = jnp.where(first, total[:block], total[block:]).astype(BF)
                outs[1][:, span] = jnp.where(first, total[block:], total[:block]).astype(BF)
            else:
                outs[0][:, span] = total.astype(BF)
            sum_ref[0:1, span] += jnp.sum(total * rows_ref[:, span].astype(F32), axis=0, keepdims=True)
            sum_ref[1:2, span] += jnp.sum(total, axis=0, keepdims=True)

    pieces = 2 if split else 1
    return rows_call(
        kernel,
        slots,
        [one, two, rows, *one_parts, *two_parts],
        [spec_rows(tile, cols), spec_rows(tile, two.shape[1]), spec_rows(tile, width)]
        + [spec_whole(part) for part in (*one_parts, *two_parts)],
        [jax.ShapeDtypeStruct((tokens // pieces, width), BF)] * pieces + [jax.ShapeDtypeStruct((8, width), F32)],
        tile,
        estimate(2 * tokens * width * (cols + two.shape[1]), 2 * tokens * (2 * width + cols + two.shape[1])),
        [spec_rows(tile // pieces, width)] * pieces + [pl.BlockSpec((8, width), lambda i, s: (0, 0))],
        tokens // tile,
    )


def norm_back(rows, cots, pieces, gain, micro, earlier=None):
    micros, tokens, width = rows.shape
    tile = tokens // 4

    def kernel(rows_ref, cot_ref, gain_ref, *refs):
        vals = rows_ref[0].astype(F32)
        mean = jnp.mean(vals, axis=-1, keepdims=True)
        centred = vals - mean
        scale = lax.rsqrt(jnp.mean(centred * centred, axis=-1, keepdims=True) + norm_epsilon)
        scaled = centred * scale
        grad = refs[0][...].astype(F32)
        for ref in refs[1 : len(pieces)]:
            grad += ref[...].astype(F32)
        grad *= gain_ref[...]
        inner = jnp.mean(grad * scaled, axis=-1, keepdims=True)
        grad = (grad - jnp.mean(grad, axis=-1, keepdims=True) - scaled * inner) * scale
        refs[-1][0] = (cot_ref[0].astype(F32) + grad).astype(BF)

    at_micro = pl.BlockSpec((1, tile, width), lambda i: (micro, i, 0))
    given = [] if earlier is None else [earlier]
    return pl.pallas_call(
        kernel,
        grid=(tokens // tile,),
        in_specs=[at_micro, at_micro, pl.BlockSpec((1, width), lambda i: (0, 0))]
        + [pl.BlockSpec((tile, width), lambda i: (i, 0))] * len(pieces)
        + [pl.BlockSpec(memory_space=pl.ANY)] * len(given),
        out_specs=at_micro,
        out_shape=jax.ShapeDtypeStruct(rows.shape, BF),
        input_output_aliases={3 + len(pieces): 0} if given else {},
        compiler_params=pltpu.CompilerParams(vmem_limit_bytes=VMEM_LIMIT),
        cost_estimate=estimate(20 * tokens * width, 10 * tokens * width),
    )(rows, cots, gain, *pieces, *given)


def weight_grad(lefts, rights):
    tile, chunk = 512, 512
    micro_count = len(lefts)
    tokens, width = lefts[0].shape
    widths = [right[0].shape[1] for right in rights]
    cols, steps = sum(widths), tokens // tile

    def kernel(*refs):
        out_ref, acc_ref = refs[-2:]
        step = pl.program_id(0)

        @pl.when(step == 0)
        def _():
            acc_ref[...] = jnp.zeros_like(acc_ref)

        for micro in range(micro_count):

            @pl.when(step // steps == micro)
            def _():
                first = 0
                for at, span in enumerate(widths):
                    right = refs[(1 + at) * micro_count + micro]
                    for row in range(0, width, chunk):
                        acc_ref[row : row + chunk, first : first + span] += dot_rows(
                            refs[micro][:, row : row + chunk], right[...]
                        )
                    first += span

        @pl.when(step == micro_count * steps - 1)
        def _():
            out_ref[...] = acc_ref[...].astype(BF)

    def side(micro, span):
        return pl.BlockSpec((tile, span), lambda i: (jnp.clip(i - micro * steps, 0, steps - 1), 0))

    return pl.pallas_call(
        kernel,
        grid=(micro_count * steps,),
        in_specs=[side(micro, span) for span in (width, *widths) for micro in range(micro_count)],
        out_specs=pl.BlockSpec((width, cols), lambda i: (0, 0)),
        out_shape=jax.ShapeDtypeStruct((width, cols), BF),
        scratch_shapes=[pltpu.VMEM((width, cols), F32)],
        compiler_params=pltpu.CompilerParams(vmem_limit_bytes=VMEM_LIMIT),
        cost_estimate=estimate(
            2 * micro_count * tokens * width * cols, 2 * micro_count * tokens * (width + cols)
        ),
    )(*lefts, *(array for right in rights for array in right))


def shards(
    inputs,
    ln_gain,
    ln_bias,
    qkv_weight,
    qkv_bias,
    out_weight,
    out_bias,
    up_weight,
    up_bias,
    down_weight,
    down_bias,
    cotangent,
):
    micro_count, _, token_rows, model_width = inputs.shape
    fsdp_size, tp_size = lax.axis_size("fsdp"), lax.axis_size("tp")
    line = fsdp_size // 2
    fsdp_at, tp_at = lax.axis_index("fsdp"), lax.axis_index("tp")
    line_at, pair_at = fsdp_at >> 1, fsdp_at & 1
    plane_size = 2 * tp_size
    planes = [[plane * plane_size + i for i in range(plane_size)] for plane in range(line)]
    ring = [(f, ((f // 2 + 1) % line) * 2 + f % 2) for f in range(fsdp_size)]
    length = token_rows * tp_size
    head_dim = qkv_bias.shape[2] * fsdp_size
    shard_rows = model_width // fsdp_size
    line_rows = 2 * shard_rows
    attn_cols = out_weight.shape[0] // 2
    qkv_cols = 3 * attn_cols
    pairs = attn_cols // LANES
    mlp_cols = up_weight.shape[1] // 2
    both_axes = ("fsdp", "tp")

    def swap_pair(vals):
        return lax.ppermute(vals, "fsdp", [(f, f ^ 1) for f in range(fsdp_size)])

    def gather_plane(vals):
        return lax.all_gather(vals, both_axes, axis=0, tiled=True, axis_index_groups=planes)

    def scatter_plane(vals):
        return lax.psum_scatter(vals, both_axes, scatter_dimension=0, tiled=True, axis_index_groups=planes)

    def doubled(cur, axis, size, at, bit):
        other = lax.ppermute(cur, axis, [(i, i ^ bit) for i in range(size)])
        upper = (at & bit) != 0
        return jnp.where(upper, jnp.concatenate([other, cur]), jnp.concatenate([cur, other]))

    def attn_half(half):
        qkv_part = lax.dynamic_slice_in_dim(qkv_weight, half * attn_cols, attn_cols, axis=2)
        qkv_part = qkv_part.reshape(shard_rows, 3, pairs, LANES).transpose(0, 2, 1, 3)
        out_part = lax.dynamic_slice_in_dim(out_weight, half * attn_cols, attn_cols, axis=0)
        return jnp.concatenate([qkv_part.reshape(shard_rows, qkv_cols), out_part.T], axis=1)

    def up_half(half):
        return lax.dynamic_slice_in_dim(up_weight, half * mlp_cols, mlp_cols, axis=1)

    def down_half(half):
        return lax.dynamic_slice_in_dim(down_weight, half * mlp_cols, mlp_cols, axis=0).T

    def pair_join(own, other):
        return jnp.where(pair_at == 0, jnp.concatenate([own, other]), jnp.concatenate([other, own]))

    class Box:
        def __init__(self, val):
            self.val = val

    class Line:
        tokens = []

        def tie(self, *boxes):
            held = []
            for box in (*boxes, *self.tokens):
                if box not in held:
                    held.append(box)
            if len(held) > 1:
                for box, val in zip(held, lax.optimization_barrier(tuple(box.val for box in held))):
                    box.val = val

        def run(self, piece, *boxes):
            self.tie(*boxes)
            results = [Box(val) for val in piece(*(box.val for box in boxes))]
            self.tokens = [results[0]]
            return results

        def sync(self, box):
            self.tokens = self.tokens + [box]

    order = Line()

    class Gather:
        def __init__(self, shard):
            self.parts = [shard]

        def move(self):
            if len(self.parts) < line:
                order.tie(self.parts[-1])
                self.parts.append(Box(lax.ppermute(self.parts[-1].val, "fsdp", ring)))

        def sync(self):
            order.sync(self.parts[-1])

        def finish(self):
            while len(self.parts) < line:
                self.move()
            self.sync()

        def vals(self):
            return [part.val for part in self.parts]

    class Scatter:
        def __init__(self, part):
            self.part, self.step, self.came = part, 1, None

        def total(self):
            at_line = lax.rem(line_at + line - self.step, line)
            own = lax.dynamic_slice_in_dim(self.part.val, at_line * line_rows, line_rows, axis=0)
            if self.came is None:
                return own
            order.tie(self.came)
            return self.came.val.astype(F32) + own.astype(F32)

        def move(self):
            if self.step < line:
                sent = Box(self.total().astype(BF))
                if self.came is None:
                    order.tie(sent)
                self.came = Box(lax.ppermute(sent.val, "fsdp", ring))
                self.step += 1

        def sync(self):
            order.sync(self.came)

        def swap(self):
            while self.step < line:
                self.move()
            total = self.total()
            self.keep = lax.dynamic_slice_in_dim(total, pair_at * shard_rows, shard_rows, axis=0)
            give = lax.dynamic_slice_in_dim(total, (1 - pair_at) * shard_rows, shard_rows, axis=0)
            self.got = Box(swap_pair(give.astype(BF)))

        def halves(self):
            got = self.got.val.astype(F32)
            return jnp.where(pair_at == 0, self.keep, got), jnp.where(pair_at == 0, got, self.keep)

    class SmallSum:
        def __init__(self, everywhere, over_fsdp):
            self.cur, self.rest = Box(everywhere), over_fsdp
            self.size = everywhere.shape[0]
            bits = [("tp", tp_size, bit) for bit in range(tp_size.bit_length() - 1)]
            self.steps = bits + [("fsdp", fsdp_size, bit) for bit in range(fsdp_size.bit_length() - 1)]

        def move(self):
            if self.steps:
                axis, size, bit = self.steps.pop(0)
                if axis == "fsdp" and bit == 0:
                    self.cur = Box(jnp.concatenate([self.cur.val, self.rest]))
                order.tie(self.cur)
                other = lax.ppermute(self.cur.val, axis, [(i, i ^ (1 << bit)) for i in range(size)])
                self.cur = Box(self.cur.val + other)

        def split(self):
            while self.steps:
                self.move()
            return self.cur.val[: self.size], self.cur.val[self.size :]

    plain = normalise(inputs[:, 0])
    cots = [cotangent[m].reshape(token_rows, model_width) for m in range(micro_count)]
    micros = range(micro_count)
    plane_rows, plane_cots = [None] * micro_count, [None] * micro_count

    def gather_behind(rows):
        sent = Box(rows)
        order.tie(sent)
        return Box(gather_plane(sent.val))

    small = jnp.concatenate(
        [vec.reshape(-1) for vec in (ln_gain, ln_bias, out_bias, down_bias, qkv_bias, up_bias)]
    )
    attn_send = Box(attn_half(1 - pair_at))
    order.tokens = [attn_send]
    plane_rows[0] = gather_behind(plain[0])
    attn_shard = Box(pair_join(attn_half(pair_at), swap_pair(attn_send.val)))
    small_all = Box(small[None])
    order.tokens = [attn_shard]
    order.tie(small_all)
    small_all = small_all.val
    for bit in range(tp_size.bit_length() - 1):
        small_all = doubled(small_all, "tp", tp_size, tp_at, 1 << bit)
    small_near = small_all

    def small_step(small_all, bit):
        if bit < fsdp_size.bit_length() - 1:
            order.tie(small_all)
            return Box(doubled(small_all.val, "fsdp", fsdp_size, fsdp_at, 1 << bit))
        return small_all

    small_all = Box(small_near)
    attn_ring = Gather(attn_shard)
    attn_ring.move()
    plane_rows[1] = gather_behind(plain[1])
    order.sync(small_all)
    small_all = small_step(small_all, 0)
    bias_total = Box(sum(jnp.sum(cots[m].astype(F32), axis=0) for m in micros))
    up_send = Box(up_half(1 - pair_at))
    order.tie(up_send)
    up_got = Box(swap_pair(up_send.val))
    attn_ring.sync()
    order.sync(small_all)
    attn_ring.move()
    order.sync(bias_total)
    small_all = small_step(small_all, 1)
    down_send = Box(down_half(1 - pair_at))
    order.tie(down_send, up_got)
    down_got = Box(swap_pair(down_send.val))
    up_shard = Box(pair_join(up_half(pair_at), up_got.val))
    attn_ring.sync()
    order.sync(small_all)
    attn_ring.move()
    plane_cots[0] = gather_behind(cots[0])
    for bit in range(2, fsdp_size.bit_length() - 1):
        small_all = small_step(small_all, bit)
    order.sync(up_shard)
    order.tie(down_got)
    down_shard = Box(pair_join(down_half(pair_at), down_got.val))
    attn_ring.finish()
    order.sync(small_all)
    order.tie(up_shard)
    small_all = small_all.val
    vec_size = ln_gain.shape[0]
    gain_vec, shift_vec, bias_out, bias_down = (
        small_all[:, i * vec_size : (i + 1) * vec_size].reshape(-1).astype(F32) for i in range(4)
    )
    bias_both = bias_out + bias_down
    mine = lax.dynamic_slice_in_dim(
        small_all.reshape(fsdp_size, tp_size, -1), tp_at, 1, axis=1
    )[:, 0].astype(F32)
    at = 4 * vec_size
    qkv_b = mine[:, at : at + qkv_bias.size].reshape(fsdp_size, 3, 2, pairs, -1, qkv_bias.shape[2])
    qkv_b = lax.dynamic_slice_in_dim(qkv_b, pair_at, 1, axis=2)[:, :, 0]
    qkv_b = qkv_b.transpose(2, 1, 3, 0, 4).reshape(1, qkv_cols)
    at += qkv_bias.size
    up_b = mine[:, at:].reshape(fsdp_size, up_bias.shape[0], up_bias.shape[1])
    up_b = up_b.transpose(1, 0, 2).reshape(2, mlp_cols)
    up_b = lax.dynamic_slice_in_dim(up_b, pair_at, 1, axis=0)

    slots = [lax.rem(line_at + line - step, line) for step in range(line)]
    slots = jnp.stack(slots + [tp_at & 1]).astype(jnp.int32)
    tables = rotary_tables(length, head_dim, ROT)
    gain_row, shift_row = gain_vec[None], shift_vec[None]
    normed, qkvs, rots, attns, lses, acts, slopes = ([None] * micro_count for _ in range(7))
    pre_grads, qkv_grads, qkv_sums, sums, attn_heads = ([None] * micro_count for _ in range(5))

    def norm_piece(m):
        normed[m], qkvs[m] = order.run(
            lambda rows: norm_qkv(slots, rows, gain_row, shift_row, attn_ring.vals(), qkv_b), plane_rows[m]
        )

    def attend_piece(m):
        rots[m], attns[m], lses[m] = order.run(
            lambda vals: attend(vals, tables, length, head_dim), qkvs[m]
        )

    def up_piece():
        def piece(*rows):
            return [val for vals in up_act(slots, rows, up_ring.vals(), up_b) for val in vals]

        results = order.run(piece, *normed)
        acts[:], slopes[:] = results[:micro_count], results[micro_count:]

    def head_grad_piece(m):
        (attn_heads[m],) = order.run(
            lambda cot: [head_grad_rows(slots, cot, attn_ring.vals(), qkv_cols)], plane_cots[m]
        )

    def attend_back_piece(m):
        qkv_grads[m], qkv_sums[m] = order.run(
            lambda rot, grad, attn, lse: attend_back(rot, grad, attn, lse, tables, length, head_dim),
            rots[m],
            attn_heads[m],
            attns[m],
            lses[m],
        )

    def pre_grad_piece():
        def piece(*vals):
            return pre_grad_rows(slots, vals[:micro_count], down_ring.vals(), vals[micro_count:])

        *pre_grads[:], up_sums = order.run(piece, *plane_cots, *slopes)
        return up_sums

    def weight_piece(lefts, *rights):
        def piece(*flat):
            sets = [flat[at : at + micro_count] for at in range(0, len(flat), micro_count)]
            return [weight_grad(sets[0], sets[1:])]

        return Scatter(order.run(piece, *lefts, *(box for right in rights for box in right))[0])

    def branch_piece():
        def piece(*vals):
            rows = branch_rows(
                slots,
                vals[:micro_count],
                attn_ring.vals(),
                qkv_cols,
                vals[micro_count:],
                down_ring.vals(),
                token_rows,
            )
            return [rows.reshape(-1, model_width)]

        return order.run(piece, *attns, *acts)[0]

    def normed_grad_piece(m, split=False):
        *back, sums[m] = order.run(
            lambda one, two, rows: normed_grad_rows(
                slots, one, attn_ring.vals(), two, up_ring.vals(), rows, token_rows, split
            ),
            qkv_grads[m],
            pre_grads[m],
            plane_rows[m],
        )
        return back

    def scatter_behind(box):
        order.tie(box)
        return Box(scatter_plane(box.val))

    up_ring, down_ring = Gather(up_shard), Gather(down_shard)
    order.sync(down_shard)
    up_ring.move()
    norm_piece(0)
    up_ring.sync()
    plane_cots[1] = gather_behind(cots[1])
    up_ring.move()
    attend_piece(0)
    norm_piece(1)
    up_ring.sync()
    up_ring.move()
    attend_piece(1)
    head_grad_piece(0)
    up_ring.finish()
    down_ring.move()
    up_piece()
    down_ring.sync()
    down_ring.move()
    attend_back_piece(0)
    down_ring.sync()
    down_ring.move()

    down_scatter = weight_piece(plane_cots, acts, attns)
    down_ring.finish()
    down_scatter.move()
    branch = branch_piece()
    down_scatter.sync()
    branch_sum = scatter_behind(branch)
    down_scatter.move()
    up_sums = pre_grad_piece()
    down_scatter.sync()
    down_scatter.move()
    up_scatter = weight_piece(normed, pre_grads)
    down_scatter.sync()
    down_scatter.swap()
    up_scatter.move()
    head_grad_piece(1)
    attend_back_piece(1)
    up_scatter.sync()
    order.sync(down_scatter.got)
    up_scatter.move()
    (back,) = normed_grad_piece(0)
    up_scatter.sync()
    order.sync(branch_sum)
    back_sum = scatter_behind(back)
    up_scatter.move()
    qkv_scatter = weight_piece(normed, qkv_grads)
    up_scatter.sync()
    up_scatter.swap()
    qkv_scatter.move()
    keep, give = normed_grad_piece(1, True)

    def swap_core(vals):
        return lax.ppermute(vals, "tp", [(t, t ^ 1) for t in range(tp_size)])

    def swap_y(vals):
        return lax.ppermute(vals, "tp", [(t, t ^ 2) for t in range(tp_size)])

    y_at, half = tp_at >> 1, model_width // 2
    up_b_grad = up_sums.val[0]
    qkv_b_grad = sum(jnp.sum(part.val.reshape(-1, 8, qkv_cols)[:, 0], axis=0) for part in qkv_sums)
    qkv_b_grad = qkv_b_grad.reshape(pairs, 3, -1).transpose(1, 0, 2).reshape(3, attn_cols)

    def in_half(vals):
        blank = jnp.zeros_like(vals)
        return jnp.where(
            pair_at == 0, jnp.concatenate([vals, blank], axis=-1), jnp.concatenate([blank, vals], axis=-1)
        )

    gain_total, shift_total = (sum(part.val[i] for part in sums) for i in range(2))
    tail = SmallSum(
        jnp.concatenate([gain_total, shift_total, bias_total.val]),
        jnp.concatenate([in_half(up_b_grad), in_half(qkv_b_grad).reshape(-1)]),
    )
    qkv_scatter.sync()
    order.sync(up_scatter.got)
    order.tie(give, tail.cur)
    tail.move()
    got = Box(swap_core(give.val))
    qkv_scatter.move()
    order.sync(tail.cur)
    order.tie(got)
    blocks = Box((got.val.astype(F32) + keep.val.astype(F32)).astype(BF).reshape(4, token_rows, model_width))
    tail.move()

    def block(pair, y):
        return lax.dynamic_index_in_dim(blocks.val, pair * 2 + y, 0, keepdims=False)

    order.sync(blocks)
    order.sync(tail.cur)
    order.tie(tail.cur)
    far = block(1 - pair_at, 1 - y_at)
    tail.move()
    from_pair, from_y = Box(swap_pair(far[:, :half])), Box(swap_y(far[:, half:]))
    qkv_scatter.sync()
    order.sync(tail.cur)
    order.tie(tail.cur)
    tail.move()
    qkv_scatter.move()
    order.tie(from_pair, from_y)
    for_y, for_pair = block(pair_at, 1 - y_at), block(1 - pair_at, y_at)
    for_y = jnp.concatenate(
        [(for_y[:, :half].astype(F32) + from_pair.val.astype(F32)).astype(BF), for_y[:, half:]], axis=1
    )
    for_pair = jnp.concatenate(
        [for_pair[:, :half], (for_pair[:, half:].astype(F32) + from_y.val.astype(F32)).astype(BF)], axis=1
    )
    for_pair, for_y = Box(for_pair), Box(for_y)
    from_pair, from_y = Box(swap_pair(for_pair.val)), Box(swap_y(for_y.val))
    order.sync(for_pair)
    order.sync(for_y)
    order.tie(back_sum)
    gained = Box(norm_back(inputs[:, 0], cotangent[:, 0], [back_sum.val], gain_row, 0))
    halves = down_scatter.halves()
    down_w_grad = Box(jnp.concatenate([part[:, :mlp_cols].T for part in halves], axis=0))
    out_w_grad = Box(jnp.concatenate([part[:, mlp_cols:].T for part in halves], axis=0))
    up_w_grad = Box(jnp.concatenate(up_scatter.halves(), axis=1))
    for box in (gained, down_w_grad, out_w_grad, up_w_grad, tail.cur):
        order.sync(box)
    qkv_scatter.sync()
    order.tie(tail.cur)
    tail.move()
    qkv_scatter.swap()
    order.tie(from_pair, from_y)
    last_pieces = [block(pair_at, y_at), from_pair.val, from_y.val]
    gained = norm_back(inputs[:, 0], cotangent[:, 0], last_pieces, gain_row, 1, gained.val)
    small_sums, bias_sums = tail.split()
    branch_sum = branch_sum.val.reshape(micro_count, token_rows, model_width)
    output = (inputs[:, 0].astype(F32) + branch_sum.astype(F32) + bias_both).astype(BF)

    small_sums = small_sums.reshape(3, fsdp_size * tp_size, vec_size)
    small_sums = lax.dynamic_slice_in_dim(small_sums, fsdp_at * tp_size + tp_at, 1, axis=1)[:, 0]
    gain_sum, shift_sum, bias_sum = small_sums[0], small_sums[1], small_sums[2]
    up_b_sum = bias_sums[: 2 * mlp_cols].reshape(up_bias.shape[0], -1)
    up_b_sum = lax.dynamic_slice_in_dim(up_b_sum, fsdp_at * up_bias.shape[1], up_bias.shape[1], axis=1)
    qkv_b_sum = bias_sums[2 * mlp_cols :].reshape(3, qkv_bias.shape[1], -1)
    qkv_b_sum = lax.dynamic_slice_in_dim(qkv_b_sum, fsdp_at * qkv_bias.shape[2], qkv_bias.shape[2], axis=2)

    def qkv_columns(vals):
        return vals.reshape(shard_rows, pairs, 3, LANES).transpose(0, 2, 1, 3).reshape(
            shard_rows, 3, attn_cols
        )

    qkv_w_grad = jnp.concatenate([qkv_columns(part) for part in qkv_scatter.halves()], axis=2)
    return (
        output[:, None],
        gained[:, None],
        gain_sum,
        shift_sum,
        qkv_w_grad,
        qkv_b_sum,
        out_w_grad.val,
        bias_sum,
        up_w_grad.val,
        up_b_sum,
        down_w_grad.val,
        bias_sum,
    )


def solution(mesh):
    return jax.shard_map(
        shards,
        mesh=mesh,
        in_specs=(
            P(None, "fsdp", "tp", None),
            P(("fsdp", "tp")),
            P(("fsdp", "tp")),
            P("fsdp", None, "tp"),
            P(None, "tp", "fsdp"),
            P("tp", "fsdp"),
            P(("fsdp", "tp")),
            P("fsdp", "tp"),
            P("tp", "fsdp"),
            P("tp", "fsdp"),
            P(("fsdp", "tp")),
            P(None, "fsdp", "tp", None),
        ),
        out_specs=(
            P(None, "fsdp", "tp", None),
            P(None, "fsdp", "tp", None),
            P(("fsdp", "tp")),
            P(("fsdp", "tp")),
            P("fsdp", None, "tp"),
            P(None, "tp", "fsdp"),
            P("tp", "fsdp"),
            P(("fsdp", "tp")),
            P("fsdp", "tp"),
            P("tp", "fsdp"),
            P("tp", "fsdp"),
            P(("fsdp", "tp")),
        ),
        check_vma=False,
    )
```

```python
import functools
import math

import jax
import jax.numpy as jnp
from jax import lax
from jax.experimental import pallas as pl
from jax.experimental.pallas import tpu as pltpu
from jax.sharding import PartitionSpec as P

ROT = 32
LANES = 128

norm_epsilon = 1e-05
gelu_factor = 0.7978845608028654
mask_fill = -1e30
BF = jnp.bfloat16
F32 = jnp.float32
VMEM_LIMIT = 56 * 1024 * 1024


def rotary_tables(length, head_dim, rot_dim):
    half_rot = rot_dim // 2
    inv_freq = 10000.0 ** (-2.0 * jnp.arange(half_rot, dtype=F32) / rot_dim)
    angles = jnp.arange(length, dtype=F32)[:, None] * inv_freq[None, :]
    cos, sin = jnp.cos(angles), jnp.sin(angles)
    rest = jnp.ones((length, head_dim - rot_dim), F32)
    cosine = jnp.concatenate([cos, cos, rest], axis=1)
    lower = jnp.concatenate([-sin, 0.0 * sin, 0.0 * rest], axis=1)
    upper = jnp.concatenate([0.0 * sin, sin, 0.0 * rest], axis=1)
    copies = LANES // head_dim
    return tuple(jnp.tile(table, (1, copies)) for table in (cosine, lower, upper))


def turn(vals, cosine, lower, upper):
    half_rot = ROT // 2
    ahead = pltpu.roll(vals, LANES - half_rot, 1)
    behind = pltpu.roll(vals, half_rot, 1)
    return vals * cosine + ahead * lower + behind * upper


def dot_rows(left, right):
    return lax.dot_general(left, right, (((0,), (0,)), ((), ())), preferred_element_type=F32)


def dot_cols(left, right):
    return lax.dot_general(left, right, (((1,), (1,)), ((), ())), preferred_element_type=F32)


def dot_plain(left, right):
    return lax.dot_general(left, right, (((1,), (0,)), ((), ())), preferred_element_type=F32)


def head_lanes(vals, head, head_dim):
    lane_ids = lax.broadcasted_iota(jnp.int32, vals.shape, 1)
    return jnp.where(lane_ids // head_dim == head, vals, jnp.zeros_like(vals))


def seen_keys(block):
    key_ids = lax.broadcasted_iota(jnp.int32, (block, block), 0)
    return key_ids <= lax.broadcasted_iota(jnp.int32, (block, block), 1)


def attend_kernel(head_dim, block, qkv_ref, cos_ref, low_ref, up_ref, rot_ref, attn_ref, lse_ref):
    length = qkv_ref.shape[0]
    scale = 1.0 / math.sqrt(head_dim)
    tables = (cos_ref[...], low_ref[...], up_ref[...])
    rot_ref[:, :LANES] = turn(qkv_ref[:, :LANES], *tables).astype(BF) * BF(scale)
    rot_ref[:, LANES : 2 * LANES] = turn(qkv_ref[:, LANES : 2 * LANES], *tables).astype(BF)
    rot_ref[:, 2 * LANES :] = qkv_ref[:, 2 * LANES :].astype(BF)
    heads = LANES // head_dim
    seen = seen_keys(block)
    for first in range(0, length, block):
        last = first + block
        total = jnp.zeros((block, LANES), F32)
        for head in range(heads):
            query_block = head_lanes(rot_ref[first:last, :LANES], head, head_dim)
            scores = jnp.where(seen, dot_cols(rot_ref[first:last, LANES : 2 * LANES], query_block), mask_fill)
            col_max = jnp.max(scores, axis=0, keepdims=True)
            if first:
                before = dot_cols(rot_ref[:first, LANES : 2 * LANES], query_block)
                col_max = jnp.maximum(col_max, jnp.max(before, axis=0, keepdims=True))
            probs = jnp.exp(scores - col_max)
            denom = jnp.sum(probs, axis=0, keepdims=True)
            part = dot_rows(probs.astype(BF), head_lanes(rot_ref[first:last, 2 * LANES :], head, head_dim))
            if first:
                probs = jnp.exp(before - col_max)
                denom += jnp.sum(probs, axis=0, keepdims=True)
                part += dot_rows(probs.astype(BF), head_lanes(rot_ref[:first, 2 * LANES :], head, head_dim))
            total += part * jnp.broadcast_to(1.0 / denom, (LANES, block)).T
            lse_ref[0, head : head + 1, first:last] = col_max + jnp.log(denom)
        attn_ref[first:last, :] = total.astype(BF)


def attend_back_kernel(head_dim, block, rot_ref, grad_ref, attn_ref, lse_ref, cos_ref, low_ref, up_ref, out_ref, sum_ref, key_acc, value_acc):
    length = rot_ref.shape[0]
    scale = 1.0 / math.sqrt(head_dim)
    heads = LANES // head_dim
    seen = seen_keys(block)

    def back(vals, span):
        return turn(vals, cos_ref[span, :], -low_ref[span, :], -up_ref[span, :])

    query_sum = jnp.zeros((1, LANES), F32)
    key_acc[...] = jnp.zeros_like(key_acc)
    value_acc[...] = jnp.zeros_like(value_acc)
    for first in range(0, length, block):
        last = first + block
        total = jnp.zeros((block, LANES), F32)
        inner = (grad_ref[first:last, :].astype(F32) * attn_ref[first:last, :].astype(F32)).T
        for head in range(heads):
            query_block = head_lanes(rot_ref[first:last, :LANES], head, head_dim)
            grad_block = head_lanes(grad_ref[first:last, :], head, head_dim)
            lse = lse_ref[0, head : head + 1, first:last]
            inner_sum = jnp.sum(inner[head * head_dim : (head + 1) * head_dim], axis=0, keepdims=True)
            for start, stop in ((0, first), (first, last)):
                if start == stop:
                    continue
                keys = rot_ref[start:stop, LANES : 2 * LANES]
                probs = jnp.exp(dot_cols(keys, query_block) - lse)
                if start == first:
                    probs = jnp.where(seen, probs, 0.0)
                value_acc[start:stop, :] += dot_plain(probs.astype(BF), grad_block)
                prob_grad = dot_cols(rot_ref[start:stop, 2 * LANES :], grad_block)
                score_grad = (probs * (prob_grad - inner_sum)).astype(BF)
                total += dot_rows(score_grad, head_lanes(keys, head, head_dim))
                key_acc[start:stop, :] += dot_plain(score_grad, query_block)
        turned = back(total * scale, slice(first, last))
        query_sum += jnp.sum(turned, axis=0, keepdims=True)
        out_ref[first:last, :LANES] = turned.astype(BF)
    turned = back(key_acc[...], slice(0, length))
    out_ref[:, LANES : 2 * LANES] = turned.astype(BF)
    out_ref[:, 2 * LANES :] = value_acc[...].astype(BF)
    sum_ref[0:1, :LANES] = query_sum
    sum_ref[0:1, LANES : 2 * LANES] = jnp.sum(turned, axis=0, keepdims=True)
    sum_ref[0:1, 2 * LANES :] = jnp.sum(value_acc[...], axis=0, keepdims=True)


def attention_cost(seqs, pairs, length, matmuls):
    flops = seqs * pairs * matmuls * 2 * 2 * length * length * LANES
    return estimate(flops, seqs * pairs * length * LANES * 16)


def attend(qkv, tables, length, head_dim):
    tokens, width = qkv.shape
    seqs, pairs = tokens // length, width // (3 * LANES)
    heads = LANES // head_dim
    block = min(512, length)
    table_spec = pl.BlockSpec((length, LANES), lambda s, h: (0, 0))
    return pl.pallas_call(
        functools.partial(attend_kernel, head_dim, block),
        grid=(seqs, pairs),
        in_specs=[pl.BlockSpec((length, 3 * LANES), lambda s, h: (s, h))] + [table_spec] * 3,
        out_specs=[
            pl.BlockSpec((length, 3 * LANES), lambda s, h: (s, h)),
            pl.BlockSpec((length, LANES), lambda s, h: (s, h)),
            pl.BlockSpec((1, heads, length), lambda s, h: (s * pairs + h, 0, 0)),
        ],
        out_shape=[
            jax.ShapeDtypeStruct((tokens, width), BF),
            jax.ShapeDtypeStruct((tokens, pairs * LANES), BF),
            jax.ShapeDtypeStruct((seqs * pairs, heads, length), F32),
        ],
        compiler_params=pltpu.CompilerParams(vmem_limit_bytes=VMEM_LIMIT),
        cost_estimate=attention_cost(seqs, pairs, length, 3),
    )(qkv, *tables)


def attend_back(rot, attn_grad, attn, lse, tables, length, head_dim):
    tokens, width = rot.shape
    seqs, pairs = tokens // length, width // (3 * LANES)
    heads = LANES // head_dim
    block = min(512, length)
    table_spec = pl.BlockSpec((length, LANES), lambda s, h: (0, 0))
    return pl.pallas_call(
        functools.partial(attend_back_kernel, head_dim, block),
        grid=(seqs, pairs),
        in_specs=[
            pl.BlockSpec((length, 3 * LANES), lambda s, h: (s, h)),
            pl.BlockSpec((length, LANES), lambda s, h: (s, h)),
            pl.BlockSpec((length, LANES), lambda s, h: (s, h)),
            pl.BlockSpec((1, heads, length), lambda s, h: (s * pairs + h, 0, 0)),
        ]
        + [table_spec] * 3,
        out_specs=[
            pl.BlockSpec((length, 3 * LANES), lambda s, h: (s, h)),
            pl.BlockSpec((8, 3 * LANES), lambda s, h: (s, h)),
        ],
        out_shape=[jax.ShapeDtypeStruct((tokens, width), BF), jax.ShapeDtypeStruct((8 * seqs, width), F32)],
        scratch_shapes=[pltpu.VMEM((length, LANES), F32), pltpu.VMEM((length, LANES), F32)],
        compiler_params=pltpu.CompilerParams(vmem_limit_bytes=VMEM_LIMIT),
        cost_estimate=attention_cost(seqs, pairs, length, 6),
    )(rot, attn_grad, attn, lse, *tables)


def spec_rows(tile, width):
    return pl.BlockSpec((tile, width), lambda i, s: (i, 0))


def spec_whole(array):
    return pl.BlockSpec(array.shape, lambda i, s: (0,) * array.ndim)


def estimate(flops, moved):
    return pl.CostEstimate(flops=int(flops) // 64, bytes_accessed=int(moved) // 64, transcendentals=0)


def lined_dot(slots_ref, rows_ref, parts, cols):
    depth = parts[0].shape[0]
    total = None
    for at, part in enumerate(parts):
        first = pl.multiple_of(slots_ref[at] * depth, depth)
        piece = dot_plain(rows_ref[:, pl.ds(first, depth)], part[:, cols])
        total = piece if total is None else total + piece
    return total


def rows_call(kernel, slots, ins, in_specs, outs, tile, cost, out_specs=None, steps=None):
    return pl.pallas_call(
        kernel,
        grid_spec=pltpu.PrefetchScalarGridSpec(
            num_scalar_prefetch=1,
            grid=(steps or outs[0].shape[0] // tile,),
            in_specs=in_specs,
            out_specs=out_specs or [spec_rows(tile, out.shape[1]) for out in outs],
        ),
        out_shape=outs,
        compiler_params=pltpu.CompilerParams(vmem_limit_bytes=VMEM_LIMIT),
        cost_estimate=cost,
    )(slots, *ins)


def normalise(rows):
    micros, tokens, width = rows.shape

    def kernel(rows_ref, out_ref):
        vals = rows_ref[0].astype(F32)
        mean = jnp.mean(vals, axis=-1, keepdims=True)
        centred = vals - mean
        var = jnp.mean(centred * centred, axis=-1, keepdims=True)
        out_ref[...] = (centred * lax.rsqrt(var + norm_epsilon)).astype(BF)

    def one(micro):
        return pl.pallas_call(
            kernel,
            grid=(2,),
            in_specs=[pl.BlockSpec((1, tokens // 2, width), lambda i: (micro, i, 0))],
            out_specs=pl.BlockSpec((tokens // 2, width), lambda i: (i, 0)),
            out_shape=jax.ShapeDtypeStruct((tokens, width), BF),
            compiler_params=pltpu.CompilerParams(vmem_limit_bytes=VMEM_LIMIT),
            cost_estimate=estimate(10 * tokens * width, 4 * tokens * width),
        )(rows)

    return [one(micro) for micro in range(micros)]


def norm_qkv(slots, rows, gain, shift, parts, bias):
    tokens, width = rows.shape
    cols, tile = bias.shape[1], 512

    def kernel(slots_ref, rows_ref, gain_ref, shift_ref, bias_ref, *refs):
        parts, (normed_ref, qkv_ref) = refs[:-2], refs[-2:]
        normed_ref[...] = (rows_ref[...].astype(F32) * gain_ref[...] + shift_ref[...]).astype(BF)
        qkv_ref[...] = lined_dot(slots_ref, normed_ref, parts, slice(0, cols)) + bias_ref[...]

    return rows_call(
        kernel,
        slots,
        [rows, gain, shift, bias, *parts],
        [spec_rows(tile, width)] + [spec_whole(array) for array in (gain, shift, bias, *parts)],
        [jax.ShapeDtypeStruct((tokens, width), BF), jax.ShapeDtypeStruct((tokens, cols), F32)],
        tile,
        estimate(2 * tokens * width * cols, tokens * (4 * width + 4 * cols)),
    )


def micro_spec(micro, steps, tile, width):
    return pl.BlockSpec((tile, width), lambda i, s: (jnp.clip(i - micro * steps, 0, steps - 1), 0))


def up_act(slots, rows, parts, bias):
    count = len(rows)
    tokens, width = rows[0].shape
    cols, tile, chunk = bias.shape[1], 512, 512
    steps = tokens // tile

    def kernel(slots_ref, bias_ref, *refs):
        ins, parts, outs = refs[:count], refs[count : -2 * count], refs[-2 * count :]
        for micro in range(count):

            @pl.when(pl.program_id(0) // steps == micro)
            def _():
                for at in range(0, cols, chunk):
                    span = slice(at, at + chunk)
                    pre = lined_dot(slots_ref, ins[micro], parts, span) + bias_ref[:, span]
                    square = pre * pre
                    tanh = jnp.tanh(pre * (gelu_factor + (gelu_factor * 0.044715) * square))
                    half = 0.5 + 0.5 * tanh
                    act = pre * half
                    outs[micro][:, span] = act.astype(BF)
                    inner = 2 * gelu_factor + (6 * 0.044715 * gelu_factor) * square
                    outs[count + micro][:, span] = (half + (act - act * half) * inner).astype(BF)

    outs = rows_call(
        kernel,
        slots,
        [bias, *rows, *parts],
        [spec_whole(bias)]
        + [micro_spec(m, steps, tile, width) for m in range(count)]
        + [spec_whole(part) for part in parts],
        [jax.ShapeDtypeStruct((tokens, cols), BF)] * (2 * count),
        tile,
        estimate(2 * count * tokens * width * cols, count * tokens * (2 * width + 4 * cols)),
        [micro_spec(m, steps, tile, cols) for m in range(count)] * 2,
        count * steps,
    )
    return outs[:count], outs[count:]


def pre_grad_rows(slots, rows, parts, slopes):
    count = len(rows)
    tokens, width = rows[0].shape
    cols, tile = slopes[0].shape[1], 512
    steps = tokens // tile

    def kernel(slots_ref, *refs):
        ins, slopes, parts = refs[:count], refs[count : 2 * count], refs[2 * count : -count - 1]
        outs, sum_ref = refs[-count - 1 : -1], refs[-1]

        @pl.when(pl.program_id(0) == 0)
        def _():
            sum_ref[...] = jnp.zeros_like(sum_ref)

        for micro in range(count):

            @pl.when(pl.program_id(0) // steps == micro)
            def _():
                act_grad = lined_dot(slots_ref, ins[micro], parts, slice(0, cols))
                grad = act_grad * slopes[micro][...].astype(F32)
                outs[micro][...] = grad.astype(BF)
                sum_ref[0:1, :] += jnp.sum(grad, axis=0, keepdims=True)

    return rows_call(
        kernel,
        slots,
        [*rows, *slopes, *parts],
        [micro_spec(m, steps, tile, width) for m in range(count)]
        + [micro_spec(m, steps, tile, cols) for m in range(count)]
        + [spec_whole(part) for part in parts],
        [jax.ShapeDtypeStruct((tokens, cols), BF)] * count + [jax.ShapeDtypeStruct((8, cols), F32)],
        tile,
        estimate(2 * count * tokens * width * cols, count * tokens * (2 * width + 4 * cols)),
        [micro_spec(m, steps, tile, cols) for m in range(count)] + [pl.BlockSpec((8, cols), lambda i, s: (0, 0))],
        count * steps,
    )


def head_grad_rows(slots, rows, parts, first):
    tokens, width = rows.shape
    cols, tile = parts[0].shape[1] - first, 1024

    def kernel(slots_ref, rows_ref, *refs):
        parts, out_ref = refs[:-1], refs[-1]
        out_ref[...] = lined_dot(slots_ref, rows_ref, parts, slice(first, first + cols)).astype(BF)

    return rows_call(
        kernel,
        slots,
        [rows, *parts],
        [spec_rows(tile, width)] + [spec_whole(part) for part in parts],
        [jax.ShapeDtypeStruct((tokens, cols), BF)],
        tile,
        estimate(2 * tokens * width * cols, tokens * (2 * width + 2 * cols)),
    )[0]


def branch_rows(slots, ones, one_parts, first, twos, two_parts, block):
    micros = len(ones)
    tokens, cols = ones[0].shape
    count, depth = len(one_parts), one_parts[0].shape[0]
    held = 2
    tile = held * block
    width, steps = count * depth, tokens // tile

    def kernel(slots_ref, *refs):
        ones, twos, out_ref = refs[:micros], refs[micros : 2 * micros], refs[-1]
        parts = refs[2 * micros : -1]
        for micro in range(micros):

            @pl.when(pl.program_id(0) // steps == micro)
            def _():
                for at in range(count):
                    where = pl.multiple_of(slots_ref[at] * depth, depth)
                    total = dot_cols(ones[micro][...], parts[at][:, first : first + cols])
                    total += dot_cols(twos[micro][...], parts[count + at][...])
                    out_ref[:, 0, :, pl.ds(where, depth)] = total.astype(BF).reshape(held, block, depth)

    return rows_call(
        kernel,
        slots,
        [*ones, *twos, *one_parts, *two_parts],
        [micro_spec(m, steps, tile, cols) for m in range(micros)]
        + [micro_spec(m, steps, tile, twos[0].shape[1]) for m in range(micros)]
        + [spec_whole(part) for part in (*one_parts, *two_parts)],
        [jax.ShapeDtypeStruct((tokens // block, micros, block, width), BF)],
        tile,
        estimate(2 * micros * tokens * width * (cols + twos[0].shape[1]), 2 * micros * tokens * (width + cols)),
        [pl.BlockSpec((held, 1, block, width), lambda i, s: (lax.rem(i, steps), i // steps, 0, 0))],
        micros * steps,
    )[0]


def normed_grad_rows(slots, one, one_parts, two, two_parts, rows, block, split):
    tokens, cols = one.shape
    count, depth = len(one_parts), one_parts[0].shape[0]
    tile = 2 * block
    width = count * depth

    def kernel(slots_ref, one_ref, two_ref, rows_ref, *refs):
        outs, sum_ref = refs[2 * count : -1], refs[-1]

        @pl.when(pl.program_id(0) == 0)
        def _():
            sum_ref[...] = jnp.zeros_like(sum_ref)

        for at in range(count):
            where = pl.multiple_of(slots_ref[at] * depth, depth)
            span = pl.ds(where, depth)
            total = dot_cols(one_ref[...], refs[at][:, :cols])
            total += dot_cols(two_ref[...], refs[count + at][...])
            if split:
                first = slots_ref[count] == 0
                outs[0][:, span] = jnp.where(first, total[:block], total[block:]).astype(BF)
                outs[1][:, span] = jnp.where(first, total[block:], total[:block]).astype(BF)
            else:
                outs[0][:, span] = total.astype(BF)
            sum_ref[0:1, span] += jnp.sum(total * rows_ref[:, span].astype(F32), axis=0, keepdims=True)
            sum_ref[1:2, span] += jnp.sum(total, axis=0, keepdims=True)

    pieces = 2 if split else 1
    return rows_call(
        kernel,
        slots,
        [one, two, rows, *one_parts, *two_parts],
        [spec_rows(tile, cols), spec_rows(tile, two.shape[1]), spec_rows(tile, width)]
        + [spec_whole(part) for part in (*one_parts, *two_parts)],
        [jax.ShapeDtypeStruct((tokens // pieces, width), BF)] * pieces + [jax.ShapeDtypeStruct((8, width), F32)],
        tile,
        estimate(2 * tokens * width * (cols + two.shape[1]), 2 * tokens * (2 * width + cols + two.shape[1])),
        [spec_rows(tile // pieces, width)] * pieces + [pl.BlockSpec((8, width), lambda i, s: (0, 0))],
        tokens // tile,
    )


def norm_back(rows, cots, pieces, gain, micro, earlier=None):
    micros, tokens, width = rows.shape
    tile = tokens // 4

    def kernel(rows_ref, cot_ref, gain_ref, *refs):
        vals = rows_ref[0].astype(F32)
        mean = jnp.mean(vals, axis=-1, keepdims=True)
        centred = vals - mean
        scale = lax.rsqrt(jnp.mean(centred * centred, axis=-1, keepdims=True) + norm_epsilon)
        scaled = centred * scale
        grad = refs[0][...].astype(F32)
        for ref in refs[1 : len(pieces)]:
            grad += ref[...].astype(F32)
        grad *= gain_ref[...]
        inner = jnp.mean(grad * scaled, axis=-1, keepdims=True)
        grad = (grad - jnp.mean(grad, axis=-1, keepdims=True) - scaled * inner) * scale
        refs[-1][0] = (cot_ref[0].astype(F32) + grad).astype(BF)

    at_micro = pl.BlockSpec((1, tile, width), lambda i: (micro, i, 0))
    given = [] if earlier is None else [earlier]
    return pl.pallas_call(
        kernel,
        grid=(tokens // tile,),
        in_specs=[at_micro, at_micro, pl.BlockSpec((1, width), lambda i: (0, 0))]
        + [pl.BlockSpec((tile, width), lambda i: (i, 0))] * len(pieces)
        + [pl.BlockSpec(memory_space=pl.ANY)] * len(given),
        out_specs=at_micro,
        out_shape=jax.ShapeDtypeStruct(rows.shape, BF),
        input_output_aliases={3 + len(pieces): 0} if given else {},
        compiler_params=pltpu.CompilerParams(vmem_limit_bytes=VMEM_LIMIT),
        cost_estimate=estimate(20 * tokens * width, 10 * tokens * width),
    )(rows, cots, gain, *pieces, *given)


def weight_grad(lefts, rights):
    tile, chunk = 512, 512
    micro_count = len(lefts)
    tokens, width = lefts[0].shape
    widths = [right[0].shape[1] for right in rights]
    cols, steps = sum(widths), tokens // tile

    def kernel(*refs):
        out_ref, acc_ref = refs[-2:]
        step = pl.program_id(0)

        @pl.when(step == 0)
        def _():
            acc_ref[...] = jnp.zeros_like(acc_ref)

        for micro in range(micro_count):

            @pl.when(step // steps == micro)
            def _():
                first = 0
                for at, span in enumerate(widths):
                    right = refs[(1 + at) * micro_count + micro]
                    for row in range(0, width, chunk):
                        acc_ref[row : row + chunk, first : first + span] += dot_rows(
                            refs[micro][:, row : row + chunk], right[...]
                        )
                    first += span

        @pl.when(step == micro_count * steps - 1)
        def _():
            out_ref[...] = acc_ref[...].astype(BF)

    def side(micro, span):
        return pl.BlockSpec((tile, span), lambda i: (jnp.clip(i - micro * steps, 0, steps - 1), 0))

    return pl.pallas_call(
        kernel,
        grid=(micro_count * steps,),
        in_specs=[side(micro, span) for span in (width, *widths) for micro in range(micro_count)],
        out_specs=pl.BlockSpec((width, cols), lambda i: (0, 0)),
        out_shape=jax.ShapeDtypeStruct((width, cols), BF),
        scratch_shapes=[pltpu.VMEM((width, cols), F32)],
        compiler_params=pltpu.CompilerParams(vmem_limit_bytes=VMEM_LIMIT),
        cost_estimate=estimate(
            2 * micro_count * tokens * width * cols, 2 * micro_count * tokens * (width + cols)
        ),
    )(*lefts, *(array for right in rights for array in right))


def shards(
    inputs,
    ln_gain,
    ln_bias,
    qkv_weight,
    qkv_bias,
    out_weight,
    out_bias,
    up_weight,
    up_bias,
    down_weight,
    down_bias,
    cotangent,
):
    micro_count, _, token_rows, model_width = inputs.shape
    fsdp_size, tp_size = lax.axis_size("fsdp"), lax.axis_size("tp")
    line = fsdp_size // 2
    fsdp_at, tp_at = lax.axis_index("fsdp"), lax.axis_index("tp")
    line_at, pair_at = fsdp_at >> 1, fsdp_at & 1
    plane_size = 2 * tp_size
    planes = [[plane * plane_size + i for i in range(plane_size)] for plane in range(line)]
    ring = [(f, ((f // 2 + 1) % line) * 2 + f % 2) for f in range(fsdp_size)]
    length = token_rows * tp_size
    head_dim = qkv_bias.shape[2] * fsdp_size
    shard_rows = model_width // fsdp_size
    line_rows = 2 * shard_rows
    attn_cols = out_weight.shape[0] // 2
    qkv_cols = 3 * attn_cols
    pairs = attn_cols // LANES
    mlp_cols = up_weight.shape[1] // 2
    both_axes = ("fsdp", "tp")

    def swap_pair(vals):
        return lax.ppermute(vals, "fsdp", [(f, f ^ 1) for f in range(fsdp_size)])

    def gather_plane(vals):
        return lax.all_gather(vals, both_axes, axis=0, tiled=True, axis_index_groups=planes)

    def scatter_plane(vals):
        return lax.psum_scatter(vals, both_axes, scatter_dimension=0, tiled=True, axis_index_groups=planes)

    def doubled(cur, axis, size, at, bit):
        other = lax.ppermute(cur, axis, [(i, i ^ bit) for i in range(size)])
        upper = (at & bit) != 0
        return jnp.where(upper, jnp.concatenate([other, cur]), jnp.concatenate([cur, other]))

    def attn_half(half):
        qkv_part = lax.dynamic_slice_in_dim(qkv_weight, half * attn_cols, attn_cols, axis=2)
        qkv_part = qkv_part.reshape(shard_rows, 3, pairs, LANES).transpose(0, 2, 1, 3)
        out_part = lax.dynamic_slice_in_dim(out_weight, half * attn_cols, attn_cols, axis=0)
        return jnp.concatenate([qkv_part.reshape(shard_rows, qkv_cols), out_part.T], axis=1)

    def up_half(half):
        return lax.dynamic_slice_in_dim(up_weight, half * mlp_cols, mlp_cols, axis=1)

    def down_half(half):
        return lax.dynamic_slice_in_dim(down_weight, half * mlp_cols, mlp_cols, axis=0).T

    def pair_join(own, other):
        return jnp.where(pair_at == 0, jnp.concatenate([own, other]), jnp.concatenate([other, own]))

    class Box:
        def __init__(self, val):
            self.val = val

    class Line:
        tokens = []

        def tie(self, *boxes):
            held = []
            for box in (*boxes, *self.tokens):
                if box not in held:
                    held.append(box)
            if len(held) > 1:
                for box, val in zip(held, lax.optimization_barrier(tuple(box.val for box in held))):
                    box.val = val

        def run(self, piece, *boxes):
            self.tie(*boxes)
            results = [Box(val) for val in piece(*(box.val for box in boxes))]
            self.tokens = [results[0]]
            return results

        def sync(self, box):
            self.tokens = self.tokens + [box]

    order = Line()

    class Gather:
        def __init__(self, shard):
            self.parts = [shard]

        def move(self):
            if len(self.parts) < line:
                order.tie(self.parts[-1])
                self.parts.append(Box(lax.ppermute(self.parts[-1].val, "fsdp", ring)))

        def sync(self):
            order.sync(self.parts[-1])

        def finish(self):
            while len(self.parts) < line:
                self.move()
            self.sync()

        def vals(self):
            return [part.val for part in self.parts]

    class Scatter:
        def __init__(self, part):
            self.part, self.step, self.came = part, 1, None

        def total(self):
            at_line = lax.rem(line_at + line - self.step, line)
            own = lax.dynamic_slice_in_dim(self.part.val, at_line * line_rows, line_rows, axis=0)
            if self.came is None:
                return own
            order.tie(self.came)
            return self.came.val.astype(F32) + own.astype(F32)

        def move(self):
            if self.step < line:
                sent = Box(self.total().astype(BF))
                if self.came is None:
                    order.tie(sent)
                self.came = Box(lax.ppermute(sent.val, "fsdp", ring))
                self.step += 1

        def sync(self):
            order.sync(self.came)

        def swap(self):
            while self.step < line:
                self.move()
            total = self.total()
            self.keep = lax.dynamic_slice_in_dim(total, pair_at * shard_rows, shard_rows, axis=0)
            give = lax.dynamic_slice_in_dim(total, (1 - pair_at) * shard_rows, shard_rows, axis=0)
            self.got = Box(swap_pair(give.astype(BF)))

        def halves(self):
            got = self.got.val.astype(F32)
            return jnp.where(pair_at == 0, self.keep, got), jnp.where(pair_at == 0, got, self.keep)

    class SmallSum:
        def __init__(self, everywhere, over_fsdp):
            self.cur, self.rest = Box(everywhere), over_fsdp
            self.size = everywhere.shape[0]
            bits = [("tp", tp_size, bit) for bit in range(tp_size.bit_length() - 1)]
            self.steps = bits + [("fsdp", fsdp_size, 0), ("line", 0, 0)]

        def move(self):
            if self.steps:
                axis, size, bit = self.steps.pop(0)
                if axis == "fsdp":
                    self.cur = Box(jnp.concatenate([self.cur.val, self.rest]))
                order.tie(self.cur)
                if axis == "line":
                    others = along_line(self.cur.val)
                else:
                    others = [lax.ppermute(self.cur.val, axis, [(i, i ^ (1 << bit)) for i in range(size)])]
                self.cur = Box(sum(others, self.cur.val))

        def split(self):
            while self.steps:
                self.move()
            return self.cur.val[: self.size], self.cur.val[self.size :]

    plain = normalise(inputs[:, 0])
    cots = [cotangent[m].reshape(token_rows, model_width) for m in range(micro_count)]
    micros = range(micro_count)
    plane_rows, plane_cots = [None] * micro_count, [None] * micro_count

    def gather_behind(rows):
        sent = Box(rows)
        order.tie(sent)
        return Box(gather_plane(sent.val))

    small = jnp.concatenate(
        [vec.reshape(-1) for vec in (ln_gain, ln_bias, out_bias, down_bias, qkv_bias, up_bias)]
    )
    attn_send = Box(attn_half(1 - pair_at))
    order.tokens = [attn_send]
    plane_rows[0] = gather_behind(plain[0])
    attn_shard = Box(pair_join(attn_half(pair_at), swap_pair(attn_send.val)))
    small_all = Box(small[None])
    order.tokens = [attn_shard]
    order.tie(small_all)
    small_all = small_all.val
    for bit in range(tp_size.bit_length() - 1):
        small_all = doubled(small_all, "tp", tp_size, tp_at, 1 << bit)
    small_near = small_all

    def along_line(vals):
        return [lax.ppermute(vals, "fsdp", [(f, f ^ (far << 1)) for f in range(fsdp_size)]) for far in range(1, line)]

    def small_step(small_all, step):
        order.tie(small_all)
        if step == 0:
            return Box(doubled(small_all.val, "fsdp", fsdp_size, fsdp_at, 1))
        held = [small_all.val] + along_line(small_all.val)
        for bit in range(line.bit_length() - 1):
            other = (line_at & (1 << bit)) != 0
            held = [jnp.where(other, held[i ^ (1 << bit)], held[i]) for i in range(line)]
        return Box(jnp.concatenate(held))

    small_all = Box(small_near)
    attn_ring = Gather(attn_shard)
    attn_ring.move()
    plane_rows[1] = gather_behind(plain[1])
    order.sync(small_all)
    small_all = small_step(small_all, 0)
    bias_total = Box(sum(jnp.sum(cots[m].astype(F32), axis=0) for m in micros))
    up_send = Box(up_half(1 - pair_at))
    order.tie(up_send)
    up_got = Box(swap_pair(up_send.val))
    attn_ring.sync()
    order.sync(small_all)
    attn_ring.move()
    order.sync(bias_total)
    small_all = small_step(small_all, 1)
    down_send = Box(down_half(1 - pair_at))
    order.tie(down_send, up_got)
    down_got = Box(swap_pair(down_send.val))
    up_shard = Box(pair_join(up_half(pair_at), up_got.val))
    attn_ring.sync()
    order.sync(small_all)
    attn_ring.move()
    plane_cots[0] = gather_behind(cots[0])
    order.sync(up_shard)
    order.tie(down_got)
    down_shard = Box(pair_join(down_half(pair_at), down_got.val))
    attn_ring.finish()
    order.sync(small_all)
    order.tie(up_shard)
    small_all = small_all.val
    vec_size = ln_gain.shape[0]
    gain_vec, shift_vec, bias_out, bias_down = (
        small_all[:, i * vec_size : (i + 1) * vec_size].reshape(-1).astype(F32) for i in range(4)
    )
    bias_both = bias_out + bias_down
    mine = lax.dynamic_slice_in_dim(
        small_all.reshape(fsdp_size, tp_size, -1), tp_at, 1, axis=1
    )[:, 0].astype(F32)
    at = 4 * vec_size
    qkv_b = mine[:, at : at + qkv_bias.size].reshape(fsdp_size, 3, 2, pairs, -1, qkv_bias.shape[2])
    qkv_b = lax.dynamic_slice_in_dim(qkv_b, pair_at, 1, axis=2)[:, :, 0]
    qkv_b = qkv_b.transpose(2, 1, 3, 0, 4).reshape(1, qkv_cols)
    at += qkv_bias.size
    up_b = mine[:, at:].reshape(fsdp_size, up_bias.shape[0], up_bias.shape[1])
    up_b = up_b.transpose(1, 0, 2).reshape(2, mlp_cols)
    up_b = lax.dynamic_slice_in_dim(up_b, pair_at, 1, axis=0)

    slots = [lax.rem(line_at + line - step, line) for step in range(line)]
    slots = jnp.stack(slots + [tp_at & 1]).astype(jnp.int32)
    tables = rotary_tables(length, head_dim, ROT)
    gain_row, shift_row = gain_vec[None], shift_vec[None]
    normed, qkvs, rots, attns, lses, acts, slopes = ([None] * micro_count for _ in range(7))
    pre_grads, qkv_grads, qkv_sums, sums, attn_heads = ([None] * micro_count for _ in range(5))

    def norm_piece(m):
        normed[m], qkvs[m] = order.run(
            lambda rows: norm_qkv(slots, rows, gain_row, shift_row, attn_ring.vals(), qkv_b), plane_rows[m]
        )

    def attend_piece(m):
        rots[m], attns[m], lses[m] = order.run(
            lambda vals: attend(vals, tables, length, head_dim), qkvs[m]
        )

    def up_piece():
        def piece(*rows):
            return [val for vals in up_act(slots, rows, up_ring.vals(), up_b) for val in vals]

        results = order.run(piece, *normed)
        acts[:], slopes[:] = results[:micro_count], results[micro_count:]

    def head_grad_piece(m):
        (attn_heads[m],) = order.run(
            lambda cot: [head_grad_rows(slots, cot, attn_ring.vals(), qkv_cols)], plane_cots[m]
        )

    def attend_back_piece(m):
        qkv_grads[m], qkv_sums[m] = order.run(
            lambda rot, grad, attn, lse: attend_back(rot, grad, attn, lse, tables, length, head_dim),
            rots[m],
            attn_heads[m],
            attns[m],
            lses[m],
        )

    def pre_grad_piece():
        def piece(*vals):
            return pre_grad_rows(slots, vals[:micro_count], down_ring.vals(), vals[micro_count:])

        *pre_grads[:], up_sums = order.run(piece, *plane_cots, *slopes)
        return up_sums

    def weight_piece(lefts, *rights):
        def piece(*flat):
            sets = [flat[at : at + micro_count] for at in range(0, len(flat), micro_count)]
            return [weight_grad(sets[0], sets[1:])]

        return Scatter(order.run(piece, *lefts, *(box for right in rights for box in right))[0])

    def branch_piece():
        def piece(*vals):
            rows = branch_rows(
                slots,
                vals[:micro_count],
                attn_ring.vals(),
                qkv_cols,
                vals[micro_count:],
                down_ring.vals(),
                token_rows,
            )
            return [rows.reshape(-1, model_width)]

        return order.run(piece, *attns, *acts)[0]

    def normed_grad_piece(m, split=False):
        *back, sums[m] = order.run(
            lambda one, two, rows: normed_grad_rows(
                slots, one, attn_ring.vals(), two, up_ring.vals(), rows, token_rows, split
            ),
            qkv_grads[m],
            pre_grads[m],
            plane_rows[m],
        )
        return back

    def scatter_behind(box):
        order.tie(box)
        return Box(scatter_plane(box.val))

    up_ring, down_ring = Gather(up_shard), Gather(down_shard)
    order.sync(down_shard)
    up_ring.move()
    norm_piece(0)
    up_ring.sync()
    plane_cots[1] = gather_behind(cots[1])
    up_ring.move()
    attend_piece(0)
    norm_piece(1)
    up_ring.sync()
    up_ring.move()
    attend_piece(1)
    head_grad_piece(0)
    up_ring.finish()
    down_ring.move()
    up_piece()
    down_ring.sync()
    down_ring.move()
    attend_back_piece(0)
    down_ring.sync()
    down_ring.move()

    down_scatter = weight_piece(plane_cots, acts, attns)
    down_ring.finish()
    down_scatter.move()
    branch = branch_piece()
    down_scatter.sync()
    branch_sum = scatter_behind(branch)
    down_scatter.move()
    up_sums = pre_grad_piece()
    down_scatter.sync()
    down_scatter.move()
    up_scatter = weight_piece(normed, pre_grads)
    down_scatter.sync()
    down_scatter.swap()
    up_scatter.move()
    head_grad_piece(1)
    attend_back_piece(1)
    up_scatter.sync()
    order.sync(down_scatter.got)
    up_scatter.move()
    (back,) = normed_grad_piece(0)
    up_scatter.sync()
    back_sum = scatter_behind(back)
    up_scatter.move()
    qkv_scatter = weight_piece(normed, qkv_grads)
    up_scatter.sync()
    order.sync(branch_sum)
    up_scatter.swap()
    qkv_scatter.move()
    keep, give = normed_grad_piece(1, True)

    def swap_core(vals):
        return lax.ppermute(vals, "tp", [(t, t ^ 1) for t in range(tp_size)])

    def swap_y(vals):
        return lax.ppermute(vals, "tp", [(t, t ^ 2) for t in range(tp_size)])

    y_at, half = tp_at >> 1, model_width // 2
    up_b_grad = up_sums.val[0]
    qkv_b_grad = sum(jnp.sum(part.val.reshape(-1, 8, qkv_cols)[:, 0], axis=0) for part in qkv_sums)
    qkv_b_grad = qkv_b_grad.reshape(pairs, 3, -1).transpose(1, 0, 2).reshape(3, attn_cols)

    def in_half(vals):
        blank = jnp.zeros_like(vals)
        return jnp.where(
            pair_at == 0, jnp.concatenate([vals, blank], axis=-1), jnp.concatenate([blank, vals], axis=-1)
        )

    gain_total, shift_total = (sum(part.val[i] for part in sums) for i in range(2))
    tail = SmallSum(
        jnp.concatenate([gain_total, shift_total, bias_total.val]),
        jnp.concatenate([in_half(up_b_grad), in_half(qkv_b_grad).reshape(-1)]),
    )
    qkv_scatter.sync()
    order.sync(up_scatter.got)
    order.tie(give, tail.cur)
    tail.move()
    got = Box(swap_core(give.val))
    qkv_scatter.move()
    order.sync(tail.cur)
    order.tie(got)
    blocks = Box((got.val.astype(F32) + keep.val.astype(F32)).astype(BF).reshape(4, token_rows, model_width))
    tail.move()

    def block(pair, y):
        return lax.dynamic_index_in_dim(blocks.val, pair * 2 + y, 0, keepdims=False)

    order.sync(blocks)
    order.sync(tail.cur)
    order.tie(tail.cur)
    far = block(1 - pair_at, 1 - y_at)
    from_pair, from_y = Box(swap_pair(far[:, :half])), Box(swap_y(far[:, half:]))
    tail.move()
    qkv_scatter.sync()
    order.tie()
    qkv_scatter.move()
    order.tie(from_pair, from_y)
    for_y, for_pair = block(pair_at, 1 - y_at), block(1 - pair_at, y_at)
    for_y = jnp.concatenate(
        [(for_y[:, :half].astype(F32) + from_pair.val.astype(F32)).astype(BF), for_y[:, half:]], axis=1
    )
    for_pair = jnp.concatenate(
        [for_pair[:, :half], (for_pair[:, half:].astype(F32) + from_y.val.astype(F32)).astype(BF)], axis=1
    )
    for_pair, for_y = Box(for_pair), Box(for_y)
    from_pair, from_y = Box(swap_pair(for_pair.val)), Box(swap_y(for_y.val))
    order.sync(for_pair)
    order.sync(for_y)
    order.tie(back_sum)
    gained = Box(norm_back(inputs[:, 0], cotangent[:, 0], [back_sum.val], gain_row, 0))
    halves = down_scatter.halves()
    down_w_grad = Box(jnp.concatenate([part[:, :mlp_cols].T for part in halves], axis=0))
    out_w_grad = Box(jnp.concatenate([part[:, mlp_cols:].T for part in halves], axis=0))
    up_w_grad = Box(jnp.concatenate(up_scatter.halves(), axis=1))
    order.sync(gained)
    qkv_scatter.sync()
    order.sync(tail.cur)
    order.tie(tail.cur)
    tail.move()
    qkv_scatter.swap()
    for box in (down_w_grad, out_w_grad, up_w_grad):
        order.sync(box)

    def qkv_columns(vals):
        return vals.reshape(shard_rows, pairs, 3, LANES).transpose(0, 2, 1, 3).reshape(shard_rows, 3, attn_cols)

    order.tie(from_pair, from_y)
    last_pieces = [block(pair_at, y_at), from_pair.val, from_y.val]
    gained = Box(norm_back(inputs[:, 0], cotangent[:, 0], last_pieces, gain_row, 1, gained.val))
    order.tokens = [gained]
    order.tie(qkv_scatter.got, tail.cur)
    qkv_w_grad = Box(jnp.concatenate([qkv_columns(part) for part in qkv_scatter.halves()], axis=2))
    small_sums, bias_sums = tail.split()
    branch_sum = branch_sum.val.reshape(micro_count, token_rows, model_width)
    output = (inputs[:, 0].astype(F32) + branch_sum.astype(F32) + bias_both).astype(BF)

    small_sums = small_sums.reshape(3, fsdp_size * tp_size, vec_size)
    small_sums = lax.dynamic_slice_in_dim(small_sums, fsdp_at * tp_size + tp_at, 1, axis=1)[:, 0]
    gain_sum, shift_sum, bias_sum = small_sums[0], small_sums[1], small_sums[2]
    up_b_sum = bias_sums[: 2 * mlp_cols].reshape(up_bias.shape[0], -1)
    up_b_sum = lax.dynamic_slice_in_dim(up_b_sum, fsdp_at * up_bias.shape[1], up_bias.shape[1], axis=1)
    qkv_b_sum = bias_sums[2 * mlp_cols :].reshape(3, qkv_bias.shape[1], -1)
    qkv_b_sum = lax.dynamic_slice_in_dim(qkv_b_sum, fsdp_at * qkv_bias.shape[2], qkv_bias.shape[2], axis=2)

    return (
        output[:, None],
        gained.val[:, None],
        gain_sum,
        shift_sum,
        qkv_w_grad.val,
        qkv_b_sum,
        out_w_grad.val,
        bias_sum,
        up_w_grad.val,
        up_b_sum,
        down_w_grad.val,
        bias_sum,
    )


def solution(mesh):
    return jax.shard_map(
        shards,
        mesh=mesh,
        in_specs=(
            P(None, "fsdp", "tp", None),
            P(("fsdp", "tp")),
            P(("fsdp", "tp")),
            P("fsdp", None, "tp"),
            P(None, "tp", "fsdp"),
            P("tp", "fsdp"),
            P(("fsdp", "tp")),
            P("fsdp", "tp"),
            P("tp", "fsdp"),
            P("tp", "fsdp"),
            P(("fsdp", "tp")),
            P(None, "fsdp", "tp", None),
        ),
        out_specs=(
            P(None, "fsdp", "tp", None),
            P(None, "fsdp", "tp", None),
            P(("fsdp", "tp")),
            P(("fsdp", "tp")),
            P("fsdp", None, "tp"),
            P(None, "tp", "fsdp"),
            P("tp", "fsdp"),
            P(("fsdp", "tp")),
            P("fsdp", "tp"),
            P("tp", "fsdp"),
            P("tp", "fsdp"),
            P(("fsdp", "tp")),
        ),
        check_vma=False,
    )
```

```python
import functools
import math

import jax
import jax.numpy as jnp
from jax import lax
from jax.experimental import pallas as pl
from jax.experimental.layout import Layout, with_layout_constraint
from jax.experimental.pallas import tpu as pltpu
from jax.sharding import PartitionSpec as P

ROT = 32
LANES = 128

norm_epsilon = 1e-05
gelu_factor = 0.7978845608028654
mask_fill = -1e30
BF = jnp.bfloat16
F32 = jnp.float32
VMEM_LIMIT = 56 * 1024 * 1024


def rotary_tables(length, head_dim, rot_dim):
    half_rot = rot_dim // 2
    places = lax.broadcasted_iota(jnp.int32, (length, LANES), 0).astype(F32)
    lanes = lax.rem(lax.broadcasted_iota(jnp.int32, (length, LANES), 1), head_dim)
    inv_freq = 10000.0 ** (-2.0 * lax.rem(lanes, half_rot).astype(F32) / rot_dim)
    angles = places * inv_freq
    sine = jnp.sin(angles)
    cosine = jnp.where(lanes < rot_dim, jnp.cos(angles), 1.0)
    lower = jnp.where(lanes < half_rot, -sine, 0.0)
    upper = jnp.where((lanes >= half_rot) & (lanes < rot_dim), sine, 0.0)
    return cosine, lower, upper


def turn(vals, cosine, lower, upper):
    half_rot = ROT // 2
    ahead = pltpu.roll(vals, LANES - half_rot, 1)
    behind = pltpu.roll(vals, half_rot, 1)
    return vals * cosine + ahead * lower + behind * upper


def dot_rows(left, right):
    return lax.dot_general(left, right, (((0,), (0,)), ((), ())), preferred_element_type=F32)


def dot_cols(left, right):
    return lax.dot_general(left, right, (((1,), (1,)), ((), ())), preferred_element_type=F32)


def dot_plain(left, right):
    return lax.dot_general(left, right, (((1,), (0,)), ((), ())), preferred_element_type=F32)


def head_lanes(vals, head, head_dim):
    lane_ids = lax.broadcasted_iota(jnp.int32, vals.shape, 1)
    return jnp.where(lane_ids // head_dim == head, vals, jnp.zeros_like(vals))


def seen_keys(block):
    key_ids = lax.broadcasted_iota(jnp.int32, (block, block), 0)
    return key_ids <= lax.broadcasted_iota(jnp.int32, (block, block), 1)


def attend_kernel(head_dim, block, qkv_ref, cos_ref, low_ref, up_ref, rot_ref, attn_ref, lse_ref):
    length = qkv_ref.shape[0]
    scale = 1.0 / math.sqrt(head_dim)
    tables = (cos_ref[...], low_ref[...], up_ref[...])
    rot_ref[:, :LANES] = turn(qkv_ref[:, :LANES], *tables).astype(BF) * BF(scale)
    rot_ref[:, LANES : 2 * LANES] = turn(qkv_ref[:, LANES : 2 * LANES], *tables).astype(BF)
    rot_ref[:, 2 * LANES :] = qkv_ref[:, 2 * LANES :].astype(BF)
    heads = LANES // head_dim
    seen = seen_keys(block)
    for first in range(0, length, block):
        last = first + block
        total = jnp.zeros((block, LANES), F32)
        for head in range(heads):
            query_block = head_lanes(rot_ref[first:last, :LANES], head, head_dim)
            scores = jnp.where(seen, dot_cols(rot_ref[first:last, LANES : 2 * LANES], query_block), mask_fill)
            col_max = jnp.max(scores, axis=0, keepdims=True)
            if first:
                before = dot_cols(rot_ref[:first, LANES : 2 * LANES], query_block)
                col_max = jnp.maximum(col_max, jnp.max(before, axis=0, keepdims=True))
            probs = jnp.exp(scores - col_max)
            denom = jnp.sum(probs, axis=0, keepdims=True)
            part = dot_rows(probs.astype(BF), head_lanes(rot_ref[first:last, 2 * LANES :], head, head_dim))
            if first:
                probs = jnp.exp(before - col_max)
                denom += jnp.sum(probs, axis=0, keepdims=True)
                part += dot_rows(probs.astype(BF), head_lanes(rot_ref[:first, 2 * LANES :], head, head_dim))
            total += part * jnp.broadcast_to(1.0 / denom, (LANES, block)).T
            lse_ref[0, head : head + 1, first:last] = col_max + jnp.log(denom)
        attn_ref[first:last, :] = total.astype(BF)


def attend_back_kernel(head_dim, block, rot_ref, grad_ref, attn_ref, lse_ref, cos_ref, low_ref, up_ref, out_ref, sum_ref, key_acc, value_acc):
    length = rot_ref.shape[0]
    scale = 1.0 / math.sqrt(head_dim)
    heads = LANES // head_dim
    seen = seen_keys(block)

    def back(vals, span):
        return turn(vals, cos_ref[span, :], -low_ref[span, :], -up_ref[span, :])

    query_sum = jnp.zeros((1, LANES), F32)
    key_acc[...] = jnp.zeros_like(key_acc)
    value_acc[...] = jnp.zeros_like(value_acc)
    for first in range(0, length, block):
        last = first + block
        total = jnp.zeros((block, LANES), F32)
        inner = (grad_ref[first:last, :].astype(F32) * attn_ref[first:last, :].astype(F32)).T
        for head in range(heads):
            query_block = head_lanes(rot_ref[first:last, :LANES], head, head_dim)
            grad_block = head_lanes(grad_ref[first:last, :], head, head_dim)
            lse = lse_ref[0, head : head + 1, first:last]
            inner_sum = jnp.sum(inner[head * head_dim : (head + 1) * head_dim], axis=0, keepdims=True)
            for start, stop in ((0, first), (first, last)):
                if start == stop:
                    continue
                keys = rot_ref[start:stop, LANES : 2 * LANES]
                probs = jnp.exp(dot_cols(keys, query_block) - lse)
                if start == first:
                    probs = jnp.where(seen, probs, 0.0)
                value_acc[start:stop, :] += dot_plain(probs.astype(BF), grad_block)
                prob_grad = dot_cols(rot_ref[start:stop, 2 * LANES :], grad_block)
                score_grad = (probs * (prob_grad - inner_sum)).astype(BF)
                total += dot_rows(score_grad, head_lanes(keys, head, head_dim))
                key_acc[start:stop, :] += dot_plain(score_grad, query_block)
        turned = back(total * scale, slice(first, last))
        query_sum += jnp.sum(turned, axis=0, keepdims=True)
        out_ref[first:last, :LANES] = turned.astype(BF)
    turned = back(key_acc[...], slice(0, length))
    out_ref[:, LANES : 2 * LANES] = turned.astype(BF)
    out_ref[:, 2 * LANES :] = value_acc[...].astype(BF)
    sum_ref[0:1, :LANES] = query_sum
    sum_ref[0:1, LANES : 2 * LANES] = jnp.sum(turned, axis=0, keepdims=True)
    sum_ref[0:1, 2 * LANES :] = jnp.sum(value_acc[...], axis=0, keepdims=True)


def attention_cost(seqs, pairs, length, matmuls):
    flops = seqs * pairs * matmuls * 2 * 2 * length * length * LANES
    return estimate(flops, seqs * pairs * length * LANES * 16)


def attend(qkv, tables, length, head_dim):
    tokens, width = qkv.shape
    seqs, pairs = tokens // length, width // (3 * LANES)
    heads = LANES // head_dim
    block = min(512, length)
    table_spec = pl.BlockSpec((length, LANES), lambda s, h: (0, 0))
    return pl.pallas_call(
        functools.partial(attend_kernel, head_dim, block),
        grid=(seqs, pairs),
        in_specs=[pl.BlockSpec((length, 3 * LANES), lambda s, h: (s, h))] + [table_spec] * 3,
        out_specs=[
            pl.BlockSpec((length, 3 * LANES), lambda s, h: (s, h)),
            pl.BlockSpec((length, LANES), lambda s, h: (s, h)),
            pl.BlockSpec((1, heads, length), lambda s, h: (s * pairs + h, 0, 0)),
        ],
        out_shape=[
            jax.ShapeDtypeStruct((tokens, width), BF),
            jax.ShapeDtypeStruct((tokens, pairs * LANES), BF),
            jax.ShapeDtypeStruct((seqs * pairs, heads, length), F32),
        ],
        compiler_params=pltpu.CompilerParams(vmem_limit_bytes=VMEM_LIMIT),
        cost_estimate=attention_cost(seqs, pairs, length, 3),
    )(qkv, *tables)


def attend_back(rot, attn_grad, attn, lse, tables, length, head_dim):
    tokens, width = rot.shape
    seqs, pairs = tokens // length, width // (3 * LANES)
    heads = LANES // head_dim
    block = min(512, length)
    table_spec = pl.BlockSpec((length, LANES), lambda s, h: (0, 0))
    return pl.pallas_call(
        functools.partial(attend_back_kernel, head_dim, block),
        grid=(seqs, pairs),
        in_specs=[
            pl.BlockSpec((length, 3 * LANES), lambda s, h: (s, h)),
            pl.BlockSpec((length, LANES), lambda s, h: (s, h)),
            pl.BlockSpec((length, LANES), lambda s, h: (s, h)),
            pl.BlockSpec((1, heads, length), lambda s, h: (s * pairs + h, 0, 0)),
        ]
        + [table_spec] * 3,
        out_specs=[
            pl.BlockSpec((length, 3 * LANES), lambda s, h: (s, h)),
            pl.BlockSpec((8, 3 * LANES), lambda s, h: (s, h)),
        ],
        out_shape=[jax.ShapeDtypeStruct((tokens, width), BF), jax.ShapeDtypeStruct((8 * seqs, width), F32)],
        scratch_shapes=[pltpu.VMEM((length, LANES), F32), pltpu.VMEM((length, LANES), F32)],
        compiler_params=pltpu.CompilerParams(vmem_limit_bytes=VMEM_LIMIT),
        cost_estimate=attention_cost(seqs, pairs, length, 6),
    )(rot, attn_grad, attn, lse, *tables)


def spec_rows(tile, width):
    return pl.BlockSpec((tile, width), lambda i, s: (i, 0))


def spec_whole(array):
    return pl.BlockSpec(array.shape, lambda i, s: (0,) * array.ndim)


def estimate(flops, moved):
    return pl.CostEstimate(flops=int(flops) // 64, bytes_accessed=int(moved) // 64, transcendentals=0)


def lined_dot(slots_ref, rows_ref, parts, cols):
    depth = parts[0].shape[0]
    total = None
    for at, part in enumerate(parts):
        first = pl.multiple_of(slots_ref[at] * depth, depth)
        piece = dot_plain(rows_ref[:, pl.ds(first, depth)], part[:, cols])
        total = piece if total is None else total + piece
    return total


def rows_call(kernel, slots, ins, in_specs, outs, tile, cost, out_specs=None, steps=None):
    return pl.pallas_call(
        kernel,
        grid_spec=pltpu.PrefetchScalarGridSpec(
            num_scalar_prefetch=1,
            grid=(steps or outs[0].shape[0] // tile,),
            in_specs=in_specs,
            out_specs=out_specs or [spec_rows(tile, out.shape[1]) for out in outs],
        ),
        out_shape=outs,
        compiler_params=pltpu.CompilerParams(vmem_limit_bytes=VMEM_LIMIT),
        cost_estimate=cost,
    )(slots, *ins)


def normalise(rows):
    micros, tokens, width = rows.shape

    def kernel(rows_ref, out_ref):
        vals = rows_ref[0].astype(F32)
        mean = jnp.mean(vals, axis=-1, keepdims=True)
        centred = vals - mean
        var = jnp.mean(centred * centred, axis=-1, keepdims=True)
        out_ref[...] = (centred * lax.rsqrt(var + norm_epsilon)).astype(BF)

    def one(micro):
        return pl.pallas_call(
            kernel,
            grid=(2,),
            in_specs=[pl.BlockSpec((1, tokens // 2, width), lambda i: (micro, i, 0))],
            out_specs=pl.BlockSpec((tokens // 2, width), lambda i: (i, 0)),
            out_shape=jax.ShapeDtypeStruct((tokens, width), BF),
            compiler_params=pltpu.CompilerParams(vmem_limit_bytes=VMEM_LIMIT),
            cost_estimate=estimate(10 * tokens * width, 4 * tokens * width),
        )(rows)

    return [one(micro) for micro in range(micros)]


def norm_qkv(slots, rows, gain, shift, parts, bias):
    tokens, width = rows.shape
    cols, tile = bias.shape[1], 512

    def kernel(slots_ref, rows_ref, gain_ref, shift_ref, bias_ref, *refs):
        parts, (normed_ref, qkv_ref) = refs[:-2], refs[-2:]
        normed_ref[...] = (rows_ref[...].astype(F32) * gain_ref[...] + shift_ref[...]).astype(BF)
        qkv_ref[...] = lined_dot(slots_ref, normed_ref, parts, slice(0, cols)) + bias_ref[...]

    return rows_call(
        kernel,
        slots,
        [rows, gain, shift, bias, *parts],
        [spec_rows(tile, width)] + [spec_whole(array) for array in (gain, shift, bias, *parts)],
        [jax.ShapeDtypeStruct((tokens, width), BF), jax.ShapeDtypeStruct((tokens, cols), F32)],
        tile,
        estimate(2 * tokens * width * cols, tokens * (4 * width + 4 * cols)),
    )


def micro_spec(micro, steps, tile, width):
    return pl.BlockSpec((tile, width), lambda i, s: (jnp.clip(i - micro * steps, 0, steps - 1), 0))


def up_act(slots, rows, parts, bias):
    count = len(rows)
    tokens, width = rows[0].shape
    cols, tile, chunk = bias.shape[1], 512, 512
    steps = tokens // tile

    def kernel(slots_ref, bias_ref, *refs):
        ins, parts, outs = refs[:count], refs[count : -2 * count], refs[-2 * count :]
        for micro in range(count):

            @pl.when(pl.program_id(0) // steps == micro)
            def _():
                for at in range(0, cols, chunk):
                    span = slice(at, at + chunk)
                    pre = lined_dot(slots_ref, ins[micro], parts, span) + bias_ref[:, span]
                    square = pre * pre
                    tanh = jnp.tanh(pre * (gelu_factor + (gelu_factor * 0.044715) * square))
                    half = 0.5 + 0.5 * tanh
                    act = pre * half
                    outs[micro][:, span] = act.astype(BF)
                    inner = 2 * gelu_factor + (6 * 0.044715 * gelu_factor) * square
                    outs[count + micro][:, span] = (half + (act - act * half) * inner).astype(BF)

    outs = rows_call(
        kernel,
        slots,
        [bias, *rows, *parts],
        [spec_whole(bias)]
        + [micro_spec(m, steps, tile, width) for m in range(count)]
        + [spec_whole(part) for part in parts],
        [jax.ShapeDtypeStruct((tokens, cols), BF)] * (2 * count),
        tile,
        estimate(2 * count * tokens * width * cols, count * tokens * (2 * width + 4 * cols)),
        [micro_spec(m, steps, tile, cols) for m in range(count)] * 2,
        count * steps,
    )
    return outs[:count], outs[count:]


def pre_grad_rows(slots, rows, parts, slopes):
    count = len(rows)
    tokens, width = rows[0].shape
    cols, tile = slopes[0].shape[1], 512
    steps = tokens // tile

    def kernel(slots_ref, *refs):
        ins, slopes, parts = refs[:count], refs[count : 2 * count], refs[2 * count : -count - 1]
        outs, sum_ref = refs[-count - 1 : -1], refs[-1]

        @pl.when(pl.program_id(0) == 0)
        def _():
            sum_ref[...] = jnp.zeros_like(sum_ref)

        for micro in range(count):

            @pl.when(pl.program_id(0) // steps == micro)
            def _():
                act_grad = lined_dot(slots_ref, ins[micro], parts, slice(0, cols))
                grad = act_grad * slopes[micro][...].astype(F32)
                outs[micro][...] = grad.astype(BF)
                sum_ref[0:1, :] += jnp.sum(grad, axis=0, keepdims=True)

    return rows_call(
        kernel,
        slots,
        [*rows, *slopes, *parts],
        [micro_spec(m, steps, tile, width) for m in range(count)]
        + [micro_spec(m, steps, tile, cols) for m in range(count)]
        + [spec_whole(part) for part in parts],
        [jax.ShapeDtypeStruct((tokens, cols), BF)] * count + [jax.ShapeDtypeStruct((8, cols), F32)],
        tile,
        estimate(2 * count * tokens * width * cols, count * tokens * (2 * width + 4 * cols)),
        [micro_spec(m, steps, tile, cols) for m in range(count)] + [pl.BlockSpec((8, cols), lambda i, s: (0, 0))],
        count * steps,
    )


def head_grad_rows(slots, rows, parts, first):
    tokens, width = rows.shape
    cols, tile = parts[0].shape[1] - first, 1024

    def kernel(slots_ref, rows_ref, *refs):
        parts, out_ref = refs[:-1], refs[-1]
        out_ref[...] = lined_dot(slots_ref, rows_ref, parts, slice(first, first + cols)).astype(BF)

    return rows_call(
        kernel,
        slots,
        [rows, *parts],
        [spec_rows(tile, width)] + [spec_whole(part) for part in parts],
        [jax.ShapeDtypeStruct((tokens, cols), BF)],
        tile,
        estimate(2 * tokens * width * cols, tokens * (2 * width + 2 * cols)),
    )[0]


def branch_rows(slots, ones, one_parts, first, twos, two_parts, block):
    micros = len(ones)
    tokens, cols = ones[0].shape
    count, depth = len(one_parts), one_parts[0].shape[0]
    held = 2
    tile = held * block
    width, steps = count * depth, tokens // tile

    def kernel(slots_ref, *refs):
        ones, twos, out_ref = refs[:micros], refs[micros : 2 * micros], refs[-1]
        parts = refs[2 * micros : -1]
        for micro in range(micros):

            @pl.when(pl.program_id(0) // steps == micro)
            def _():
                for at in range(count):
                    where = pl.multiple_of(slots_ref[at] * depth, depth)
                    total = dot_cols(ones[micro][...], parts[at][:, first : first + cols])
                    total += dot_cols(twos[micro][...], parts[count + at][...])
                    out_ref[:, 0, :, pl.ds(where, depth)] = total.astype(BF).reshape(held, block, depth)

    return rows_call(
        kernel,
        slots,
        [*ones, *twos, *one_parts, *two_parts],
        [micro_spec(m, steps, tile, cols) for m in range(micros)]
        + [micro_spec(m, steps, tile, twos[0].shape[1]) for m in range(micros)]
        + [spec_whole(part) for part in (*one_parts, *two_parts)],
        [jax.ShapeDtypeStruct((tokens // block, micros, block, width), BF)],
        tile,
        estimate(2 * micros * tokens * width * (cols + twos[0].shape[1]), 2 * micros * tokens * (width + cols)),
        [pl.BlockSpec((held, 1, block, width), lambda i, s: (lax.rem(i, steps), i // steps, 0, 0))],
        micros * steps,
    )[0]


def normed_grad_rows(slots, one, one_parts, two, two_parts, rows, block, split):
    tokens, cols = one.shape
    count, depth = len(one_parts), one_parts[0].shape[0]
    tile = 2 * block
    width = count * depth

    def kernel(slots_ref, one_ref, two_ref, rows_ref, *refs):
        outs, sum_ref = refs[2 * count : -1], refs[-1]

        @pl.when(pl.program_id(0) == 0)
        def _():
            sum_ref[...] = jnp.zeros_like(sum_ref)

        for at in range(count):
            where = pl.multiple_of(slots_ref[at] * depth, depth)
            span = pl.ds(where, depth)
            total = dot_cols(one_ref[...], refs[at][:, :cols])
            total += dot_cols(two_ref[...], refs[count + at][...])
            if split:
                first = slots_ref[count] == 0
                outs[0][:, span] = jnp.where(first, total[:block], total[block:]).astype(BF)
                outs[1][:, span] = jnp.where(first, total[block:], total[:block]).astype(BF)
            else:
                outs[0][:, span] = total.astype(BF)
            sum_ref[0:1, span] += jnp.sum(total * rows_ref[:, span].astype(F32), axis=0, keepdims=True)
            sum_ref[1:2, span] += jnp.sum(total, axis=0, keepdims=True)

    pieces = 2 if split else 1
    return rows_call(
        kernel,
        slots,
        [one, two, rows, *one_parts, *two_parts],
        [spec_rows(tile, cols), spec_rows(tile, two.shape[1]), spec_rows(tile, width)]
        + [spec_whole(part) for part in (*one_parts, *two_parts)],
        [jax.ShapeDtypeStruct((tokens // pieces, width), BF)] * pieces + [jax.ShapeDtypeStruct((8, width), F32)],
        tile,
        estimate(2 * tokens * width * (cols + two.shape[1]), 2 * tokens * (2 * width + cols + two.shape[1])),
        [spec_rows(tile // pieces, width)] * pieces + [pl.BlockSpec((8, width), lambda i, s: (0, 0))],
        tokens // tile,
    )


def norm_back(rows, cots, pieces, gain, micro, earlier=None):
    micros, tokens, width = rows.shape
    tile = tokens // 4

    def kernel(rows_ref, cot_ref, gain_ref, *refs):
        vals = rows_ref[0].astype(F32)
        mean = jnp.mean(vals, axis=-1, keepdims=True)
        centred = vals - mean
        scale = lax.rsqrt(jnp.mean(centred * centred, axis=-1, keepdims=True) + norm_epsilon)
        scaled = centred * scale
        grad = refs[0][...].astype(F32)
        for ref in refs[1 : len(pieces)]:
            grad += ref[...].astype(F32)
        grad *= gain_ref[...]
        inner = jnp.mean(grad * scaled, axis=-1, keepdims=True)
        grad = (grad - jnp.mean(grad, axis=-1, keepdims=True) - scaled * inner) * scale
        refs[-1][0] = (cot_ref[0].astype(F32) + grad).astype(BF)

    at_micro = pl.BlockSpec((1, tile, width), lambda i: (micro, i, 0))
    given = [] if earlier is None else [earlier]
    return pl.pallas_call(
        kernel,
        grid=(tokens // tile,),
        in_specs=[at_micro, at_micro, pl.BlockSpec((1, width), lambda i: (0, 0))]
        + [pl.BlockSpec((tile, width), lambda i: (i, 0))] * len(pieces)
        + [pl.BlockSpec(memory_space=pl.ANY)] * len(given),
        out_specs=at_micro,
        out_shape=jax.ShapeDtypeStruct(rows.shape, BF),
        input_output_aliases={3 + len(pieces): 0} if given else {},
        compiler_params=pltpu.CompilerParams(vmem_limit_bytes=VMEM_LIMIT),
        cost_estimate=estimate(20 * tokens * width, 10 * tokens * width),
    )(rows, cots, gain, *pieces, *given)


def weight_grad(lefts, rights):
    tile, chunk = 512, 512
    micro_count = len(lefts)
    tokens, width = lefts[0].shape
    widths = [right[0].shape[1] for right in rights]
    cols, steps = sum(widths), tokens // tile

    def kernel(*refs):
        out_ref, acc_ref = refs[-2:]
        step = pl.program_id(0)

        @pl.when(step == 0)
        def _():
            acc_ref[...] = jnp.zeros_like(acc_ref)

        for micro in range(micro_count):

            @pl.when(step // steps == micro)
            def _():
                first = 0
                for at, span in enumerate(widths):
                    right = refs[(1 + at) * micro_count + micro]
                    for row in range(0, width, chunk):
                        acc_ref[row : row + chunk, first : first + span] += dot_rows(
                            refs[micro][:, row : row + chunk], right[...]
                        )
                    first += span

        @pl.when(step == micro_count * steps - 1)
        def _():
            out_ref[...] = acc_ref[...].astype(BF)

    def side(micro, span):
        return pl.BlockSpec((tile, span), lambda i: (jnp.clip(i - micro * steps, 0, steps - 1), 0))

    return pl.pallas_call(
        kernel,
        grid=(micro_count * steps,),
        in_specs=[side(micro, span) for span in (width, *widths) for micro in range(micro_count)],
        out_specs=pl.BlockSpec((width, cols), lambda i: (0, 0)),
        out_shape=jax.ShapeDtypeStruct((width, cols), BF),
        scratch_shapes=[pltpu.VMEM((width, cols), F32)],
        compiler_params=pltpu.CompilerParams(vmem_limit_bytes=VMEM_LIMIT),
        cost_estimate=estimate(
            2 * micro_count * tokens * width * cols, 2 * micro_count * tokens * (width + cols)
        ),
    )(*lefts, *(array for right in rights for array in right))


def shards(
    inputs,
    ln_gain,
    ln_bias,
    qkv_weight,
    qkv_bias,
    out_weight,
    out_bias,
    up_weight,
    up_bias,
    down_weight,
    down_bias,
    cotangent,
):
    micro_count, _, token_rows, model_width = inputs.shape
    fsdp_size, tp_size = lax.axis_size("fsdp"), lax.axis_size("tp")
    line = fsdp_size // 2
    fsdp_at, tp_at = lax.axis_index("fsdp"), lax.axis_index("tp")
    line_at, pair_at = fsdp_at >> 1, fsdp_at & 1
    plane_size = 2 * tp_size
    planes = [[plane * plane_size + i for i in range(plane_size)] for plane in range(line)]
    ring = [(f, ((f // 2 + 1) % line) * 2 + f % 2) for f in range(fsdp_size)]
    length = token_rows * tp_size
    head_dim = qkv_bias.shape[2] * fsdp_size
    shard_rows = model_width // fsdp_size
    line_rows = 2 * shard_rows
    attn_cols = out_weight.shape[0] // 2
    qkv_cols = 3 * attn_cols
    pairs = attn_cols // LANES
    mlp_cols = up_weight.shape[1] // 2
    both_axes = ("fsdp", "tp")

    def swap_pair(vals):
        return lax.ppermute(vals, "fsdp", [(f, f ^ 1) for f in range(fsdp_size)])

    def gather_plane(vals):
        return lax.all_gather(vals, both_axes, axis=0, tiled=True, axis_index_groups=planes)

    def scatter_plane(vals):
        return lax.psum_scatter(vals, both_axes, scatter_dimension=0, tiled=True, axis_index_groups=planes)

    def doubled(cur, axis, size, at, bit):
        other = lax.ppermute(cur, axis, [(i, i ^ bit) for i in range(size)])
        upper = (at & bit) != 0
        return jnp.where(upper, jnp.concatenate([other, cur]), jnp.concatenate([cur, other]))

    def attn_half(half):
        qkv_part = lax.dynamic_slice_in_dim(qkv_weight, half * attn_cols, attn_cols, axis=2)
        qkv_part = qkv_part.reshape(shard_rows, 3, pairs, LANES).transpose(0, 2, 1, 3)
        out_part = lax.dynamic_slice_in_dim(out_weight, half * attn_cols, attn_cols, axis=0)
        return jnp.concatenate([qkv_part.reshape(shard_rows, qkv_cols), out_part.T], axis=1)

    def up_half(half):
        return lax.dynamic_slice_in_dim(up_weight, half * mlp_cols, mlp_cols, axis=1)

    def down_half(half):
        return lax.dynamic_slice_in_dim(down_weight, half * mlp_cols, mlp_cols, axis=0).T

    def pair_join(own, other):
        return jnp.where(pair_at == 0, jnp.concatenate([own, other]), jnp.concatenate([other, own]))

    class Box:
        def __init__(self, val):
            self.val = val

    class Line:
        tokens = []

        def tie(self, *boxes):
            held = []
            for box in (*boxes, *self.tokens):
                if box not in held:
                    held.append(box)
            if len(held) > 1:
                for box, val in zip(held, lax.optimization_barrier(tuple(box.val for box in held))):
                    box.val = val

        def run(self, piece, *boxes):
            self.tie(*boxes)
            results = [Box(val) for val in piece(*(box.val for box in boxes))]
            self.tokens = [results[0]]
            return results

        def sync(self, box):
            self.tokens = self.tokens + [box]

    order = Line()

    class Gather:
        def __init__(self, shard):
            self.parts = [shard]

        def move(self):
            if len(self.parts) < line:
                order.tie(self.parts[-1])
                self.parts.append(Box(lax.ppermute(self.parts[-1].val, "fsdp", ring)))

        def sync(self):
            order.sync(self.parts[-1])

        def finish(self):
            while len(self.parts) < line:
                self.move()
            self.sync()

        def vals(self):
            return [part.val for part in self.parts]

    class Scatter:
        def __init__(self, part):
            self.part, self.step, self.came = part, 1, None

        def total(self):
            at_line = lax.rem(line_at + line - self.step, line)
            own = lax.dynamic_slice_in_dim(self.part.val, at_line * line_rows, line_rows, axis=0)
            if self.came is None:
                return own
            order.tie(self.came)
            return self.came.val.astype(F32) + own.astype(F32)

        def move(self):
            if self.step < line:
                sent = Box(self.total().astype(BF))
                if self.came is None:
                    order.tie(sent)
                self.came = Box(lax.ppermute(sent.val, "fsdp", ring))
                self.step += 1

        def sync(self):
            order.sync(self.came)

        def rows_at(self, half):
            own = lax.dynamic_slice_in_dim(
                self.part.val, line_at * line_rows + half * shard_rows, shard_rows, axis=0
            )
            came = lax.dynamic_slice_in_dim(self.came.val, half * shard_rows, shard_rows, axis=0)
            return came.astype(F32) + own.astype(F32)

        def swap(self):
            while self.step < line:
                self.move()
            order.tie(self.came)
            self.sent = Box(self.rows_at(1 - pair_at).astype(BF))
            self.got = Box(swap_pair(self.sent.val))

        def halves(self):
            order.tie(self.came)
            keep, got = self.rows_at(pair_at), self.got.val.astype(F32)
            return jnp.where(pair_at == 0, keep, got), jnp.where(pair_at == 0, got, keep)

    class SmallSum:
        def __init__(self, everywhere, over_fsdp):
            self.cur, self.rest = Box(everywhere), over_fsdp
            self.size = everywhere.shape[0]
            bits = [("tp", tp_size, bit) for bit in range(tp_size.bit_length() - 1)]
            self.steps = bits + [("fsdp", fsdp_size, 0), ("line", 0, 0)]

        def move(self):
            if self.steps:
                axis, size, bit = self.steps.pop(0)
                if axis == "fsdp":
                    self.cur = Box(jnp.concatenate([self.cur.val, self.rest]))
                order.tie(self.cur)
                if axis == "line":
                    others = along_line(self.cur.val)
                else:
                    others = [lax.ppermute(self.cur.val, axis, [(i, i ^ (1 << bit)) for i in range(size)])]
                self.cur = Box(sum(others, self.cur.val))

        def split(self):
            while self.steps:
                self.move()
            return self.cur.val[: self.size], self.cur.val[self.size :]

    plain = normalise(inputs[:, 0])
    cots = [cotangent[m].reshape(token_rows, model_width) for m in range(micro_count)]
    micros = range(micro_count)
    plane_rows, plane_cots = [None] * micro_count, [None] * micro_count

    def gather_behind(rows):
        sent = Box(rows)
        order.tie(sent)
        return Box(gather_plane(sent.val))

    small = jnp.concatenate(
        [vec.reshape(-1) for vec in (ln_gain, ln_bias, out_bias, down_bias, qkv_bias, up_bias)]
    )
    attn_send = Box(attn_half(1 - pair_at))
    order.tokens = [attn_send]
    plane_rows[0] = gather_behind(plain[0])
    attn_shard = Box(pair_join(attn_half(pair_at), swap_pair(attn_send.val)))
    small_all = Box(small[None])
    order.tokens = [attn_shard]
    order.tie(small_all)
    small_all = small_all.val
    for bit in range(tp_size.bit_length() - 1):
        small_all = doubled(small_all, "tp", tp_size, tp_at, 1 << bit)
    small_near = small_all

    def along_line(vals):
        return [lax.ppermute(vals, "fsdp", [(f, f ^ (far << 1)) for f in range(fsdp_size)]) for far in range(1, line)]

    def small_step(small_all, step):
        order.tie(small_all)
        if step == 0:
            return Box(doubled(small_all.val, "fsdp", fsdp_size, fsdp_at, 1))
        held = [small_all.val] + along_line(small_all.val)
        for bit in range(line.bit_length() - 1):
            other = (line_at & (1 << bit)) != 0
            held = [jnp.where(other, held[i ^ (1 << bit)], held[i]) for i in range(line)]
        return Box(jnp.concatenate(held))

    small_all = Box(small_near)
    attn_ring = Gather(attn_shard)
    attn_ring.move()
    plane_rows[1] = gather_behind(plain[1])
    order.sync(small_all)
    small_all = small_step(small_all, 0)
    bias_total = Box(sum(jnp.sum(cots[m].astype(F32), axis=0) for m in micros))
    up_send = Box(up_half(1 - pair_at))
    order.tie(up_send)
    up_got = Box(swap_pair(up_send.val))
    attn_ring.sync()
    order.sync(small_all)
    attn_ring.move()
    order.sync(bias_total)
    small_all = small_step(small_all, 1)
    down_send = Box(down_half(1 - pair_at))
    order.tie(down_send, up_got)
    down_got = Box(swap_pair(down_send.val))
    up_shard = Box(pair_join(up_half(pair_at), up_got.val))
    attn_ring.sync()
    order.sync(small_all)
    attn_ring.move()
    plane_cots[0] = gather_behind(cots[0])
    order.sync(up_shard)
    order.tie(small_all)
    small_all = small_all.val
    vec_size = ln_gain.shape[0]
    gain_vec, shift_vec, bias_out, bias_down = (
        small_all[:, i * vec_size : (i + 1) * vec_size].reshape(-1).astype(F32) for i in range(4)
    )
    bias_both = bias_out + bias_down
    mine = lax.dynamic_slice_in_dim(
        small_all.reshape(fsdp_size, tp_size, -1), tp_at, 1, axis=1
    )[:, 0].astype(F32)
    at = 4 * vec_size
    qkv_b = mine[:, at : at + qkv_bias.size].reshape(fsdp_size, 3, 2, pairs, -1, qkv_bias.shape[2])
    qkv_b = lax.dynamic_slice_in_dim(qkv_b, pair_at, 1, axis=2)[:, :, 0]
    qkv_b = qkv_b.transpose(2, 1, 3, 0, 4).reshape(1, qkv_cols)
    at += qkv_bias.size
    up_b = mine[:, at:].reshape(fsdp_size, up_bias.shape[0], up_bias.shape[1])
    up_b = up_b.transpose(1, 0, 2).reshape(2, mlp_cols)
    up_b = lax.dynamic_slice_in_dim(up_b, pair_at, 1, axis=0)

    slots = [lax.rem(line_at + line - step, line) for step in range(line)]
    slots = jnp.stack(slots + [tp_at & 1]).astype(jnp.int32)
    tables = rotary_tables(length, head_dim, ROT)
    prepared = [Box(val) for val in (gain_vec[None], shift_vec[None], qkv_b, up_b, slots, *tables)]
    for box in prepared:
        order.sync(box)
    order.tie(down_got)
    down_shard = Box(pair_join(down_half(pair_at), down_got.val))
    order.tokens = [down_shard]
    attn_ring.finish()
    order.tie(up_shard, *prepared)
    gain_row, shift_row, qkv_b, up_b, slots, *tables = (box.val for box in prepared)
    normed, qkvs, rots, attns, lses, acts, slopes = ([None] * micro_count for _ in range(7))
    pre_grads, qkv_grads, qkv_sums, sums, attn_heads = ([None] * micro_count for _ in range(5))

    def norm_piece(m):
        normed[m], qkvs[m] = order.run(
            lambda rows: norm_qkv(slots, rows, gain_row, shift_row, attn_ring.vals(), qkv_b), plane_rows[m]
        )

    def attend_piece(m):
        rots[m], attns[m], lses[m] = order.run(
            lambda vals: attend(vals, tables, length, head_dim), qkvs[m]
        )

    def up_piece():
        def piece(*rows):
            return [val for vals in up_act(slots, rows, up_ring.vals(), up_b) for val in vals]

        results = order.run(piece, *normed)
        acts[:], slopes[:] = results[:micro_count], results[micro_count:]

    def head_grad_piece(m):
        (attn_heads[m],) = order.run(
            lambda cot: [head_grad_rows(slots, cot, attn_ring.vals(), qkv_cols)], plane_cots[m]
        )

    def attend_back_piece(m):
        qkv_grads[m], qkv_sums[m] = order.run(
            lambda rot, grad, attn, lse: attend_back(rot, grad, attn, lse, tables, length, head_dim),
            rots[m],
            attn_heads[m],
            attns[m],
            lses[m],
        )

    def pre_grad_piece():
        def piece(*vals):
            return pre_grad_rows(slots, vals[:micro_count], down_ring.vals(), vals[micro_count:])

        *pre_grads[:], up_sums = order.run(piece, *plane_cots, *slopes)
        return up_sums

    def weight_piece(lefts, *rights):
        def piece(*flat):
            sets = [flat[at : at + micro_count] for at in range(0, len(flat), micro_count)]
            return [weight_grad(sets[0], sets[1:])]

        return Scatter(order.run(piece, *lefts, *(box for right in rights for box in right))[0])

    def branch_piece():
        def piece(*vals):
            rows = branch_rows(
                slots,
                vals[:micro_count],
                attn_ring.vals(),
                qkv_cols,
                vals[micro_count:],
                down_ring.vals(),
                token_rows,
            )
            return [rows.reshape(-1, model_width)]

        return order.run(piece, *attns, *acts)[0]

    def normed_grad_piece(m, split=False):
        *back, sums[m] = order.run(
            lambda one, two, rows: normed_grad_rows(
                slots, one, attn_ring.vals(), two, up_ring.vals(), rows, token_rows, split
            ),
            qkv_grads[m],
            pre_grads[m],
            plane_rows[m],
        )
        return back

    def scatter_behind(box):
        order.tie(box)
        return Box(scatter_plane(box.val))

    up_ring, down_ring = Gather(up_shard), Gather(down_shard)
    order.sync(down_shard)
    up_ring.move()
    norm_piece(0)
    up_ring.sync()
    plane_cots[1] = gather_behind(cots[1])
    up_ring.move()
    attend_piece(0)
    norm_piece(1)
    up_ring.sync()
    up_ring.move()
    attend_piece(1)
    up_ring.finish()
    down_ring.move()
    up_piece()
    down_ring.sync()
    down_ring.move()
    head_grad_piece(0)
    attend_back_piece(0)
    down_ring.sync()
    down_ring.move()

    down_scatter = weight_piece(plane_cots, acts, attns)
    down_ring.finish()
    down_scatter.move()
    branch = branch_piece()
    down_scatter.sync()
    branch_sum = scatter_behind(branch)
    down_scatter.move()
    up_sums = pre_grad_piece()
    down_scatter.sync()
    down_scatter.move()
    up_scatter = weight_piece(normed, pre_grads)
    down_scatter.sync()
    down_scatter.swap()
    up_scatter.move()
    head_grad_piece(1)
    attend_back_piece(1)
    up_scatter.sync()
    order.sync(down_scatter.got)
    up_scatter.move()
    (back,) = normed_grad_piece(0)
    up_scatter.sync()
    back_sum = scatter_behind(back)
    up_scatter.move()
    qkv_scatter = weight_piece(normed, qkv_grads)
    up_scatter.sync()
    order.sync(branch_sum)
    up_scatter.swap()
    qkv_scatter.move()
    keep, give = normed_grad_piece(1, True)

    def swap_core(vals):
        return lax.ppermute(vals, "tp", [(t, t ^ 1) for t in range(tp_size)])

    def swap_y(vals):
        return lax.ppermute(vals, "tp", [(t, t ^ 2) for t in range(tp_size)])

    y_at, half = tp_at >> 1, model_width // 2
    up_b_grad = up_sums.val[0]
    qkv_b_grad = sum(jnp.sum(part.val.reshape(-1, 8, qkv_cols)[:, 0], axis=0) for part in qkv_sums)
    qkv_b_grad = qkv_b_grad.reshape(pairs, 3, -1).transpose(1, 0, 2).reshape(3, attn_cols)

    def in_half(vals):
        blank = jnp.zeros_like(vals)
        return jnp.where(
            pair_at == 0, jnp.concatenate([vals, blank], axis=-1), jnp.concatenate([blank, vals], axis=-1)
        )

    gain_total, shift_total = (sum(part.val[i] for part in sums) for i in range(2))
    tail = SmallSum(
        jnp.concatenate([gain_total, shift_total, bias_total.val]),
        jnp.concatenate([in_half(up_b_grad), in_half(qkv_b_grad).reshape(-1)]),
    )
    qkv_scatter.sync()
    order.sync(up_scatter.got)
    order.tie(give, tail.cur)
    tail.move()
    got = Box(swap_core(give.val))
    qkv_scatter.move()
    order.sync(tail.cur)
    order.tie(got)
    blocks = Box((got.val.astype(F32) + keep.val.astype(F32)).astype(BF).reshape(4, token_rows, model_width))
    tail.move()

    def block(pair, y):
        return lax.dynamic_index_in_dim(blocks.val, pair * 2 + y, 0, keepdims=False)

    order.sync(blocks)
    order.sync(tail.cur)
    order.tie(tail.cur)
    far = block(1 - pair_at, 1 - y_at)
    from_pair, from_y = Box(swap_pair(far[:, :half])), Box(swap_y(far[:, half:]))
    tail.move()
    row_major = Layout(major_to_minor=(0, 1))
    halves = [with_layout_constraint(part, row_major) for part in down_scatter.halves()]
    down_w_grad = jnp.concatenate([part[:, :mlp_cols].T for part in halves], axis=0)
    down_w_grad = Box(with_layout_constraint(down_w_grad, row_major))
    out_w_grad = jnp.concatenate([part[:, mlp_cols:].T for part in halves], axis=0)
    out_w_grad = Box(with_layout_constraint(out_w_grad, row_major))
    for box in (down_w_grad, out_w_grad):
        order.sync(box)

    qkv_scatter.sync()
    order.tie()
    qkv_scatter.move()
    order.tie(from_pair, from_y)
    for_y, for_pair = block(pair_at, 1 - y_at), block(1 - pair_at, y_at)
    for_y = jnp.concatenate(
        [(for_y[:, :half].astype(F32) + from_pair.val.astype(F32)).astype(BF), for_y[:, half:]], axis=1
    )
    for_pair = jnp.concatenate(
        [for_pair[:, :half], (for_pair[:, half:].astype(F32) + from_y.val.astype(F32)).astype(BF)], axis=1
    )
    for_pair, for_y = Box(for_pair), Box(for_y)
    from_pair, from_y = Box(swap_pair(for_pair.val)), Box(swap_y(for_y.val))
    own_block = Box(block(pair_at, y_at))
    for box in (for_pair, for_y, own_block):
        order.sync(box)
    order.tie(back_sum)
    gained = Box(norm_back(inputs[:, 0], cotangent[:, 0], [back_sum.val], gain_row, 0))
    order.sync(gained)
    qkv_scatter.sync()
    order.sync(tail.cur)
    order.tie(tail.cur)
    tail.move()
    qkv_scatter.swap()
    up_w_grad = Box(jnp.concatenate(up_scatter.halves(), axis=1))
    order.sync(up_w_grad)
    order.tie(from_pair, from_y)
    last_pieces = [own_block.val, from_pair.val, from_y.val]
    gained = Box(norm_back(inputs[:, 0], cotangent[:, 0], last_pieces, gain_row, 1, gained.val))
    order.tokens = [gained]
    order.tie(qkv_scatter.got, tail.cur)
    halves = qkv_scatter.halves()
    planes = [
        jnp.concatenate(
            [
                part[:, (pair * 3 + plane) * LANES : (pair * 3 + plane + 1) * LANES]
                for part in halves
                for pair in range(pairs)
            ],
            axis=1,
        )
        for plane in range(3)
    ]
    qkv_w_grad = jnp.stack(planes, axis=0).transpose(1, 0, 2)
    small_sums, bias_sums = tail.split()
    branch_sum = branch_sum.val.reshape(micro_count, token_rows, model_width)
    output = (inputs[:, 0].astype(F32) + branch_sum.astype(F32) + bias_both).astype(BF)

    small_sums = small_sums.reshape(3, fsdp_size * tp_size, vec_size)
    small_sums = lax.dynamic_slice_in_dim(small_sums, fsdp_at * tp_size + tp_at, 1, axis=1)[:, 0]
    gain_sum, shift_sum, bias_sum = small_sums[0], small_sums[1], small_sums[2]
    up_b_sum = bias_sums[: 2 * mlp_cols].reshape(up_bias.shape[0], -1)
    up_b_sum = lax.dynamic_slice_in_dim(up_b_sum, fsdp_at * up_bias.shape[1], up_bias.shape[1], axis=1)
    qkv_b_sum = bias_sums[2 * mlp_cols :].reshape(3, qkv_bias.shape[1], -1)
    qkv_b_sum = lax.dynamic_slice_in_dim(qkv_b_sum, fsdp_at * qkv_bias.shape[2], qkv_bias.shape[2], axis=2)

    return (
        output[:, None],
        gained.val[:, None],
        gain_sum,
        shift_sum,
        qkv_w_grad,
        qkv_b_sum,
        out_w_grad.val,
        bias_sum,
        up_w_grad.val,
        up_b_sum,
        down_w_grad.val,
        bias_sum,
    )


def solution(mesh):
    return jax.shard_map(
        shards,
        mesh=mesh,
        in_specs=(
            P(None, "fsdp", "tp", None),
            P(("fsdp", "tp")),
            P(("fsdp", "tp")),
            P("fsdp", None, "tp"),
            P(None, "tp", "fsdp"),
            P("tp", "fsdp"),
            P(("fsdp", "tp")),
            P("fsdp", "tp"),
            P("tp", "fsdp"),
            P("tp", "fsdp"),
            P(("fsdp", "tp")),
            P(None, "fsdp", "tp", None),
        ),
        out_specs=(
            P(None, "fsdp", "tp", None),
            P(None, "fsdp", "tp", None),
            P(("fsdp", "tp")),
            P(("fsdp", "tp")),
            P("fsdp", None, "tp"),
            P(None, "tp", "fsdp"),
            P("tp", "fsdp"),
            P(("fsdp", "tp")),
            P("fsdp", "tp"),
            P("tp", "fsdp"),
            P("tp", "fsdp"),
            P(("fsdp", "tp")),
        ),
        check_vma=False,
    )
```

```python
import functools
import math

import jax
import jax.numpy as jnp
from jax import lax
from jax.experimental import pallas as pl
from jax.experimental.pallas import tpu as pltpu
from jax.sharding import PartitionSpec as P

ROT = 32
LANES = 128

norm_epsilon = 1e-05
gelu_factor = 0.7978845608028654
mask_fill = -1e30
BF = jnp.bfloat16
F32 = jnp.float32
VMEM_LIMIT = 56 * 1024 * 1024


def rotary_tables(length, head_dim, rot_dim):
    half_rot = rot_dim // 2
    places = lax.broadcasted_iota(jnp.int32, (length, LANES), 0).astype(F32)
    lanes = lax.rem(lax.broadcasted_iota(jnp.int32, (length, LANES), 1), head_dim)
    inv_freq = 10000.0 ** (-2.0 * lax.rem(lanes, half_rot).astype(F32) / rot_dim)
    angles = places * inv_freq
    sine = jnp.sin(angles)
    cosine = jnp.where(lanes < rot_dim, jnp.cos(angles), 1.0)
    lower = jnp.where(lanes < half_rot, -sine, 0.0)
    upper = jnp.where((lanes >= half_rot) & (lanes < rot_dim), sine, 0.0)
    return cosine, lower, upper


def turn(vals, cosine, lower, upper):
    half_rot = ROT // 2
    ahead = pltpu.roll(vals, LANES - half_rot, 1)
    behind = pltpu.roll(vals, half_rot, 1)
    return vals * cosine + ahead * lower + behind * upper


def dot_rows(left, right):
    return lax.dot_general(left, right, (((0,), (0,)), ((), ())), preferred_element_type=F32)


def dot_cols(left, right):
    return lax.dot_general(left, right, (((1,), (1,)), ((), ())), preferred_element_type=F32)


def dot_plain(left, right):
    return lax.dot_general(left, right, (((1,), (0,)), ((), ())), preferred_element_type=F32)


def head_lanes(vals, head, head_dim):
    lane_ids = lax.broadcasted_iota(jnp.int32, vals.shape, 1)
    return jnp.where(lane_ids // head_dim == head, vals, jnp.zeros_like(vals))


def seen_keys(block):
    key_ids = lax.broadcasted_iota(jnp.int32, (block, block), 0)
    return key_ids <= lax.broadcasted_iota(jnp.int32, (block, block), 1)


def attend_kernel(head_dim, block, qkv_ref, cos_ref, low_ref, up_ref, rot_ref, attn_ref, lse_ref):
    length = qkv_ref.shape[0]
    scale = 1.0 / math.sqrt(head_dim)
    tables = (cos_ref[...], low_ref[...], up_ref[...])
    rot_ref[:, :LANES] = turn(qkv_ref[:, :LANES], *tables).astype(BF) * BF(scale)
    rot_ref[:, LANES : 2 * LANES] = turn(qkv_ref[:, LANES : 2 * LANES], *tables).astype(BF)
    rot_ref[:, 2 * LANES :] = qkv_ref[:, 2 * LANES :].astype(BF)
    heads = LANES // head_dim
    seen = seen_keys(block)
    for first in range(0, length, block):
        last = first + block
        total = jnp.zeros((block, LANES), F32)
        for head in range(heads):
            query_block = head_lanes(rot_ref[first:last, :LANES], head, head_dim)
            scores = jnp.where(seen, dot_cols(rot_ref[first:last, LANES : 2 * LANES], query_block), mask_fill)
            col_max = jnp.max(scores, axis=0, keepdims=True)
            if first:
                before = dot_cols(rot_ref[:first, LANES : 2 * LANES], query_block)
                col_max = jnp.maximum(col_max, jnp.max(before, axis=0, keepdims=True))
            probs = jnp.exp(scores - col_max)
            denom = jnp.sum(probs, axis=0, keepdims=True)
            part = dot_rows(probs.astype(BF), head_lanes(rot_ref[first:last, 2 * LANES :], head, head_dim))
            if first:
                probs = jnp.exp(before - col_max)
                denom += jnp.sum(probs, axis=0, keepdims=True)
                part += dot_rows(probs.astype(BF), head_lanes(rot_ref[:first, 2 * LANES :], head, head_dim))
            total += part * jnp.broadcast_to(1.0 / denom, (LANES, block)).T
            lse_ref[0, head : head + 1, first:last] = col_max + jnp.log(denom)
        attn_ref[first:last, :] = total.astype(BF)


def attend_back_kernel(head_dim, block, rot_ref, grad_ref, attn_ref, lse_ref, cos_ref, low_ref, up_ref, out_ref, sum_ref, key_acc, value_acc):
    length = rot_ref.shape[0]
    scale = 1.0 / math.sqrt(head_dim)
    heads = LANES // head_dim
    seen = seen_keys(block)

    def back(vals, span):
        return turn(vals, cos_ref[span, :], -low_ref[span, :], -up_ref[span, :])

    query_sum = jnp.zeros((1, LANES), F32)
    key_acc[...] = jnp.zeros_like(key_acc)
    value_acc[...] = jnp.zeros_like(value_acc)
    for first in range(0, length, block):
        last = first + block
        total = jnp.zeros((block, LANES), F32)
        inner = (grad_ref[first:last, :].astype(F32) * attn_ref[first:last, :].astype(F32)).T
        for head in range(heads):
            query_block = head_lanes(rot_ref[first:last, :LANES], head, head_dim)
            grad_block = head_lanes(grad_ref[first:last, :], head, head_dim)
            lse = lse_ref[0, head : head + 1, first:last]
            inner_sum = jnp.sum(inner[head * head_dim : (head + 1) * head_dim], axis=0, keepdims=True)
            for start, stop in ((0, first), (first, last)):
                if start == stop:
                    continue
                keys = rot_ref[start:stop, LANES : 2 * LANES]
                probs = jnp.exp(dot_cols(keys, query_block) - lse)
                if start == first:
                    probs = jnp.where(seen, probs, 0.0)
                value_acc[start:stop, :] += dot_plain(probs.astype(BF), grad_block)
                prob_grad = dot_cols(rot_ref[start:stop, 2 * LANES :], grad_block)
                score_grad = (probs * (prob_grad - inner_sum)).astype(BF)
                total += dot_rows(score_grad, head_lanes(keys, head, head_dim))
                key_acc[start:stop, :] += dot_plain(score_grad, query_block)
        turned = back(total * scale, slice(first, last))
        query_sum += jnp.sum(turned, axis=0, keepdims=True)
        out_ref[first:last, :LANES] = turned.astype(BF)
    turned = back(key_acc[...], slice(0, length))
    out_ref[:, LANES : 2 * LANES] = turned.astype(BF)
    out_ref[:, 2 * LANES :] = value_acc[...].astype(BF)
    sum_ref[0:1, :LANES] = query_sum
    sum_ref[0:1, LANES : 2 * LANES] = jnp.sum(turned, axis=0, keepdims=True)
    sum_ref[0:1, 2 * LANES :] = jnp.sum(value_acc[...], axis=0, keepdims=True)


def attention_cost(seqs, pairs, length, matmuls):
    flops = seqs * pairs * matmuls * 2 * 2 * length * length * LANES
    return estimate(flops, seqs * pairs * length * LANES * 16)


def attend(qkv, tables, length, head_dim):
    tokens, width = qkv.shape
    seqs, pairs = tokens // length, width // (3 * LANES)
    heads = LANES // head_dim
    block = min(512, length)
    table_spec = pl.BlockSpec((length, LANES), lambda s, h: (0, 0))
    return pl.pallas_call(
        functools.partial(attend_kernel, head_dim, block),
        grid=(seqs, pairs),
        in_specs=[pl.BlockSpec((length, 3 * LANES), lambda s, h: (s, h))] + [table_spec] * 3,
        out_specs=[
            pl.BlockSpec((length, 3 * LANES), lambda s, h: (s, h)),
            pl.BlockSpec((length, LANES), lambda s, h: (s, h)),
            pl.BlockSpec((1, heads, length), lambda s, h: (s * pairs + h, 0, 0)),
        ],
        out_shape=[
            jax.ShapeDtypeStruct((tokens, width), BF),
            jax.ShapeDtypeStruct((tokens, pairs * LANES), BF),
            jax.ShapeDtypeStruct((seqs * pairs, heads, length), F32),
        ],
        compiler_params=pltpu.CompilerParams(vmem_limit_bytes=VMEM_LIMIT),
        cost_estimate=attention_cost(seqs, pairs, length, 3),
    )(qkv, *tables)


def attend_back(rot, attn_grad, attn, lse, tables, length, head_dim):
    tokens, width = rot.shape
    seqs, pairs = tokens // length, width // (3 * LANES)
    heads = LANES // head_dim
    block = min(512, length)
    table_spec = pl.BlockSpec((length, LANES), lambda s, h: (0, 0))
    return pl.pallas_call(
        functools.partial(attend_back_kernel, head_dim, block),
        grid=(seqs, pairs),
        in_specs=[
            pl.BlockSpec((length, 3 * LANES), lambda s, h: (s, h)),
            pl.BlockSpec((length, LANES), lambda s, h: (s, h)),
            pl.BlockSpec((length, LANES), lambda s, h: (s, h)),
            pl.BlockSpec((1, heads, length), lambda s, h: (s * pairs + h, 0, 0)),
        ]
        + [table_spec] * 3,
        out_specs=[
            pl.BlockSpec((length, 3 * LANES), lambda s, h: (s, h)),
            pl.BlockSpec((8, 3 * LANES), lambda s, h: (s, h)),
        ],
        out_shape=[jax.ShapeDtypeStruct((tokens, width), BF), jax.ShapeDtypeStruct((8 * seqs, width), F32)],
        scratch_shapes=[pltpu.VMEM((length, LANES), F32), pltpu.VMEM((length, LANES), F32)],
        compiler_params=pltpu.CompilerParams(vmem_limit_bytes=VMEM_LIMIT),
        cost_estimate=attention_cost(seqs, pairs, length, 6),
    )(rot, attn_grad, attn, lse, *tables)


def spec_rows(tile, width):
    return pl.BlockSpec((tile, width), lambda i, s: (i, 0))


def spec_whole(array):
    return pl.BlockSpec(array.shape, lambda i, s: (0,) * array.ndim)


def estimate(flops, moved):
    return pl.CostEstimate(flops=int(flops) // 64, bytes_accessed=int(moved) // 64, transcendentals=0)


def lined_dot(slots_ref, rows_ref, parts, cols):
    depth = parts[0].shape[0]
    total = None
    for at, part in enumerate(parts):
        first = pl.multiple_of(slots_ref[at] * depth, depth)
        piece = dot_plain(rows_ref[:, pl.ds(first, depth)], part[:, cols])
        total = piece if total is None else total + piece
    return total


def rows_call(kernel, slots, ins, in_specs, outs, tile, cost, out_specs=None, steps=None):
    return pl.pallas_call(
        kernel,
        grid_spec=pltpu.PrefetchScalarGridSpec(
            num_scalar_prefetch=1,
            grid=(steps or outs[0].shape[0] // tile,),
            in_specs=in_specs,
            out_specs=out_specs or [spec_rows(tile, out.shape[1]) for out in outs],
        ),
        out_shape=outs,
        compiler_params=pltpu.CompilerParams(vmem_limit_bytes=VMEM_LIMIT),
        cost_estimate=cost,
    )(slots, *ins)


def normalise(rows):
    micros, tokens, width = rows.shape

    def kernel(rows_ref, out_ref):
        vals = rows_ref[0].astype(F32)
        mean = jnp.mean(vals, axis=-1, keepdims=True)
        centred = vals - mean
        var = jnp.mean(centred * centred, axis=-1, keepdims=True)
        out_ref[...] = (centred * lax.rsqrt(var + norm_epsilon)).astype(BF)

    def one(micro):
        return pl.pallas_call(
            kernel,
            grid=(2,),
            in_specs=[pl.BlockSpec((1, tokens // 2, width), lambda i: (micro, i, 0))],
            out_specs=pl.BlockSpec((tokens // 2, width), lambda i: (i, 0)),
            out_shape=jax.ShapeDtypeStruct((tokens, width), BF),
            compiler_params=pltpu.CompilerParams(vmem_limit_bytes=VMEM_LIMIT),
            cost_estimate=estimate(10 * tokens * width, 4 * tokens * width),
        )(rows)

    return [one(micro) for micro in range(micros)]


def norm_qkv(slots, rows, gain, shift, parts, bias):
    tokens, width = rows.shape
    cols, tile = bias.shape[1], 512

    def kernel(slots_ref, rows_ref, gain_ref, shift_ref, bias_ref, *refs):
        parts, (normed_ref, qkv_ref) = refs[:-2], refs[-2:]
        normed_ref[...] = (rows_ref[...].astype(F32) * gain_ref[...] + shift_ref[...]).astype(BF)
        qkv_ref[...] = lined_dot(slots_ref, normed_ref, parts, slice(0, cols)) + bias_ref[...]

    return rows_call(
        kernel,
        slots,
        [rows, gain, shift, bias, *parts],
        [spec_rows(tile, width)] + [spec_whole(array) for array in (gain, shift, bias, *parts)],
        [jax.ShapeDtypeStruct((tokens, width), BF), jax.ShapeDtypeStruct((tokens, cols), F32)],
        tile,
        estimate(2 * tokens * width * cols, tokens * (4 * width + 4 * cols)),
    )


def micro_spec(micro, steps, tile, width):
    return pl.BlockSpec((tile, width), lambda i, s: (jnp.clip(i - micro * steps, 0, steps - 1), 0))


def up_act(slots, rows, parts, bias):
    count = len(rows)
    tokens, width = rows[0].shape
    cols, tile, chunk = bias.shape[1], 512, 512
    steps = tokens // tile

    def kernel(slots_ref, bias_ref, *refs):
        ins, parts, outs = refs[:count], refs[count : -2 * count], refs[-2 * count :]
        for micro in range(count):

            @pl.when(pl.program_id(0) // steps == micro)
            def _():
                for at in range(0, cols, chunk):
                    span = slice(at, at + chunk)
                    pre = lined_dot(slots_ref, ins[micro], parts, span) + bias_ref[:, span]
                    square = pre * pre
                    tanh = jnp.tanh(pre * (gelu_factor + (gelu_factor * 0.044715) * square))
                    half = 0.5 + 0.5 * tanh
                    act = pre * half
                    outs[micro][:, span] = act.astype(BF)
                    inner = 2 * gelu_factor + (6 * 0.044715 * gelu_factor) * square
                    outs[count + micro][:, span] = (half + (act - act * half) * inner).astype(BF)

    outs = rows_call(
        kernel,
        slots,
        [bias, *rows, *parts],
        [spec_whole(bias)]
        + [micro_spec(m, steps, tile, width) for m in range(count)]
        + [spec_whole(part) for part in parts],
        [jax.ShapeDtypeStruct((tokens, cols), BF)] * (2 * count),
        tile,
        estimate(2 * count * tokens * width * cols, count * tokens * (2 * width + 4 * cols)),
        [micro_spec(m, steps, tile, cols) for m in range(count)] * 2,
        count * steps,
    )
    return outs[:count], outs[count:]


def pre_grad_rows(slots, rows, parts, slopes):
    count = len(rows)
    tokens, width = rows[0].shape
    cols, tile = slopes[0].shape[1], 512
    steps = tokens // tile

    def kernel(slots_ref, *refs):
        ins, slopes, parts = refs[:count], refs[count : 2 * count], refs[2 * count : -count - 1]
        outs, sum_ref = refs[-count - 1 : -1], refs[-1]

        @pl.when(pl.program_id(0) == 0)
        def _():
            sum_ref[...] = jnp.zeros_like(sum_ref)

        for micro in range(count):

            @pl.when(pl.program_id(0) // steps == micro)
            def _():
                act_grad = lined_dot(slots_ref, ins[micro], parts, slice(0, cols))
                grad = act_grad * slopes[micro][...].astype(F32)
                outs[micro][...] = grad.astype(BF)
                sum_ref[0:1, :] += jnp.sum(grad, axis=0, keepdims=True)

    return rows_call(
        kernel,
        slots,
        [*rows, *slopes, *parts],
        [micro_spec(m, steps, tile, width) for m in range(count)]
        + [micro_spec(m, steps, tile, cols) for m in range(count)]
        + [spec_whole(part) for part in parts],
        [jax.ShapeDtypeStruct((tokens, cols), BF)] * count + [jax.ShapeDtypeStruct((8, cols), F32)],
        tile,
        estimate(2 * count * tokens * width * cols, count * tokens * (2 * width + 4 * cols)),
        [micro_spec(m, steps, tile, cols) for m in range(count)] + [pl.BlockSpec((8, cols), lambda i, s: (0, 0))],
        count * steps,
    )


def head_grad_rows(slots, rows, parts, first):
    tokens, width = rows.shape
    cols, tile = parts[0].shape[1] - first, 1024

    def kernel(slots_ref, rows_ref, *refs):
        parts, out_ref = refs[:-1], refs[-1]
        out_ref[...] = lined_dot(slots_ref, rows_ref, parts, slice(first, first + cols)).astype(BF)

    return rows_call(
        kernel,
        slots,
        [rows, *parts],
        [spec_rows(tile, width)] + [spec_whole(part) for part in parts],
        [jax.ShapeDtypeStruct((tokens, cols), BF)],
        tile,
        estimate(2 * tokens * width * cols, tokens * (2 * width + 2 * cols)),
    )[0]


def branch_rows(slots, ones, one_parts, first, twos, two_parts, block):
    micros = len(ones)
    tokens, cols = ones[0].shape
    count, depth = len(one_parts), one_parts[0].shape[0]
    held = 2
    tile = held * block
    width, steps = count * depth, tokens // tile

    def kernel(slots_ref, *refs):
        ones, twos, out_ref = refs[:micros], refs[micros : 2 * micros], refs[-1]
        parts = refs[2 * micros : -1]
        for micro in range(micros):

            @pl.when(pl.program_id(0) // steps == micro)
            def _():
                for at in range(count):
                    where = pl.multiple_of(slots_ref[at] * depth, depth)
                    total = dot_cols(ones[micro][...], parts[at][:, first : first + cols])
                    total += dot_cols(twos[micro][...], parts[count + at][...])
                    out_ref[:, 0, :, pl.ds(where, depth)] = total.astype(BF).reshape(held, block, depth)

    return rows_call(
        kernel,
        slots,
        [*ones, *twos, *one_parts, *two_parts],
        [micro_spec(m, steps, tile, cols) for m in range(micros)]
        + [micro_spec(m, steps, tile, twos[0].shape[1]) for m in range(micros)]
        + [spec_whole(part) for part in (*one_parts, *two_parts)],
        [jax.ShapeDtypeStruct((tokens // block, micros, block, width), BF)],
        tile,
        estimate(2 * micros * tokens * width * (cols + twos[0].shape[1]), 2 * micros * tokens * (width + cols)),
        [pl.BlockSpec((held, 1, block, width), lambda i, s: (lax.rem(i, steps), i // steps, 0, 0))],
        micros * steps,
    )[0]


def normed_grad_rows(slots, one, one_parts, two, two_parts, rows, block, split):
    tokens, cols = one.shape
    count, depth = len(one_parts), one_parts[0].shape[0]
    tile = 2 * block
    width = count * depth

    def kernel(slots_ref, one_ref, two_ref, rows_ref, *refs):
        outs, sum_ref = refs[2 * count : -1], refs[-1]

        @pl.when(pl.program_id(0) == 0)
        def _():
            sum_ref[...] = jnp.zeros_like(sum_ref)

        for at in range(count):
            where = pl.multiple_of(slots_ref[at] * depth, depth)
            span = pl.ds(where, depth)
            total = dot_cols(one_ref[...], refs[at][:, :cols])
            total += dot_cols(two_ref[...], refs[count + at][...])
            if split:
                first = slots_ref[count] == 0
                outs[0][:, span] = jnp.where(first, total[:block], total[block:]).astype(BF)
                outs[1][:, span] = jnp.where(first, total[block:], total[:block]).astype(BF)
            else:
                outs[0][:, span] = total.astype(BF)
            sum_ref[0:1, span] += jnp.sum(total * rows_ref[:, span].astype(F32), axis=0, keepdims=True)
            sum_ref[1:2, span] += jnp.sum(total, axis=0, keepdims=True)

    pieces = 2 if split else 1
    return rows_call(
        kernel,
        slots,
        [one, two, rows, *one_parts, *two_parts],
        [spec_rows(tile, cols), spec_rows(tile, two.shape[1]), spec_rows(tile, width)]
        + [spec_whole(part) for part in (*one_parts, *two_parts)],
        [jax.ShapeDtypeStruct((tokens // pieces, width), BF)] * pieces + [jax.ShapeDtypeStruct((8, width), F32)],
        tile,
        estimate(2 * tokens * width * (cols + two.shape[1]), 2 * tokens * (2 * width + cols + two.shape[1])),
        [spec_rows(tile // pieces, width)] * pieces + [pl.BlockSpec((8, width), lambda i, s: (0, 0))],
        tokens // tile,
    )


def norm_back(rows, cots, pieces, gain, micro, earlier=None):
    micros, tokens, width = rows.shape
    tile = tokens // 4

    def kernel(rows_ref, cot_ref, gain_ref, *refs):
        vals = rows_ref[0].astype(F32)
        mean = jnp.mean(vals, axis=-1, keepdims=True)
        centred = vals - mean
        scale = lax.rsqrt(jnp.mean(centred * centred, axis=-1, keepdims=True) + norm_epsilon)
        scaled = centred * scale
        grad = refs[0][...].astype(F32)
        for ref in refs[1 : len(pieces)]:
            grad += ref[...].astype(F32)
        grad *= gain_ref[...]
        inner = jnp.mean(grad * scaled, axis=-1, keepdims=True)
        grad = (grad - jnp.mean(grad, axis=-1, keepdims=True) - scaled * inner) * scale
        refs[-1][0] = (cot_ref[0].astype(F32) + grad).astype(BF)

    at_micro = pl.BlockSpec((1, tile, width), lambda i: (micro, i, 0))
    given = [] if earlier is None else [earlier]
    return pl.pallas_call(
        kernel,
        grid=(tokens // tile,),
        in_specs=[at_micro, at_micro, pl.BlockSpec((1, width), lambda i: (0, 0))]
        + [pl.BlockSpec((tile, width), lambda i: (i, 0))] * len(pieces)
        + [pl.BlockSpec(memory_space=pl.ANY)] * len(given),
        out_specs=at_micro,
        out_shape=jax.ShapeDtypeStruct(rows.shape, BF),
        input_output_aliases={3 + len(pieces): 0} if given else {},
        compiler_params=pltpu.CompilerParams(vmem_limit_bytes=VMEM_LIMIT),
        cost_estimate=estimate(20 * tokens * width, 10 * tokens * width),
    )(rows, cots, gain, *pieces, *given)


def weight_grad(lefts, rights, turned=False):
    tile, chunk = 512, 512
    micro_count = len(lefts)
    tokens, width = lefts[0].shape
    widths = [right[0].shape[1] for right in rights]
    cols, steps = sum(widths), tokens // tile
    shape = (cols, width) if turned else (width, cols)

    def kernel(*refs):
        out_ref, acc_ref = refs[-2:]
        step = pl.program_id(0)

        @pl.when(step == 0)
        def _():
            acc_ref[...] = jnp.zeros_like(acc_ref)

        for micro in range(micro_count):

            @pl.when(step // steps == micro)
            def _():
                first = 0
                for at, span in enumerate(widths):
                    right = refs[(1 + at) * micro_count + micro]
                    if turned:
                        for row in range(0, span, min(chunk, span)):
                            rows = slice(row, row + min(chunk, span))
                            acc_ref[first + row : first + rows.stop, :] += dot_rows(right[:, rows], refs[micro][...])
                    else:
                        for row in range(0, width, chunk):
                            acc_ref[row : row + chunk, first : first + span] += dot_rows(
                                refs[micro][:, row : row + chunk], right[...]
                            )
                    first += span

        @pl.when(step == micro_count * steps - 1)
        def _():
            out_ref[...] = acc_ref[...].astype(BF)

    def side(micro, span):
        return pl.BlockSpec((tile, span), lambda i: (jnp.clip(i - micro * steps, 0, steps - 1), 0))

    return pl.pallas_call(
        kernel,
        grid=(micro_count * steps,),
        in_specs=[side(micro, span) for span in (width, *widths) for micro in range(micro_count)],
        out_specs=pl.BlockSpec(shape, lambda i: (0, 0)),
        out_shape=jax.ShapeDtypeStruct(shape, BF),
        scratch_shapes=[pltpu.VMEM(shape, F32)],
        compiler_params=pltpu.CompilerParams(vmem_limit_bytes=VMEM_LIMIT),
        cost_estimate=estimate(
            2 * micro_count * tokens * width * cols, 2 * micro_count * tokens * (width + cols)
        ),
    )(*lefts, *(array for right in rights for array in right))


def shards(
    inputs,
    ln_gain,
    ln_bias,
    qkv_weight,
    qkv_bias,
    out_weight,
    out_bias,
    up_weight,
    up_bias,
    down_weight,
    down_bias,
    cotangent,
):
    micro_count, _, token_rows, model_width = inputs.shape
    fsdp_size, tp_size = lax.axis_size("fsdp"), lax.axis_size("tp")
    line = fsdp_size // 2
    fsdp_at, tp_at = lax.axis_index("fsdp"), lax.axis_index("tp")
    line_at, pair_at = fsdp_at >> 1, fsdp_at & 1
    plane_size = 2 * tp_size
    planes = [[plane * plane_size + i for i in range(plane_size)] for plane in range(line)]
    ring = [(f, ((f // 2 + 1) % line) * 2 + f % 2) for f in range(fsdp_size)]
    length = token_rows * tp_size
    head_dim = qkv_bias.shape[2] * fsdp_size
    shard_rows = model_width // fsdp_size
    line_rows = 2 * shard_rows
    attn_cols = out_weight.shape[0] // 2
    qkv_cols = 3 * attn_cols
    pairs = attn_cols // LANES
    mlp_cols = up_weight.shape[1] // 2
    both_axes = ("fsdp", "tp")

    def swap_pair(vals):
        return lax.ppermute(vals, "fsdp", [(f, f ^ 1) for f in range(fsdp_size)])

    def gather_plane(vals):
        return lax.all_gather(vals, both_axes, axis=0, tiled=True, axis_index_groups=planes)

    def scatter_plane(vals):
        return lax.psum_scatter(vals, both_axes, scatter_dimension=0, tiled=True, axis_index_groups=planes)

    def doubled(cur, axis, size, at, bit):
        other = lax.ppermute(cur, axis, [(i, i ^ bit) for i in range(size)])
        upper = (at & bit) != 0
        return jnp.where(upper, jnp.concatenate([other, cur]), jnp.concatenate([cur, other]))

    def attn_half(half):
        qkv_part = lax.dynamic_slice_in_dim(qkv_weight, half * attn_cols, attn_cols, axis=2)
        qkv_part = qkv_part.reshape(shard_rows, 3, pairs, LANES).transpose(0, 2, 1, 3)
        out_part = lax.dynamic_slice_in_dim(out_weight, half * attn_cols, attn_cols, axis=0)
        return jnp.concatenate([qkv_part.reshape(shard_rows, qkv_cols), out_part.T], axis=1)

    def up_half(half):
        return lax.dynamic_slice_in_dim(up_weight, half * mlp_cols, mlp_cols, axis=1)

    def down_half(half):
        return lax.dynamic_slice_in_dim(down_weight, half * mlp_cols, mlp_cols, axis=0).T

    def pair_join(own, other):
        return jnp.where(pair_at == 0, jnp.concatenate([own, other]), jnp.concatenate([other, own]))

    class Box:
        def __init__(self, val):
            self.val = val

    class Line:
        tokens = []

        def tie(self, *boxes):
            held = []
            for box in (*boxes, *self.tokens):
                if box not in held:
                    held.append(box)
            if len(held) > 1:
                for box, val in zip(held, lax.optimization_barrier(tuple(box.val for box in held))):
                    box.val = val

        def run(self, piece, *boxes):
            self.tie(*boxes)
            results = [Box(val) for val in piece(*(box.val for box in boxes))]
            self.tokens = [results[0]]
            return results

        def sync(self, box):
            self.tokens = self.tokens + [box]

    order = Line()

    class Gather:
        def __init__(self, shard):
            self.parts = [shard]

        def move(self):
            if len(self.parts) < line:
                order.tie(self.parts[-1])
                self.parts.append(Box(lax.ppermute(self.parts[-1].val, "fsdp", ring)))

        def sync(self):
            order.sync(self.parts[-1])

        def finish(self):
            while len(self.parts) < line:
                self.move()
            self.sync()

        def vals(self):
            return [part.val for part in self.parts]

    class Scatter:
        def __init__(self, part, axis):
            self.part, self.step, self.came, self.axis = part, 1, None, axis

        def total(self):
            at_line = lax.rem(line_at + line - self.step, line)
            own = lax.dynamic_slice_in_dim(self.part.val, at_line * line_rows, line_rows, axis=self.axis)
            if self.came is None:
                return own
            order.tie(self.came)
            return self.came.val.astype(F32) + own.astype(F32)

        def move(self):
            if self.step < line:
                sent = Box(self.total().astype(BF))
                if self.came is None:
                    order.tie(sent)
                self.came = Box(lax.ppermute(sent.val, "fsdp", ring))
                self.step += 1

        def sync(self):
            order.sync(self.came)

        def rows_at(self, half):
            own = lax.dynamic_slice_in_dim(
                self.part.val, line_at * line_rows + half * shard_rows, shard_rows, axis=self.axis
            )
            came = lax.dynamic_slice_in_dim(self.came.val, half * shard_rows, shard_rows, axis=self.axis)
            return came.astype(F32) + own.astype(F32)

        def swap(self):
            while self.step < line:
                self.move()
            order.tie(self.came)
            self.sent = Box(self.rows_at(1 - pair_at).astype(BF))
            self.got = Box(swap_pair(self.sent.val))

        def halves(self):
            order.tie(self.came)
            keep, got = self.rows_at(pair_at), self.got.val.astype(F32)
            return jnp.where(pair_at == 0, keep, got), jnp.where(pair_at == 0, got, keep)

    class SmallSum:
        def __init__(self, everywhere, over_fsdp):
            self.cur, self.rest = Box(everywhere), over_fsdp
            self.size = everywhere.shape[0]
            bits = [("tp", tp_size, bit) for bit in range(tp_size.bit_length() - 1)]
            self.steps = bits + [("fsdp", fsdp_size, 0), ("line", 0, 0)]

        def move(self):
            if self.steps:
                axis, size, bit = self.steps.pop(0)
                if axis == "fsdp":
                    self.cur = Box(jnp.concatenate([self.cur.val, self.rest]))
                order.tie(self.cur)
                if axis == "line":
                    others = along_line(self.cur.val)
                else:
                    others = [lax.ppermute(self.cur.val, axis, [(i, i ^ (1 << bit)) for i in range(size)])]
                self.cur = Box(sum(others, self.cur.val))

        def split(self):
            while self.steps:
                self.move()
            return self.cur.val[: self.size], self.cur.val[self.size :]

    plain = normalise(inputs[:, 0])
    cots = [cotangent[m].reshape(token_rows, model_width) for m in range(micro_count)]
    micros = range(micro_count)
    plane_rows, plane_cots = [None] * micro_count, [None] * micro_count

    def gather_behind(rows):
        sent = Box(rows)
        order.tie(sent)
        return Box(gather_plane(sent.val))

    small = jnp.concatenate(
        [vec.reshape(-1) for vec in (ln_gain, ln_bias, out_bias, down_bias, qkv_bias, up_bias)]
    )
    attn_send = Box(attn_half(1 - pair_at))
    order.tokens = [attn_send]
    plane_rows[0] = gather_behind(plain[0])
    attn_shard = Box(pair_join(attn_half(pair_at), swap_pair(attn_send.val)))
    small_all = Box(small[None])
    order.tokens = [attn_shard]
    order.tie(small_all)
    small_all = small_all.val
    for bit in range(tp_size.bit_length() - 1):
        small_all = doubled(small_all, "tp", tp_size, tp_at, 1 << bit)
    small_near = small_all

    def along_line(vals):
        return [lax.ppermute(vals, "fsdp", [(f, f ^ (far << 1)) for f in range(fsdp_size)]) for far in range(1, line)]

    def small_step(small_all, step):
        order.tie(small_all)
        if step == 0:
            return Box(doubled(small_all.val, "fsdp", fsdp_size, fsdp_at, 1))
        held = [small_all.val] + along_line(small_all.val)
        for bit in range(line.bit_length() - 1):
            other = (line_at & (1 << bit)) != 0
            held = [jnp.where(other, held[i ^ (1 << bit)], held[i]) for i in range(line)]
        return Box(jnp.concatenate(held))

    small_all = Box(small_near)
    attn_ring = Gather(attn_shard)
    attn_ring.move()
    plane_rows[1] = gather_behind(plain[1])
    order.sync(small_all)
    small_all = small_step(small_all, 0)
    bias_total = Box(sum(jnp.sum(cots[m].astype(F32), axis=0) for m in micros))
    up_send = Box(up_half(1 - pair_at))
    order.tie(up_send)
    up_got = Box(swap_pair(up_send.val))
    attn_ring.sync()
    order.sync(small_all)
    attn_ring.move()
    order.sync(bias_total)
    small_all = small_step(small_all, 1)
    down_send = Box(down_half(1 - pair_at))
    order.tie(down_send, up_got)
    down_got = Box(swap_pair(down_send.val))
    up_shard = Box(pair_join(up_half(pair_at), up_got.val))
    attn_ring.sync()
    order.sync(small_all)
    attn_ring.move()
    plane_cots[0] = gather_behind(cots[0])
    order.sync(up_shard)
    order.tie(small_all)
    small_all = small_all.val
    vec_size = ln_gain.shape[0]
    gain_vec, shift_vec, bias_out, bias_down = (
        small_all[:, i * vec_size : (i + 1) * vec_size].reshape(-1).astype(F32) for i in range(4)
    )
    bias_both = bias_out + bias_down
    mine = lax.dynamic_slice_in_dim(
        small_all.reshape(fsdp_size, tp_size, -1), tp_at, 1, axis=1
    )[:, 0].astype(F32)
    at = 4 * vec_size
    qkv_b = mine[:, at : at + qkv_bias.size].reshape(fsdp_size, 3, 2, pairs, -1, qkv_bias.shape[2])
    qkv_b = lax.dynamic_slice_in_dim(qkv_b, pair_at, 1, axis=2)[:, :, 0]
    qkv_b = qkv_b.transpose(2, 1, 3, 0, 4).reshape(1, qkv_cols)
    at += qkv_bias.size
    up_b = mine[:, at:].reshape(fsdp_size, up_bias.shape[0], up_bias.shape[1])
    up_b = up_b.transpose(1, 0, 2).reshape(2, mlp_cols)
    up_b = lax.dynamic_slice_in_dim(up_b, pair_at, 1, axis=0)

    slots = [lax.rem(line_at + line - step, line) for step in range(line)]
    slots = jnp.stack(slots + [tp_at & 1]).astype(jnp.int32)
    tables = rotary_tables(length, head_dim, ROT)
    prepared = [Box(val) for val in (gain_vec[None], shift_vec[None], qkv_b, up_b, slots, *tables)]
    for box in prepared:
        order.sync(box)
    order.tie(down_got)
    down_shard = Box(pair_join(down_half(pair_at), down_got.val))
    order.tokens = [down_shard]
    attn_ring.finish()
    order.tie(up_shard, *prepared)
    gain_row, shift_row, qkv_b, up_b, slots, *tables = (box.val for box in prepared)
    normed, qkvs, rots, attns, lses, acts, slopes = ([None] * micro_count for _ in range(7))
    pre_grads, qkv_grads, qkv_sums, sums, attn_heads = ([None] * micro_count for _ in range(5))

    def norm_piece(m):
        normed[m], qkvs[m] = order.run(
            lambda rows: norm_qkv(slots, rows, gain_row, shift_row, attn_ring.vals(), qkv_b), plane_rows[m]
        )

    def attend_piece(m):
        rots[m], attns[m], lses[m] = order.run(
            lambda vals: attend(vals, tables, length, head_dim), qkvs[m]
        )

    def up_piece():
        def piece(*rows):
            return [val for vals in up_act(slots, rows, up_ring.vals(), up_b) for val in vals]

        results = order.run(piece, *normed)
        acts[:], slopes[:] = results[:micro_count], results[micro_count:]

    def head_grad_piece(m):
        (attn_heads[m],) = order.run(
            lambda cot: [head_grad_rows(slots, cot, attn_ring.vals(), qkv_cols)], plane_cots[m]
        )

    def attend_back_piece(m):
        qkv_grads[m], qkv_sums[m] = order.run(
            lambda rot, grad, attn, lse: attend_back(rot, grad, attn, lse, tables, length, head_dim),
            rots[m],
            attn_heads[m],
            attns[m],
            lses[m],
        )

    def pre_grad_piece():
        def piece(*vals):
            return pre_grad_rows(slots, vals[:micro_count], down_ring.vals(), vals[micro_count:])

        *pre_grads[:], up_sums = order.run(piece, *plane_cots, *slopes)
        return up_sums

    def weight_piece(lefts, *rights, turned=False):
        def piece(*flat):
            sets = [flat[at : at + micro_count] for at in range(0, len(flat), micro_count)]
            return [weight_grad(sets[0], sets[1:], turned)]

        part = order.run(piece, *lefts, *(box for right in rights for box in right))[0]
        return Scatter(part, 1 if turned else 0)

    def branch_piece():
        def piece(*vals):
            rows = branch_rows(
                slots,
                vals[:micro_count],
                attn_ring.vals(),
                qkv_cols,
                vals[micro_count:],
                down_ring.vals(),
                token_rows,
            )
            return [rows.reshape(-1, model_width)]

        return order.run(piece, *attns, *acts)[0]

    def normed_grad_piece(m, split=False):
        *back, sums[m] = order.run(
            lambda one, two, rows: normed_grad_rows(
                slots, one, attn_ring.vals(), two, up_ring.vals(), rows, token_rows, split
            ),
            qkv_grads[m],
            pre_grads[m],
            plane_rows[m],
        )
        return back

    def scatter_behind(box):
        order.tie(box)
        return Box(scatter_plane(box.val))

    up_ring, down_ring = Gather(up_shard), Gather(down_shard)
    order.sync(down_shard)
    up_ring.move()
    norm_piece(0)
    up_ring.sync()
    plane_cots[1] = gather_behind(cots[1])
    up_ring.move()
    attend_piece(0)
    norm_piece(1)
    up_ring.sync()
    up_ring.move()
    attend_piece(1)
    up_ring.finish()
    down_ring.move()
    up_piece()
    down_ring.sync()
    down_ring.move()
    head_grad_piece(0)
    attend_back_piece(0)
    down_ring.sync()
    down_ring.move()

    down_scatter = weight_piece(plane_cots, acts, attns, turned=True)
    down_ring.finish()
    down_scatter.move()
    branch = branch_piece()
    down_scatter.sync()
    branch_sum = scatter_behind(branch)
    down_scatter.move()
    up_sums = pre_grad_piece()
    down_scatter.sync()
    down_scatter.move()
    up_scatter = weight_piece(normed, pre_grads)
    down_scatter.sync()
    down_scatter.swap()
    up_scatter.move()
    head_grad_piece(1)
    attend_back_piece(1)
    up_scatter.sync()
    order.sync(down_scatter.got)
    up_scatter.move()
    (back,) = normed_grad_piece(0)
    up_scatter.sync()
    back_sum = scatter_behind(back)
    up_scatter.move()
    qkv_scatter = weight_piece(normed, qkv_grads)
    up_scatter.sync()
    order.sync(branch_sum)
    up_scatter.swap()
    qkv_scatter.move()
    keep, give = normed_grad_piece(1, True)

    def swap_core(vals):
        return lax.ppermute(vals, "tp", [(t, t ^ 1) for t in range(tp_size)])

    def swap_y(vals):
        return lax.ppermute(vals, "tp", [(t, t ^ 2) for t in range(tp_size)])

    y_at, half = tp_at >> 1, model_width // 2
    up_b_grad = up_sums.val[0]
    qkv_b_grad = sum(jnp.sum(part.val.reshape(-1, 8, qkv_cols)[:, 0], axis=0) for part in qkv_sums)
    qkv_b_grad = qkv_b_grad.reshape(pairs, 3, -1).transpose(1, 0, 2).reshape(3, attn_cols)

    def in_half(vals):
        blank = jnp.zeros_like(vals)
        return jnp.where(
            pair_at == 0, jnp.concatenate([vals, blank], axis=-1), jnp.concatenate([blank, vals], axis=-1)
        )

    gain_total, shift_total = (sum(part.val[i] for part in sums) for i in range(2))
    tail = SmallSum(
        jnp.concatenate([gain_total, shift_total, bias_total.val]),
        jnp.concatenate([in_half(up_b_grad), in_half(qkv_b_grad).reshape(-1)]),
    )
    qkv_scatter.sync()
    order.sync(up_scatter.got)
    order.tie(give, tail.cur)
    tail.move()
    got = Box(swap_core(give.val))
    qkv_scatter.move()
    order.sync(tail.cur)
    order.tie(got)
    blocks = Box((got.val.astype(F32) + keep.val.astype(F32)).astype(BF).reshape(4, token_rows, model_width))
    tail.move()

    def block(pair, y):
        return lax.dynamic_index_in_dim(blocks.val, pair * 2 + y, 0, keepdims=False)

    order.sync(blocks)
    order.sync(tail.cur)
    order.tie(tail.cur)
    far = block(1 - pair_at, 1 - y_at)
    from_pair, from_y = Box(swap_pair(far[:, :half])), Box(swap_y(far[:, half:]))
    tail.move()
    halves = down_scatter.halves()
    down_w_grad = Box(jnp.concatenate([part[:mlp_cols] for part in halves], axis=0))
    out_w_grad = Box(jnp.concatenate([part[mlp_cols:] for part in halves], axis=0))
    for box in (down_w_grad, out_w_grad):
        order.sync(box)

    qkv_scatter.sync()
    order.tie()
    qkv_scatter.move()
    order.tie(from_pair, from_y)
    for_y, for_pair = block(pair_at, 1 - y_at), block(1 - pair_at, y_at)
    for_y = jnp.concatenate(
        [(for_y[:, :half].astype(F32) + from_pair.val.astype(F32)).astype(BF), for_y[:, half:]], axis=1
    )
    for_pair = jnp.concatenate(
        [for_pair[:, :half], (for_pair[:, half:].astype(F32) + from_y.val.astype(F32)).astype(BF)], axis=1
    )
    for_pair, for_y = Box(for_pair), Box(for_y)
    from_pair, from_y = Box(swap_pair(for_pair.val)), Box(swap_y(for_y.val))
    own_block = Box(block(pair_at, y_at))
    for box in (for_pair, for_y, own_block):
        order.sync(box)
    order.tie(back_sum)
    gained = Box(norm_back(inputs[:, 0], cotangent[:, 0], [back_sum.val], gain_row, 0))
    order.sync(gained)
    qkv_scatter.sync()
    order.sync(tail.cur)
    order.tie(tail.cur)
    tail.move()
    qkv_scatter.swap()
    up_w_grad = Box(jnp.concatenate(up_scatter.halves(), axis=1))
    order.sync(up_w_grad)
    order.tie(from_pair, from_y)
    last_pieces = [own_block.val, from_pair.val, from_y.val]
    gained = Box(norm_back(inputs[:, 0], cotangent[:, 0], last_pieces, gain_row, 1, gained.val))
    order.tokens = [gained]
    order.tie(qkv_scatter.got, tail.cur)
    halves = qkv_scatter.halves()
    planes = [
        jnp.concatenate(
            [
                part[:, (pair * 3 + plane) * LANES : (pair * 3 + plane + 1) * LANES]
                for part in halves
                for pair in range(pairs)
            ],
            axis=1,
        )
        for plane in range(3)
    ]
    qkv_w_grad = jnp.stack(planes, axis=0).transpose(1, 0, 2)
    small_sums, bias_sums = tail.split()
    branch_sum = branch_sum.val.reshape(micro_count, token_rows, model_width)
    output = (inputs[:, 0].astype(F32) + branch_sum.astype(F32) + bias_both).astype(BF)

    small_sums = small_sums.reshape(3, fsdp_size * tp_size, vec_size)
    small_sums = lax.dynamic_slice_in_dim(small_sums, fsdp_at * tp_size + tp_at, 1, axis=1)[:, 0]
    gain_sum, shift_sum, bias_sum = small_sums[0], small_sums[1], small_sums[2]
    up_b_sum = bias_sums[: 2 * mlp_cols].reshape(up_bias.shape[0], -1)
    up_b_sum = lax.dynamic_slice_in_dim(up_b_sum, fsdp_at * up_bias.shape[1], up_bias.shape[1], axis=1)
    qkv_b_sum = bias_sums[2 * mlp_cols :].reshape(3, qkv_bias.shape[1], -1)
    qkv_b_sum = lax.dynamic_slice_in_dim(qkv_b_sum, fsdp_at * qkv_bias.shape[2], qkv_bias.shape[2], axis=2)

    return (
        output[:, None],
        gained.val[:, None],
        gain_sum,
        shift_sum,
        qkv_w_grad,
        qkv_b_sum,
        out_w_grad.val,
        bias_sum,
        up_w_grad.val,
        up_b_sum,
        down_w_grad.val,
        bias_sum,
    )


def solution(mesh):
    return jax.shard_map(
        shards,
        mesh=mesh,
        in_specs=(
            P(None, "fsdp", "tp", None),
            P(("fsdp", "tp")),
            P(("fsdp", "tp")),
            P("fsdp", None, "tp"),
            P(None, "tp", "fsdp"),
            P("tp", "fsdp"),
            P(("fsdp", "tp")),
            P("fsdp", "tp"),
            P("tp", "fsdp"),
            P("tp", "fsdp"),
            P(("fsdp", "tp")),
            P(None, "fsdp", "tp", None),
        ),
        out_specs=(
            P(None, "fsdp", "tp", None),
            P(None, "fsdp", "tp", None),
            P(("fsdp", "tp")),
            P(("fsdp", "tp")),
            P("fsdp", None, "tp"),
            P(None, "tp", "fsdp"),
            P("tp", "fsdp"),
            P(("fsdp", "tp")),
            P("fsdp", "tp"),
            P("tp", "fsdp"),
            P("tp", "fsdp"),
            P(("fsdp", "tp")),
        ),
        check_vma=False,
    )
```

```python
import functools
import math

import jax
import jax.numpy as jnp
from jax import lax
from jax.experimental import pallas as pl
from jax.experimental.pallas import tpu as pltpu
from jax.sharding import PartitionSpec as P

ROT = 32
LANES = 128

norm_epsilon = 1e-05
gelu_factor = 0.7978845608028654
mask_fill = -1e30
BF = jnp.bfloat16
F32 = jnp.float32
VMEM_LIMIT = 56 * 1024 * 1024


def rotary_tables(length, head_dim, rot_dim):
    half_rot = rot_dim // 2
    places = lax.broadcasted_iota(jnp.int32, (length, LANES), 0).astype(F32)
    lanes = lax.rem(lax.broadcasted_iota(jnp.int32, (length, LANES), 1), head_dim)
    inv_freq = 10000.0 ** (-2.0 * lax.rem(lanes, half_rot).astype(F32) / rot_dim)
    angles = places * inv_freq
    sine = jnp.sin(angles)
    cosine = jnp.where(lanes < rot_dim, jnp.cos(angles), 1.0)
    lower = jnp.where(lanes < half_rot, -sine, 0.0)
    upper = jnp.where((lanes >= half_rot) & (lanes < rot_dim), sine, 0.0)
    return cosine, lower, upper


def turn(vals, cosine, lower, upper):
    half_rot = ROT // 2
    ahead = pltpu.roll(vals, LANES - half_rot, 1)
    behind = pltpu.roll(vals, half_rot, 1)
    return vals * cosine + ahead * lower + behind * upper


def dot_rows(left, right):
    return lax.dot_general(left, right, (((0,), (0,)), ((), ())), preferred_element_type=F32)


def dot_cols(left, right):
    return lax.dot_general(left, right, (((1,), (1,)), ((), ())), preferred_element_type=F32)


def dot_plain(left, right):
    return lax.dot_general(left, right, (((1,), (0,)), ((), ())), preferred_element_type=F32)


def head_lanes(vals, head, head_dim):
    lane_ids = lax.broadcasted_iota(jnp.int32, vals.shape, 1)
    return jnp.where(lane_ids // head_dim == head, vals, jnp.zeros_like(vals))


def seen_keys(block):
    key_ids = lax.broadcasted_iota(jnp.int32, (block, block), 0)
    return key_ids <= lax.broadcasted_iota(jnp.int32, (block, block), 1)


def attend_kernel(head_dim, block, qkv_ref, cos_ref, low_ref, up_ref, rot_ref, attn_ref, lse_ref):
    length = qkv_ref.shape[0]
    scale = 1.0 / math.sqrt(head_dim)
    tables = (cos_ref[...], low_ref[...], up_ref[...])
    rot_ref[:, :LANES] = turn(qkv_ref[:, :LANES], *tables).astype(BF) * BF(scale)
    rot_ref[:, LANES : 2 * LANES] = turn(qkv_ref[:, LANES : 2 * LANES], *tables).astype(BF)
    rot_ref[:, 2 * LANES :] = qkv_ref[:, 2 * LANES :].astype(BF)
    heads = LANES // head_dim
    seen = seen_keys(block)
    for first in range(0, length, block):
        last = first + block
        total = jnp.zeros((block, LANES), F32)
        for head in range(heads):
            query_block = head_lanes(rot_ref[first:last, :LANES], head, head_dim)
            scores = jnp.where(seen, dot_cols(rot_ref[first:last, LANES : 2 * LANES], query_block), mask_fill)
            col_max = jnp.max(scores, axis=0, keepdims=True)
            if first:
                before = dot_cols(rot_ref[:first, LANES : 2 * LANES], query_block)
                col_max = jnp.maximum(col_max, jnp.max(before, axis=0, keepdims=True))
            probs = jnp.exp(scores - col_max)
            denom = jnp.sum(probs, axis=0, keepdims=True)
            part = dot_rows(probs.astype(BF), head_lanes(rot_ref[first:last, 2 * LANES :], head, head_dim))
            if first:
                probs = jnp.exp(before - col_max)
                denom += jnp.sum(probs, axis=0, keepdims=True)
                part += dot_rows(probs.astype(BF), head_lanes(rot_ref[:first, 2 * LANES :], head, head_dim))
            total += part * jnp.broadcast_to(1.0 / denom, (LANES, block)).T
            lse_ref[0, head : head + 1, first:last] = col_max + jnp.log(denom)
        attn_ref[first:last, :] = total.astype(BF)


def attend_back_kernel(head_dim, block, rot_ref, grad_ref, attn_ref, lse_ref, cos_ref, low_ref, up_ref, out_ref, sum_ref, key_acc, value_acc):
    length = rot_ref.shape[0]
    scale = 1.0 / math.sqrt(head_dim)
    heads = LANES // head_dim
    seen = seen_keys(block)

    def back(vals, span):
        return turn(vals, cos_ref[span, :], -low_ref[span, :], -up_ref[span, :])

    query_sum = jnp.zeros((1, LANES), F32)
    key_acc[...] = jnp.zeros_like(key_acc)
    value_acc[...] = jnp.zeros_like(value_acc)
    for first in range(0, length, block):
        last = first + block
        total = jnp.zeros((block, LANES), F32)
        inner = (grad_ref[first:last, :].astype(F32) * attn_ref[first:last, :].astype(F32)).T
        for head in range(heads):
            query_block = head_lanes(rot_ref[first:last, :LANES], head, head_dim)
            grad_block = head_lanes(grad_ref[first:last, :], head, head_dim)
            lse = lse_ref[0, head : head + 1, first:last]
            inner_sum = jnp.sum(inner[head * head_dim : (head + 1) * head_dim], axis=0, keepdims=True)
            for start, stop in ((0, first), (first, last)):
                if start == stop:
                    continue
                keys = rot_ref[start:stop, LANES : 2 * LANES]
                probs = jnp.exp(dot_cols(keys, query_block) - lse)
                if start == first:
                    probs = jnp.where(seen, probs, 0.0)
                value_acc[start:stop, :] += dot_plain(probs.astype(BF), grad_block)
                prob_grad = dot_cols(rot_ref[start:stop, 2 * LANES :], grad_block)
                score_grad = (probs * (prob_grad - inner_sum)).astype(BF)
                total += dot_rows(score_grad, head_lanes(keys, head, head_dim))
                key_acc[start:stop, :] += dot_plain(score_grad, query_block)
        turned = back(total * scale, slice(first, last))
        query_sum += jnp.sum(turned, axis=0, keepdims=True)
        out_ref[first:last, :LANES] = turned.astype(BF)
    turned = back(key_acc[...], slice(0, length))
    out_ref[:, LANES : 2 * LANES] = turned.astype(BF)
    out_ref[:, 2 * LANES :] = value_acc[...].astype(BF)
    sum_ref[0:1, :LANES] = query_sum
    sum_ref[0:1, LANES : 2 * LANES] = jnp.sum(turned, axis=0, keepdims=True)
    sum_ref[0:1, 2 * LANES :] = jnp.sum(value_acc[...], axis=0, keepdims=True)


def attention_cost(seqs, pairs, length, matmuls):
    flops = seqs * pairs * matmuls * 2 * 2 * length * length * LANES
    return estimate(flops, seqs * pairs * length * LANES * 16)


def attend(qkv, tables, length, head_dim):
    tokens, width = qkv.shape
    seqs, pairs = tokens // length, width // (3 * LANES)
    heads = LANES // head_dim
    block = min(512, length)
    table_spec = pl.BlockSpec((length, LANES), lambda s, h: (0, 0))
    return pl.pallas_call(
        functools.partial(attend_kernel, head_dim, block),
        grid=(seqs, pairs),
        in_specs=[pl.BlockSpec((length, 3 * LANES), lambda s, h: (s, h))] + [table_spec] * 3,
        out_specs=[
            pl.BlockSpec((length, 3 * LANES), lambda s, h: (s, h)),
            pl.BlockSpec((length, LANES), lambda s, h: (s, h)),
            pl.BlockSpec((1, heads, length), lambda s, h: (s * pairs + h, 0, 0)),
        ],
        out_shape=[
            jax.ShapeDtypeStruct((tokens, width), BF),
            jax.ShapeDtypeStruct((tokens, pairs * LANES), BF),
            jax.ShapeDtypeStruct((seqs * pairs, heads, length), F32),
        ],
        compiler_params=pltpu.CompilerParams(vmem_limit_bytes=VMEM_LIMIT),
        cost_estimate=attention_cost(seqs, pairs, length, 3),
    )(qkv, *tables)


def attend_back(rot, attn_grad, attn, lse, tables, length, head_dim):
    tokens, width = rot.shape
    seqs, pairs = tokens // length, width // (3 * LANES)
    heads = LANES // head_dim
    block = min(512, length)
    table_spec = pl.BlockSpec((length, LANES), lambda s, h: (0, 0))
    return pl.pallas_call(
        functools.partial(attend_back_kernel, head_dim, block),
        grid=(seqs, pairs),
        in_specs=[
            pl.BlockSpec((length, 3 * LANES), lambda s, h: (s, h)),
            pl.BlockSpec((length, LANES), lambda s, h: (s, h)),
            pl.BlockSpec((length, LANES), lambda s, h: (s, h)),
            pl.BlockSpec((1, heads, length), lambda s, h: (s * pairs + h, 0, 0)),
        ]
        + [table_spec] * 3,
        out_specs=[
            pl.BlockSpec((length, 3 * LANES), lambda s, h: (s, h)),
            pl.BlockSpec((8, 3 * LANES), lambda s, h: (s, h)),
        ],
        out_shape=[jax.ShapeDtypeStruct((tokens, width), BF), jax.ShapeDtypeStruct((8 * seqs, width), F32)],
        scratch_shapes=[pltpu.VMEM((length, LANES), F32), pltpu.VMEM((length, LANES), F32)],
        compiler_params=pltpu.CompilerParams(vmem_limit_bytes=VMEM_LIMIT),
        cost_estimate=attention_cost(seqs, pairs, length, 6),
    )(rot, attn_grad, attn, lse, *tables)


def spec_rows(tile, width):
    return pl.BlockSpec((tile, width), lambda i, s: (i, 0))


def spec_whole(array):
    return pl.BlockSpec(array.shape, lambda i, s: (0,) * array.ndim)


def estimate(flops, moved):
    return pl.CostEstimate(flops=int(flops) // 64, bytes_accessed=int(moved) // 64, transcendentals=0)


def lined_dot(slots_ref, rows_ref, parts, cols):
    depth = parts[0].shape[0]
    total = None
    for at, part in enumerate(parts):
        first = pl.multiple_of(slots_ref[at] * depth, depth)
        piece = dot_plain(rows_ref[:, pl.ds(first, depth)], part[:, cols])
        total = piece if total is None else total + piece
    return total


def rows_call(kernel, slots, ins, in_specs, outs, tile, cost, out_specs=None, steps=None):
    return pl.pallas_call(
        kernel,
        grid_spec=pltpu.PrefetchScalarGridSpec(
            num_scalar_prefetch=1,
            grid=(steps or outs[0].shape[0] // tile,),
            in_specs=in_specs,
            out_specs=out_specs or [spec_rows(tile, out.shape[1]) for out in outs],
        ),
        out_shape=outs,
        compiler_params=pltpu.CompilerParams(vmem_limit_bytes=VMEM_LIMIT),
        cost_estimate=cost,
    )(slots, *ins)


def normalise(rows):
    micros, tokens, width = rows.shape

    def kernel(rows_ref, out_ref):
        vals = rows_ref[0].astype(F32)
        mean = jnp.mean(vals, axis=-1, keepdims=True)
        centred = vals - mean
        var = jnp.mean(centred * centred, axis=-1, keepdims=True)
        out_ref[...] = (centred * lax.rsqrt(var + norm_epsilon)).astype(BF)

    def one(micro):
        return pl.pallas_call(
            kernel,
            grid=(2,),
            in_specs=[pl.BlockSpec((1, tokens // 2, width), lambda i: (micro, i, 0))],
            out_specs=pl.BlockSpec((tokens // 2, width), lambda i: (i, 0)),
            out_shape=jax.ShapeDtypeStruct((tokens, width), BF),
            compiler_params=pltpu.CompilerParams(vmem_limit_bytes=VMEM_LIMIT),
            cost_estimate=estimate(10 * tokens * width, 4 * tokens * width),
        )(rows)

    return [one(micro) for micro in range(micros)]


def norm_qkv(slots, rows, gain, shift, parts, bias):
    tokens, width = rows.shape
    cols, tile = bias.shape[1], 512

    def kernel(slots_ref, rows_ref, gain_ref, shift_ref, bias_ref, *refs):
        parts, (normed_ref, qkv_ref) = refs[:-2], refs[-2:]
        normed_ref[...] = (rows_ref[...].astype(F32) * gain_ref[...] + shift_ref[...]).astype(BF)
        qkv_ref[...] = lined_dot(slots_ref, normed_ref, parts, slice(0, cols)) + bias_ref[...]

    return rows_call(
        kernel,
        slots,
        [rows, gain, shift, bias, *parts],
        [spec_rows(tile, width)] + [spec_whole(array) for array in (gain, shift, bias, *parts)],
        [jax.ShapeDtypeStruct((tokens, width), BF), jax.ShapeDtypeStruct((tokens, cols), F32)],
        tile,
        estimate(2 * tokens * width * cols, tokens * (4 * width + 4 * cols)),
    )


def micro_spec(micro, steps, tile, width):
    return pl.BlockSpec((tile, width), lambda i, s: (jnp.clip(i - micro * steps, 0, steps - 1), 0))


def up_act(slots, rows, parts, bias):
    count = len(rows)
    tokens, width = rows[0].shape
    cols, tile, chunk = bias.shape[1], 512, 512
    steps = tokens // tile

    def kernel(slots_ref, bias_ref, *refs):
        ins, parts, outs = refs[:count], refs[count : -2 * count], refs[-2 * count :]
        for micro in range(count):

            @pl.when(pl.program_id(0) // steps == micro)
            def _():
                for at in range(0, cols, chunk):
                    span = slice(at, at + chunk)
                    pre = lined_dot(slots_ref, ins[micro], parts, span) + bias_ref[:, span]
                    square = pre * pre
                    tanh = jnp.tanh(pre * (gelu_factor + (gelu_factor * 0.044715) * square))
                    half = 0.5 + 0.5 * tanh
                    act = pre * half
                    outs[micro][:, span] = act.astype(BF)
                    inner = 2 * gelu_factor + (6 * 0.044715 * gelu_factor) * square
                    outs[count + micro][:, span] = (half + (act - act * half) * inner).astype(BF)

    outs = rows_call(
        kernel,
        slots,
        [bias, *rows, *parts],
        [spec_whole(bias)]
        + [micro_spec(m, steps, tile, width) for m in range(count)]
        + [spec_whole(part) for part in parts],
        [jax.ShapeDtypeStruct((tokens, cols), BF)] * (2 * count),
        tile,
        estimate(2 * count * tokens * width * cols, count * tokens * (2 * width + 4 * cols)),
        [micro_spec(m, steps, tile, cols) for m in range(count)] * 2,
        count * steps,
    )
    return outs[:count], outs[count:]


def pre_grad_rows(slots, rows, parts, slopes):
    count = len(rows)
    tokens, width = rows[0].shape
    cols, tile = slopes[0].shape[1], 512
    steps = tokens // tile

    def kernel(slots_ref, *refs):
        ins, slopes, parts = refs[:count], refs[count : 2 * count], refs[2 * count : -count - 1]
        outs, sum_ref = refs[-count - 1 : -1], refs[-1]

        @pl.when(pl.program_id(0) == 0)
        def _():
            sum_ref[...] = jnp.zeros_like(sum_ref)

        for micro in range(count):

            @pl.when(pl.program_id(0) // steps == micro)
            def _():
                act_grad = lined_dot(slots_ref, ins[micro], parts, slice(0, cols))
                grad = act_grad * slopes[micro][...].astype(F32)
                outs[micro][...] = grad.astype(BF)
                sum_ref[0:1, :] += jnp.sum(grad, axis=0, keepdims=True)

    return rows_call(
        kernel,
        slots,
        [*rows, *slopes, *parts],
        [micro_spec(m, steps, tile, width) for m in range(count)]
        + [micro_spec(m, steps, tile, cols) for m in range(count)]
        + [spec_whole(part) for part in parts],
        [jax.ShapeDtypeStruct((tokens, cols), BF)] * count + [jax.ShapeDtypeStruct((8, cols), F32)],
        tile,
        estimate(2 * count * tokens * width * cols, count * tokens * (2 * width + 4 * cols)),
        [micro_spec(m, steps, tile, cols) for m in range(count)] + [pl.BlockSpec((8, cols), lambda i, s: (0, 0))],
        count * steps,
    )


def head_grad_rows(slots, rows, parts, first):
    tokens, width = rows.shape
    cols, tile = parts[0].shape[1] - first, 1024

    def kernel(slots_ref, rows_ref, *refs):
        parts, out_ref = refs[:-1], refs[-1]
        out_ref[...] = lined_dot(slots_ref, rows_ref, parts, slice(first, first + cols)).astype(BF)

    return rows_call(
        kernel,
        slots,
        [rows, *parts],
        [spec_rows(tile, width)] + [spec_whole(part) for part in parts],
        [jax.ShapeDtypeStruct((tokens, cols), BF)],
        tile,
        estimate(2 * tokens * width * cols, tokens * (2 * width + 2 * cols)),
    )[0]


def branch_rows(slots, ones, one_parts, first, twos, two_parts, block):
    micros = len(ones)
    tokens, cols = ones[0].shape
    count, depth = len(one_parts), one_parts[0].shape[0]
    held = 2
    tile = held * block
    width, steps = count * depth, tokens // tile

    def kernel(slots_ref, *refs):
        ones, twos, out_ref = refs[:micros], refs[micros : 2 * micros], refs[-1]
        parts = refs[2 * micros : -1]
        for micro in range(micros):

            @pl.when(pl.program_id(0) // steps == micro)
            def _():
                for at in range(count):
                    where = pl.multiple_of(slots_ref[at] * depth, depth)
                    total = dot_cols(ones[micro][...], parts[at][:, first : first + cols])
                    total += dot_cols(twos[micro][...], parts[count + at][...])
                    out_ref[:, 0, :, pl.ds(where, depth)] = total.astype(BF).reshape(held, block, depth)

    return rows_call(
        kernel,
        slots,
        [*ones, *twos, *one_parts, *two_parts],
        [micro_spec(m, steps, tile, cols) for m in range(micros)]
        + [micro_spec(m, steps, tile, twos[0].shape[1]) for m in range(micros)]
        + [spec_whole(part) for part in (*one_parts, *two_parts)],
        [jax.ShapeDtypeStruct((tokens // block, micros, block, width), BF)],
        tile,
        estimate(2 * micros * tokens * width * (cols + twos[0].shape[1]), 2 * micros * tokens * (width + cols)),
        [pl.BlockSpec((held, 1, block, width), lambda i, s: (lax.rem(i, steps), i // steps, 0, 0))],
        micros * steps,
    )[0]


def normed_grad_rows(slots, one, one_parts, two, two_parts, rows, block, split):
    tokens, cols = one.shape
    count, depth = len(one_parts), one_parts[0].shape[0]
    tile = 2 * block
    width = count * depth

    def kernel(slots_ref, one_ref, two_ref, rows_ref, *refs):
        outs, sum_ref = refs[2 * count : -1], refs[-1]

        @pl.when(pl.program_id(0) == 0)
        def _():
            sum_ref[...] = jnp.zeros_like(sum_ref)

        for at in range(count):
            where = pl.multiple_of(slots_ref[at] * depth, depth)
            span = pl.ds(where, depth)
            total = dot_cols(one_ref[...], refs[at][:, :cols])
            total += dot_cols(two_ref[...], refs[count + at][...])
            if split:
                first = slots_ref[count] == 0
                outs[0][:, span] = jnp.where(first, total[:block], total[block:]).astype(BF)
                outs[1][:, span] = jnp.where(first, total[block:], total[:block]).astype(BF)
            else:
                outs[0][:, span] = total.astype(BF)
            sum_ref[0:1, span] += jnp.sum(total * rows_ref[:, span].astype(F32), axis=0, keepdims=True)
            sum_ref[1:2, span] += jnp.sum(total, axis=0, keepdims=True)

    pieces = 2 if split else 1
    return rows_call(
        kernel,
        slots,
        [one, two, rows, *one_parts, *two_parts],
        [spec_rows(tile, cols), spec_rows(tile, two.shape[1]), spec_rows(tile, width)]
        + [spec_whole(part) for part in (*one_parts, *two_parts)],
        [jax.ShapeDtypeStruct((tokens // pieces, width), BF)] * pieces + [jax.ShapeDtypeStruct((8, width), F32)],
        tile,
        estimate(2 * tokens * width * (cols + two.shape[1]), 2 * tokens * (2 * width + cols + two.shape[1])),
        [spec_rows(tile // pieces, width)] * pieces + [pl.BlockSpec((8, width), lambda i, s: (0, 0))],
        tokens // tile,
    )


def norm_back(rows, cots, pieces, gain, micro, earlier=None):
    micros, tokens, width = rows.shape
    tile = tokens // 4

    def kernel(rows_ref, cot_ref, gain_ref, *refs):
        vals = rows_ref[0].astype(F32)
        mean = jnp.mean(vals, axis=-1, keepdims=True)
        centred = vals - mean
        scale = lax.rsqrt(jnp.mean(centred * centred, axis=-1, keepdims=True) + norm_epsilon)
        scaled = centred * scale
        grad = refs[0][...].astype(F32)
        for ref in refs[1 : len(pieces)]:
            grad += ref[...].astype(F32)
        grad *= gain_ref[...]
        inner = jnp.mean(grad * scaled, axis=-1, keepdims=True)
        grad = (grad - jnp.mean(grad, axis=-1, keepdims=True) - scaled * inner) * scale
        refs[-1][0] = (cot_ref[0].astype(F32) + grad).astype(BF)

    at_micro = pl.BlockSpec((1, tile, width), lambda i: (micro, i, 0))
    given = [] if earlier is None else [earlier]
    return pl.pallas_call(
        kernel,
        grid=(tokens // tile,),
        in_specs=[at_micro, at_micro, pl.BlockSpec((1, width), lambda i: (0, 0))]
        + [pl.BlockSpec((tile, width), lambda i: (i, 0))] * len(pieces)
        + [pl.BlockSpec(memory_space=pl.ANY)] * len(given),
        out_specs=at_micro,
        out_shape=jax.ShapeDtypeStruct(rows.shape, BF),
        input_output_aliases={3 + len(pieces): 0} if given else {},
        compiler_params=pltpu.CompilerParams(vmem_limit_bytes=VMEM_LIMIT),
        cost_estimate=estimate(20 * tokens * width, 10 * tokens * width),
    )(rows, cots, gain, *pieces, *given)


def weight_grad(lefts, rights, turned=False):
    tile, chunk = 512, 512
    micro_count = len(lefts)
    tokens, width = lefts[0].shape
    widths = [right[0].shape[1] for right in rights]
    cols, steps = sum(widths), tokens // tile
    shape = (cols, width) if turned else (width, cols)

    def kernel(*refs):
        out_ref, acc_ref = refs[-2:]
        step = pl.program_id(0)

        @pl.when(step == 0)
        def _():
            acc_ref[...] = jnp.zeros_like(acc_ref)

        for micro in range(micro_count):

            @pl.when(step // steps == micro)
            def _():
                first = 0
                for at, span in enumerate(widths):
                    right = refs[(1 + at) * micro_count + micro]
                    if turned:
                        for row in range(0, span, min(chunk, span)):
                            rows = slice(row, row + min(chunk, span))
                            acc_ref[first + row : first + rows.stop, :] += dot_rows(right[:, rows], refs[micro][...])
                    else:
                        for row in range(0, width, chunk):
                            acc_ref[row : row + chunk, first : first + span] += dot_rows(
                                refs[micro][:, row : row + chunk], right[...]
                            )
                    first += span

        @pl.when(step == micro_count * steps - 1)
        def _():
            out_ref[...] = acc_ref[...].astype(BF)

    def side(micro, span):
        return pl.BlockSpec((tile, span), lambda i: (jnp.clip(i - micro * steps, 0, steps - 1), 0))

    return pl.pallas_call(
        kernel,
        grid=(micro_count * steps,),
        in_specs=[side(micro, span) for span in (width, *widths) for micro in range(micro_count)],
        out_specs=pl.BlockSpec(shape, lambda i: (0, 0)),
        out_shape=jax.ShapeDtypeStruct(shape, BF),
        scratch_shapes=[pltpu.VMEM(shape, F32)],
        compiler_params=pltpu.CompilerParams(vmem_limit_bytes=VMEM_LIMIT),
        cost_estimate=estimate(
            2 * micro_count * tokens * width * cols, 2 * micro_count * tokens * (width + cols)
        ),
    )(*lefts, *(array for right in rights for array in right))


def shards(
    inputs,
    ln_gain,
    ln_bias,
    qkv_weight,
    qkv_bias,
    out_weight,
    out_bias,
    up_weight,
    up_bias,
    down_weight,
    down_bias,
    cotangent,
):
    micro_count, _, token_rows, model_width = inputs.shape
    fsdp_size, tp_size = lax.axis_size("fsdp"), lax.axis_size("tp")
    line = fsdp_size // 2
    fsdp_at, tp_at = lax.axis_index("fsdp"), lax.axis_index("tp")
    line_at, pair_at = fsdp_at >> 1, fsdp_at & 1
    plane_size = 2 * tp_size
    planes = [[plane * plane_size + i for i in range(plane_size)] for plane in range(line)]
    ring = [(f, ((f // 2 + 1) % line) * 2 + f % 2) for f in range(fsdp_size)]
    length = token_rows * tp_size
    head_dim = qkv_bias.shape[2] * fsdp_size
    shard_rows = model_width // fsdp_size
    line_rows = 2 * shard_rows
    attn_cols = out_weight.shape[0] // 2
    qkv_cols = 3 * attn_cols
    pairs = attn_cols // LANES
    mlp_cols = up_weight.shape[1] // 2
    both_axes = ("fsdp", "tp")

    def swap_pair(vals):
        return lax.ppermute(vals, "fsdp", [(f, f ^ 1) for f in range(fsdp_size)])

    def gather_plane(vals):
        return lax.all_gather(vals, both_axes, axis=0, tiled=True, axis_index_groups=planes)

    def scatter_plane(vals):
        return lax.psum_scatter(vals, both_axes, scatter_dimension=0, tiled=True, axis_index_groups=planes)

    def doubled(cur, axis, size, at, bit):
        other = lax.ppermute(cur, axis, [(i, i ^ bit) for i in range(size)])
        upper = (at & bit) != 0
        return jnp.where(upper, jnp.concatenate([other, cur]), jnp.concatenate([cur, other]))

    def attn_half(half):
        qkv_part = lax.dynamic_slice_in_dim(qkv_weight, half * attn_cols, attn_cols, axis=2)
        qkv_part = qkv_part.reshape(shard_rows, 3, pairs, LANES).transpose(0, 2, 1, 3)
        out_part = lax.dynamic_slice_in_dim(out_weight, half * attn_cols, attn_cols, axis=0)
        return jnp.concatenate([qkv_part.reshape(shard_rows, qkv_cols), out_part.T], axis=1)

    def up_half(half):
        return lax.dynamic_slice_in_dim(up_weight, half * mlp_cols, mlp_cols, axis=1)

    def down_half(half):
        return lax.dynamic_slice_in_dim(down_weight, half * mlp_cols, mlp_cols, axis=0).T

    def pair_join(own, other):
        return jnp.where(pair_at == 0, jnp.concatenate([own, other]), jnp.concatenate([other, own]))

    class Box:
        def __init__(self, val):
            self.val = val

    class Line:
        tokens = []

        def tie(self, *boxes):
            held = []
            for box in (*boxes, *self.tokens):
                if box not in held:
                    held.append(box)
            if len(held) > 1:
                for box, val in zip(held, lax.optimization_barrier(tuple(box.val for box in held))):
                    box.val = val

        def run(self, piece, *boxes):
            self.tie(*boxes)
            results = [Box(val) for val in piece(*(box.val for box in boxes))]
            self.tokens = [results[0]]
            return results

        def sync(self, box):
            self.tokens = self.tokens + [box]

    order = Line()

    class Gather:
        def __init__(self, shard):
            self.parts = [shard]

        def move(self):
            if len(self.parts) < line:
                order.tie(self.parts[-1])
                self.parts.append(Box(lax.ppermute(self.parts[-1].val, "fsdp", ring)))

        def sync(self):
            order.sync(self.parts[-1])

        def finish(self):
            while len(self.parts) < line:
                self.move()
            self.sync()

        def vals(self):
            return [part.val for part in self.parts]

    class Scatter:
        def __init__(self, part, axis):
            self.part, self.step, self.came, self.axis = part, 1, None, axis

        def total(self):
            at_line = lax.rem(line_at + line - self.step, line)
            own = lax.dynamic_slice_in_dim(self.part.val, at_line * line_rows, line_rows, axis=self.axis)
            if self.came is None:
                return own
            order.tie(self.came)
            return self.came.val.astype(F32) + own.astype(F32)

        def move(self):
            if self.step < line:
                sent = Box(self.total().astype(BF))
                if self.came is None:
                    order.tie(sent)
                self.came = Box(lax.ppermute(sent.val, "fsdp", ring))
                self.step += 1

        def sync(self):
            order.sync(self.came)

        def rows_at(self, half):
            own = lax.dynamic_slice_in_dim(
                self.part.val, line_at * line_rows + half * shard_rows, shard_rows, axis=self.axis
            )
            came = lax.dynamic_slice_in_dim(self.came.val, half * shard_rows, shard_rows, axis=self.axis)
            return came.astype(F32) + own.astype(F32)

        def swap(self):
            while self.step < line:
                self.move()
            order.tie(self.came)
            self.sent = Box(self.rows_at(1 - pair_at).astype(BF))
            self.got = Box(swap_pair(self.sent.val))

        def halves(self):
            order.tie(self.came)
            keep, got = self.rows_at(pair_at), self.got.val.astype(F32)
            return jnp.where(pair_at == 0, keep, got), jnp.where(pair_at == 0, got, keep)

    class SmallSum:
        def __init__(self, everywhere, over_fsdp):
            self.cur, self.rest = Box(everywhere), over_fsdp
            self.size = everywhere.shape[0]
            bits = [("tp", tp_size, bit) for bit in range(tp_size.bit_length() - 1)]
            self.steps = bits + [("fsdp", fsdp_size, 0), ("line", 0, 0)]

        def move(self):
            if self.steps:
                axis, size, bit = self.steps.pop(0)
                if axis == "fsdp":
                    self.cur = Box(jnp.concatenate([self.cur.val, self.rest]))
                order.tie(self.cur)
                if axis == "line":
                    others = along_line(self.cur.val)
                else:
                    others = [lax.ppermute(self.cur.val, axis, [(i, i ^ (1 << bit)) for i in range(size)])]
                self.cur = Box(sum(others, self.cur.val))

        def split(self):
            while self.steps:
                self.move()
            return self.cur.val[: self.size], self.cur.val[self.size :]

    plain = normalise(inputs[:, 0])
    cots = [cotangent[m].reshape(token_rows, model_width) for m in range(micro_count)]
    micros = range(micro_count)
    plane_rows, plane_cots = [None] * micro_count, [None] * micro_count

    def gather_behind(rows):
        sent = Box(rows)
        order.tie(sent)
        return Box(gather_plane(sent.val))

    small = jnp.concatenate(
        [vec.reshape(-1) for vec in (ln_gain, ln_bias, out_bias, down_bias, qkv_bias, up_bias)]
    )
    attn_send = Box(attn_half(1 - pair_at))
    order.tokens = [attn_send]
    plane_rows[0] = gather_behind(plain[0])
    attn_shard = Box(pair_join(attn_half(pair_at), swap_pair(attn_send.val)))
    small_all = Box(small[None])
    order.tokens = [attn_shard]
    order.tie(small_all)
    small_all = small_all.val
    for bit in range(tp_size.bit_length() - 1):
        small_all = doubled(small_all, "tp", tp_size, tp_at, 1 << bit)
    small_near = small_all

    def along_line(vals):
        return [lax.ppermute(vals, "fsdp", [(f, f ^ (far << 1)) for f in range(fsdp_size)]) for far in range(1, line)]

    def small_step(small_all, step):
        order.tie(small_all)
        if step == 0:
            return Box(doubled(small_all.val, "fsdp", fsdp_size, fsdp_at, 1))
        held = [small_all.val] + along_line(small_all.val)
        for bit in range(line.bit_length() - 1):
            other = (line_at & (1 << bit)) != 0
            held = [jnp.where(other, held[i ^ (1 << bit)], held[i]) for i in range(line)]
        return Box(jnp.concatenate(held))

    small_all = Box(small_near)
    attn_ring = Gather(attn_shard)
    attn_ring.move()
    plane_rows[1] = gather_behind(plain[1])
    order.sync(small_all)
    small_all = small_step(small_all, 0)
    bias_total = Box(sum(jnp.sum(cots[m].astype(F32), axis=0) for m in micros))
    up_send = Box(up_half(1 - pair_at))
    order.tie(up_send)
    up_got = Box(swap_pair(up_send.val))
    attn_ring.sync()
    order.sync(small_all)
    attn_ring.move()
    order.sync(bias_total)
    small_all = small_step(small_all, 1)
    down_send = Box(down_half(1 - pair_at))
    order.tie(down_send, up_got)
    down_got = Box(swap_pair(down_send.val))
    up_shard = Box(pair_join(up_half(pair_at), up_got.val))
    attn_ring.sync()
    order.sync(small_all)
    attn_ring.move()
    plane_cots[0] = gather_behind(cots[0])
    order.sync(up_shard)
    order.tie(small_all)
    small_all = small_all.val
    vec_size = ln_gain.shape[0]
    gain_vec, shift_vec, bias_out, bias_down = (
        small_all[:, i * vec_size : (i + 1) * vec_size].reshape(-1).astype(F32) for i in range(4)
    )
    bias_both = bias_out + bias_down
    mine = lax.dynamic_slice_in_dim(
        small_all.reshape(fsdp_size, tp_size, -1), tp_at, 1, axis=1
    )[:, 0].astype(F32)
    at = 4 * vec_size
    qkv_b = mine[:, at : at + qkv_bias.size].reshape(fsdp_size, 3, 2, pairs, -1, qkv_bias.shape[2])
    qkv_b = lax.dynamic_slice_in_dim(qkv_b, pair_at, 1, axis=2)[:, :, 0]
    qkv_b = qkv_b.transpose(2, 1, 3, 0, 4).reshape(1, qkv_cols)
    at += qkv_bias.size
    up_b = mine[:, at:].reshape(fsdp_size, up_bias.shape[0], up_bias.shape[1])
    up_b = up_b.transpose(1, 0, 2).reshape(2, mlp_cols)
    up_b = lax.dynamic_slice_in_dim(up_b, pair_at, 1, axis=0)

    slots = [lax.rem(line_at + line - step, line) for step in range(line)]
    slots = jnp.stack(slots + [tp_at & 1]).astype(jnp.int32)
    tables = rotary_tables(length, head_dim, ROT)
    prepared = [Box(val) for val in (gain_vec[None], shift_vec[None], qkv_b, up_b, slots, *tables)]
    for box in prepared:
        order.sync(box)
    order.tie(down_got)
    down_shard = Box(pair_join(down_half(pair_at), down_got.val))
    order.tokens = [down_shard]
    attn_ring.finish()
    order.tie(up_shard, *prepared)
    gain_row, shift_row, qkv_b, up_b, slots, *tables = (box.val for box in prepared)
    normed, qkvs, rots, attns, lses, acts, slopes = ([None] * micro_count for _ in range(7))
    pre_grads, qkv_grads, qkv_sums, sums, attn_heads = ([None] * micro_count for _ in range(5))

    def norm_piece(m):
        normed[m], qkvs[m] = order.run(
            lambda rows: norm_qkv(slots, rows, gain_row, shift_row, attn_ring.vals(), qkv_b), plane_rows[m]
        )

    def attend_piece(m):
        rots[m], attns[m], lses[m] = order.run(
            lambda vals: attend(vals, tables, length, head_dim), qkvs[m]
        )

    def up_piece():
        def piece(*rows):
            return [val for vals in up_act(slots, rows, up_ring.vals(), up_b) for val in vals]

        results = order.run(piece, *normed)
        acts[:], slopes[:] = results[:micro_count], results[micro_count:]

    def head_grad_piece(m):
        (attn_heads[m],) = order.run(
            lambda cot: [head_grad_rows(slots, cot, attn_ring.vals(), qkv_cols)], plane_cots[m]
        )

    def attend_back_piece(m):
        qkv_grads[m], qkv_sums[m] = order.run(
            lambda rot, grad, attn, lse: attend_back(rot, grad, attn, lse, tables, length, head_dim),
            rots[m],
            attn_heads[m],
            attns[m],
            lses[m],
        )

    def pre_grad_piece():
        def piece(*vals):
            return pre_grad_rows(slots, vals[:micro_count], down_ring.vals(), vals[micro_count:])

        *pre_grads[:], up_sums = order.run(piece, *plane_cots, *slopes)
        return up_sums

    def weight_piece(lefts, *rights, turned=False):
        def piece(*flat):
            sets = [flat[at : at + micro_count] for at in range(0, len(flat), micro_count)]
            return [weight_grad(sets[0], sets[1:], turned)]

        part = order.run(piece, *lefts, *(box for right in rights for box in right))[0]
        return Scatter(part, 1 if turned else 0)

    def branch_piece():
        def piece(*vals):
            rows = branch_rows(
                slots,
                vals[:micro_count],
                attn_ring.vals(),
                qkv_cols,
                vals[micro_count:],
                down_ring.vals(),
                token_rows,
            )
            return [rows.reshape(-1, model_width)]

        return order.run(piece, *attns, *acts)[0]

    def normed_grad_piece(m, split=False):
        *back, sums[m] = order.run(
            lambda one, two, rows: normed_grad_rows(
                slots, one, attn_ring.vals(), two, up_ring.vals(), rows, token_rows, split
            ),
            qkv_grads[m],
            pre_grads[m],
            plane_rows[m],
        )
        return back

    def scatter_behind(box):
        order.tie(box)
        return Box(scatter_plane(box.val))

    up_ring, down_ring = Gather(up_shard), Gather(down_shard)
    order.sync(down_shard)
    up_ring.move()
    norm_piece(0)
    up_ring.sync()
    plane_cots[1] = gather_behind(cots[1])
    up_ring.move()
    attend_piece(0)
    norm_piece(1)
    up_ring.sync()
    up_ring.move()
    attend_piece(1)
    up_ring.finish()
    down_ring.move()
    up_piece()
    down_ring.sync()
    down_ring.move()
    head_grad_piece(0)
    attend_back_piece(0)
    down_ring.sync()
    down_ring.move()

    down_scatter = weight_piece(plane_cots, acts, attns, turned=True)
    down_ring.finish()
    down_scatter.move()
    branch = branch_piece()
    down_scatter.sync()
    branch_sum = scatter_behind(branch)
    down_scatter.move()
    up_sums = pre_grad_piece()
    down_scatter.sync()
    down_scatter.move()
    up_scatter = weight_piece(normed, pre_grads)
    down_scatter.sync()
    down_scatter.swap()
    up_scatter.move()
    head_grad_piece(1)
    attend_back_piece(1)
    up_scatter.sync()
    order.sync(down_scatter.got)
    up_scatter.move()
    (back,) = normed_grad_piece(0)
    up_scatter.sync()
    back_sum = scatter_behind(back)
    up_scatter.move()
    qkv_scatter = weight_piece(normed, qkv_grads)
    up_scatter.sync()
    order.sync(branch_sum)
    up_scatter.swap()
    qkv_scatter.move()
    keep, give = normed_grad_piece(1, True)

    def swap_core(vals):
        return lax.ppermute(vals, "tp", [(t, t ^ 1) for t in range(tp_size)])

    def swap_y(vals):
        return lax.ppermute(vals, "tp", [(t, t ^ 2) for t in range(tp_size)])

    y_at, half = tp_at >> 1, model_width // 2
    up_b_grad = up_sums.val[0]
    qkv_b_grad = sum(jnp.sum(part.val.reshape(-1, 8, qkv_cols)[:, 0], axis=0) for part in qkv_sums)
    qkv_b_grad = qkv_b_grad.reshape(pairs, 3, -1).transpose(1, 0, 2).reshape(3, attn_cols)

    def in_half(vals):
        blank = jnp.zeros_like(vals)
        return jnp.where(
            pair_at == 0, jnp.concatenate([vals, blank], axis=-1), jnp.concatenate([blank, vals], axis=-1)
        )

    gain_total, shift_total = (sum(part.val[i] for part in sums) for i in range(2))
    tail = SmallSum(
        jnp.concatenate([gain_total, shift_total, bias_total.val]),
        jnp.concatenate([in_half(up_b_grad), in_half(qkv_b_grad).reshape(-1)]),
    )
    qkv_scatter.sync()
    order.sync(up_scatter.got)
    order.tie(give, tail.cur)
    tail.move()
    got = Box(swap_core(give.val))
    qkv_scatter.move()
    order.sync(tail.cur)
    order.tie(got)
    blocks = Box((got.val.astype(F32) + keep.val.astype(F32)).astype(BF).reshape(4, token_rows, model_width))
    tail.move()

    def block(pair, y):
        return lax.dynamic_index_in_dim(blocks.val, pair * 2 + y, 0, keepdims=False)

    order.sync(blocks)
    order.sync(tail.cur)
    order.tie(tail.cur)
    far = block(1 - pair_at, 1 - y_at)
    from_pair, from_y = Box(swap_pair(far[:, :half])), Box(swap_y(far[:, half:]))
    tail.move()
    halves = down_scatter.halves()
    down_w_grad = Box(jnp.concatenate([part[:mlp_cols] for part in halves], axis=0))
    out_w_grad = Box(jnp.concatenate([part[mlp_cols:] for part in halves], axis=0))
    for box in (down_w_grad, out_w_grad):
        order.sync(box)

    qkv_scatter.sync()
    order.tie()
    qkv_scatter.move()
    order.tie(from_pair, from_y)
    for_y, for_pair = block(pair_at, 1 - y_at), block(1 - pair_at, y_at)
    for_y = jnp.concatenate(
        [(for_y[:, :half].astype(F32) + from_pair.val.astype(F32)).astype(BF), for_y[:, half:]], axis=1
    )
    for_pair = jnp.concatenate(
        [for_pair[:, :half], (for_pair[:, half:].astype(F32) + from_y.val.astype(F32)).astype(BF)], axis=1
    )
    for_pair, for_y = Box(for_pair), Box(for_y)
    from_pair, from_y = Box(swap_pair(for_pair.val)), Box(swap_y(for_y.val))
    own_block = Box(block(pair_at, y_at))
    for box in (for_pair, for_y, own_block):
        order.sync(box)
    order.tie(back_sum)
    gained = Box(norm_back(inputs[:, 0], cotangent[:, 0], [back_sum.val], gain_row, 0))
    order.sync(gained)
    order.tie(branch_sum)
    branch_rows_sum = branch_sum.val.reshape(micro_count, token_rows, model_width).astype(F32)
    output = Box((inputs[:, 0].astype(F32) + branch_rows_sum + bias_both).astype(BF))
    order.sync(output)
    qkv_scatter.sync()
    order.sync(tail.cur)
    order.tie(tail.cur)
    tail.move()
    qkv_scatter.swap()
    up_w_grad = Box(jnp.concatenate(up_scatter.halves(), axis=1))
    order.sync(up_w_grad)
    order.tie(from_pair, from_y)
    last_pieces = [own_block.val, from_pair.val, from_y.val]
    gained = Box(norm_back(inputs[:, 0], cotangent[:, 0], last_pieces, gain_row, 1, gained.val))
    order.tokens = [gained]
    order.tie(qkv_scatter.got, tail.cur)
    halves = qkv_scatter.halves()
    planes = [
        jnp.concatenate(
            [
                part[:, (pair * 3 + plane) * LANES : (pair * 3 + plane + 1) * LANES]
                for part in halves
                for pair in range(pairs)
            ],
            axis=1,
        )
        for plane in range(3)
    ]
    qkv_w_grad = jnp.stack(planes, axis=0).transpose(1, 0, 2)
    small_sums, bias_sums = tail.split()

    small_sums = small_sums.reshape(3, fsdp_size * tp_size, vec_size)
    small_sums = lax.dynamic_slice_in_dim(small_sums, fsdp_at * tp_size + tp_at, 1, axis=1)[:, 0]
    gain_sum, shift_sum, bias_sum = small_sums[0], small_sums[1], small_sums[2]
    up_b_sum = bias_sums[: 2 * mlp_cols].reshape(up_bias.shape[0], -1)
    up_b_sum = lax.dynamic_slice_in_dim(up_b_sum, fsdp_at * up_bias.shape[1], up_bias.shape[1], axis=1)
    qkv_b_sum = bias_sums[2 * mlp_cols :].reshape(3, qkv_bias.shape[1], -1)
    qkv_b_sum = lax.dynamic_slice_in_dim(qkv_b_sum, fsdp_at * qkv_bias.shape[2], qkv_bias.shape[2], axis=2)

    return (
        output.val[:, None],
        gained.val[:, None],
        gain_sum,
        shift_sum,
        qkv_w_grad,
        qkv_b_sum,
        out_w_grad.val,
        bias_sum,
        up_w_grad.val,
        up_b_sum,
        down_w_grad.val,
        bias_sum,
    )


def solution(mesh):
    return jax.shard_map(
        shards,
        mesh=mesh,
        in_specs=(
            P(None, "fsdp", "tp", None),
            P(("fsdp", "tp")),
            P(("fsdp", "tp")),
            P("fsdp", None, "tp"),
            P(None, "tp", "fsdp"),
            P("tp", "fsdp"),
            P(("fsdp", "tp")),
            P("fsdp", "tp"),
            P("tp", "fsdp"),
            P("tp", "fsdp"),
            P(("fsdp", "tp")),
            P(None, "fsdp", "tp", None),
        ),
        out_specs=(
            P(None, "fsdp", "tp", None),
            P(None, "fsdp", "tp", None),
            P(("fsdp", "tp")),
            P(("fsdp", "tp")),
            P("fsdp", None, "tp"),
            P(None, "tp", "fsdp"),
            P("tp", "fsdp"),
            P(("fsdp", "tp")),
            P("fsdp", "tp"),
            P("tp", "fsdp"),
            P("tp", "fsdp"),
            P(("fsdp", "tp")),
        ),
        check_vma=False,
    )
```
